32 devices in a mesh: dp: 8 (over z, x), section: 4 (over y, core).
Axes of the slice: x: 2, y: 2, z: 4, core: 2. Of those that a mesh axis runs over, the one named last changes fastest.
Arguments:
- patches: bfloat16 [256, 1600], P(('dp', 'section')), may hold values from -6 to 6
- gain: float32 [1600], replicated, may hold values from 0.5 to 2
- expand_weight: bfloat16 [1600, 8192], P('dp', 'section'), may hold values from -0.15625 to 0.15625
- project_weight: bfloat16 [8192, 1600], P('section', 'dp'), may hold values from -0.0625 to 0.0625
- counts: int32 [8, 4], P('dp'), may hold values from 1 to 8
- positions: int32 [32, 8], P(('dp', 'section')), may hold values from 0 to 15, as said below
- text: bfloat16 [512, 1600], P(('dp', 'section')), may hold values from -6 to 6
- cotangent: bfloat16 [512, 1600], P(('dp', 'section')), may hold values from -6 to 6
Outputs:
- embedded: bfloat16 [512, 1600], P(('dp', 'section'))
- grad_rows: bfloat16 [256, 1600], P(('dp', 'section'))
- expand_grad: bfloat16 [1600, 8192], P(None, 'section')
- project_grad: bfloat16 [8192, 1600], P('section')
The draws below stay inside these ranges and needn't reach their ends.
Inputs may be any that keep to these rules, and one draw needn't show every extreme that they name: `positions`: within each row the values are distinct.
All inputs are finite; a program needn't handle non-finite values.
Results may differ from the reference program's by a relative error of at most 0.015.
Values may be sent and summed in bfloat16 or wider, within the bound.
No kernel may reach another device: no remote copies, remote signals or barrier semaphores. Data moves between devices by JAX's collectives and lax.ppermute only.
A program may use at most 64 MiB of HBM per device.

```python
import math
import jax
import jax.numpy as jnp
from jax import lax

DV = 1600
FF = 8192
CAP = 2
ROWS = 8
SEQ_DEV = 16
N_DP = 8
N_SECTION = 4


def draw_positions(key, part):
    subkeys = jax.random.split(jax.random.fold_in(key, 17), N_DP * N_SECTION)

    def one_row(subkey):
        return jax.random.permutation(subkey, SEQ_DEV)[:ROWS]
    return jax.vmap(one_row)(subkeys).astype(jnp.int32)


def place_ends(entries, rng, low, top_value):
    index_at = [jax.random.randint(jax.random.fold_in(rng, axis), (), 0, length) for axis, length in enumerate(entries.shape)]
    main_axis = entries.shape.index(max(entries.shape))
    next_to = index_at[:main_axis] + [(index_at[main_axis] + 1) % entries.shape[main_axis]] + index_at[main_axis + 1:]
    return entries.at[tuple(index_at)].set(low).at[tuple(next_to)].set(top_value)


def block_scale(stream_key, extent, cuts, smallest, largest):
    def one(position, shards_of):
        steps = jax.random.uniform(jax.random.fold_in(jax.random.fold_in(stream_key, 6), position), (shards_of,), jnp.float32, smallest / len(cuts), largest / len(cuts))
        return jnp.repeat(jnp.exp(steps), extent[position] // shards_of).reshape((-1,) + (1,) * (len(extent) - position - 1))

    level = one(*cuts[0])
    for cut in cuts[1:]:
        level = level * one(*cut)
    return level


def scatter_about(own_key, dims, spread, bound, pieces=(), held_as=jnp.bfloat16):
    values = spread * jax.random.normal(own_key, dims, jnp.float32)
    if pieces:
        values = values * block_scale(own_key, dims, pieces, -0.22, 0.18)
    return jnp.clip(values, -bound, bound).astype(held_as)


def setup_inputs(seed: int = 0) -> dict:
    key_list = jax.random.split(jax.random.key(seed), 9)
    patches = scatter_about(key_list[0], (N_DP * N_SECTION * ROWS, DV), 1.0, 6.0, ((0, 32),))
    gain = jnp.clip(jnp.exp(jax.random.uniform(key_list[1], (DV,), jnp.float32, math.log(0.5), math.log(2.0))), 0.5, 2.0)
    expand_weight = scatter_about(key_list[2], (DV, FF), DV ** -0.5, 0.15625, ((0, 8), (1, 4)))
    project_weight = scatter_about(key_list[3], (FF, DV), FF ** -0.5, 0.0625, ((0, 4), (1, 8)))
    counts = place_ends(jax.random.randint(key_list[4], (N_DP, N_SECTION), 1, ROWS + 1), jax.random.fold_in(key_list[4], 1), 1, ROWS).astype(jnp.int32)
    positions = draw_positions(jax.random.fold_in(key_list[8], 71), 0)
    text = scatter_about(key_list[6], (N_DP * N_SECTION * SEQ_DEV, DV), 1.0, 6.0, ((0, 32),))
    cotangent = scatter_about(key_list[7], (N_DP * N_SECTION * SEQ_DEV, DV), 1.0, 6.0, ((0, 32),))
    return dict(patches=patches, gain=gain, expand_weight=expand_weight, project_weight=project_weight, counts=counts, positions=positions, text=text, cotangent=cotangent)


def gelu_pair(values):
    coeff = 0.7978845608
    inner = coeff * (values + 0.044715 * values * values * values)
    tangent = jnp.tanh(inner)
    activated = 0.5 * values * (1.0 + tangent)
    derivative = 0.5 * (1.0 + tangent) + 0.5 * values * (1.0 - tangent * tangent) * coeff * (1.0 + 3.0 * 0.044715 * values * values)
    return (activated, derivative)

def block_round_sum(terms):
    rounded = lax.optimization_barrier(terms.astype(jnp.bfloat16))
    return lax.optimization_barrier(jnp.sum(rounded.astype(jnp.float32), axis=0))

def swap_order(array):
    return array.reshape(N_SECTION, N_SECTION, CAP, DV).transpose(1, 0, 2, 3).reshape(N_SECTION * ROWS, DV)

def reference(patches, gain, expand_weight, project_weight, counts, positions, text, cotangent):
    width = FF // N_SECTION
    group = N_SECTION * ROWS
    length = N_SECTION * SEQ_DEV
    expand_blocks = expand_weight.astype(jnp.float32).reshape(DV, N_SECTION, width).transpose(1, 0, 2)
    project_blocks = project_weight.astype(jnp.float32).reshape(N_SECTION, width, DV)
    dest_section = jnp.arange(N_SECTION, dtype=jnp.int32)[None, :, None]
    slot_offset = jnp.arange(CAP, dtype=jnp.int32)[None, None, :]
    bases = (jnp.arange(N_SECTION, dtype=jnp.int32) * SEQ_DEV)[:, None]

    def replica_step(carry, items):
        expand_acc, project_acc = carry
        patch_rows, count_row, position_rows, text_rows, cot_rows = items
        inputs = patch_rows.astype(jnp.float32)
        inv_rms = lax.rsqrt(lax.optimization_barrier(jnp.mean(inputs * inputs, axis=-1, keepdims=True)) + 1e-06)
        normed = (inputs * inv_rms * gain).astype(jnp.bfloat16)
        preact = jnp.dot(normed, expand_weight, preferred_element_type=jnp.float32)
        activated, derivative = gelu_pair(preact)
        hidden = activated.astype(jnp.bfloat16)
        parts = hidden.astype(jnp.float32).reshape(group, N_SECTION, width)
        mixed = block_round_sum(jnp.einsum('rnb,nbd->nrd', parts, project_blocks))
        out_rows = (inputs + mixed).astype(jnp.bfloat16)
        live_source = dest_section * CAP + slot_offset < count_row[:, None, None]
        is_live = live_source.transpose(1, 0, 2).reshape(group)[:, None]
        flat_index = (bases + position_rows).reshape(group).astype(jnp.int32)
        arriving = swap_order(out_rows)
        current = text_rows[flat_index]
        embedded_rows = text_rows.at[flat_index].set(jnp.where(is_live, arriving, current))
        picked = jnp.where(is_live, cot_rows[flat_index], jnp.zeros_like(current))
        grad_out = swap_order(picked).astype(jnp.bfloat16)
        grad_hidden = lax.dot_general(grad_out, project_weight, (((1,), (1,)), ((), ())), preferred_element_type=jnp.float32)
        grad_pre = (grad_hidden * derivative).astype(jnp.bfloat16)
        pre_parts = grad_pre.astype(jnp.float32).reshape(group, N_SECTION, width)
        grad_normed = block_round_sum(jnp.einsum('rnb,ndb->nrd', pre_parts, expand_blocks))
        scaled_grad = grad_normed * gain
        centred = lax.optimization_barrier(jnp.mean(scaled_grad * inputs, axis=-1, keepdims=True))
        grad_rows = (grad_out.astype(jnp.float32) + inv_rms * scaled_grad - inputs * inv_rms ** 3 * centred).astype(jnp.bfloat16)
        project_part = lax.dot_general(hidden, grad_out, (((0,), (0,)), ((), ())), preferred_element_type=jnp.float32)
        expand_part = lax.dot_general(normed, grad_pre, (((0,), (0,)), ((), ())), preferred_element_type=jnp.float32)
        project_part = lax.optimization_barrier(project_part.astype(jnp.bfloat16)).astype(jnp.float32)
        expand_part = lax.optimization_barrier(expand_part.astype(jnp.bfloat16)).astype(jnp.float32)
        return ((expand_acc + expand_part, project_acc + project_part), (embedded_rows, grad_rows))
    start = (jnp.zeros((DV, FF), jnp.float32), jnp.zeros((FF, DV), jnp.float32))
    items = (patches.reshape(N_DP, group, DV), counts, positions.reshape(N_DP, N_SECTION, ROWS), text.reshape(N_DP, length, DV), cotangent.reshape(N_DP, length, DV))
    totals, outputs = lax.scan(replica_step, start, items)
    embedded = outputs[0].reshape(N_DP * length, DV)
    grad_rows = outputs[1].reshape(N_DP * group, DV)
    return (embedded, grad_rows, totals[0].astype(jnp.bfloat16), totals[1].astype(jnp.bfloat16))
```

```python
import jax
import jax.numpy as jnp
from jax import lax
from jax.sharding import PartitionSpec as P


def gelu_pair(values):
    coeff = 0.7978845608
    inner = coeff * (values + 0.044715 * values * values * values)
    tangent = jnp.tanh(inner)
    activated = 0.5 * values * (1.0 + tangent)
    derivative = 0.5 * (1.0 + tangent) + 0.5 * values * (1.0 - tangent * tangent) * coeff * (
        1.0 + 3.0 * 0.044715 * values * values
    )
    return (activated, derivative)


def gather_weights_plan(
    patches, gain, expand_weight, project_weight, counts, positions, text, cotangent
):
    sections = lax.axis_size("section")
    slot_count = patches.shape[0]
    features = patches.shape[1]
    capacity = slot_count // sections
    inputs = patches.astype(jnp.float32)
    inv_rms = lax.rsqrt(jnp.mean(inputs * inputs, axis=-1, keepdims=True) + 1e-06)
    normed = (inputs * inv_rms * gain).astype(jnp.bfloat16)
    gathered = lax.all_gather(normed, "section", axis=0, tiled=True)
    expand_full, project_full = (
        lax.all_gather(expand_weight, "dp", axis=0, tiled=True),
        lax.all_gather(project_weight, "dp", axis=1, tiled=True),
    )
    preact = jnp.dot(gathered, expand_full, preferred_element_type=jnp.float32)
    activated, derivative = gelu_pair(preact)
    hidden = activated.astype(jnp.bfloat16)
    row_block = hidden
    mixed = lax.psum_scatter(
        jnp.dot(row_block, project_full, preferred_element_type=jnp.float32).astype(jnp.bfloat16),
        "section",
        scatter_dimension=0,
        tiled=True,
    ).astype(jnp.float32)
    out_rows = (inputs + mixed).astype(jnp.bfloat16)
    arrived = lax.all_to_all(out_rows, "section", split_axis=0, concat_axis=0, tiled=True)
    section_id = lax.axis_index("section")
    arrival = jnp.arange(slot_count, dtype=jnp.int32)
    source = arrival // capacity
    slot_index = section_id * capacity + arrival % capacity
    is_live = (slot_index < counts[0][source])[:, None]
    targets = positions[0]
    current = text[targets]
    embedded = text.at[targets].set(jnp.where(is_live, arrived, current))
    picked = jnp.where(is_live, cotangent[targets], jnp.zeros_like(current))
    collected = lax.all_gather(picked, "section", axis=0, tiled=True)
    grad_all = (
        collected.reshape(sections, sections, capacity, features)
        .transpose(1, 0, 2, 3)
        .reshape(sections * slot_count, features)
    )
    returned = lax.dynamic_slice_in_dim(grad_all, section_id * slot_count, slot_count, 0)
    grad_own = returned.astype(jnp.float32)
    project_local = lax.dot_general(
        hidden, grad_all, (((0,), (0,)), ((), ())), preferred_element_type=jnp.float32
    )
    grad_hidden = lax.dot_general(
        grad_all, project_full, (((1,), (1,)), ((), ())), preferred_element_type=jnp.float32
    )
    grad_pre = (grad_hidden * derivative).astype(jnp.bfloat16)
    row_block = grad_pre
    grad_normed = lax.psum_scatter(
        lax.dot_general(
            row_block, expand_full, (((1,), (1,)), ((), ())), preferred_element_type=jnp.float32
        ).astype(jnp.bfloat16),
        "section",
        scatter_dimension=0,
        tiled=True,
    ).astype(jnp.float32)
    expand_local = lax.dot_general(
        gathered, grad_pre, (((0,), (0,)), ((), ())), preferred_element_type=jnp.float32
    )
    project_total, expand_total = (
        lax.psum(project_local.astype(jnp.bfloat16), "dp").astype(jnp.float32),
        lax.psum(expand_local.astype(jnp.bfloat16), "dp").astype(jnp.float32),
    )
    scaled_grad = grad_normed * gain
    centred = jnp.mean(scaled_grad * inputs, axis=-1, keepdims=True)
    grad_rows = (grad_own + inv_rms * scaled_grad - inputs * inv_rms**3 * centred).astype(
        jnp.bfloat16
    )
    return (
        embedded,
        grad_rows,
        expand_total.astype(jnp.bfloat16),
        project_total.astype(jnp.bfloat16),
    )


def exchange_bits(size):
    bits = []
    step = 1
    while step < size:
        bits.append(step)
        step *= 2
    return bits


def swap(array, axis, step):
    size = lax.axis_size(axis)
    return lax.ppermute(array, axis, [(i, i ^ step) for i in range(size)])


def doubling_gather(array, axis, steps):
    me = lax.axis_index(axis)
    held = array.reshape((1,) * len(steps) + array.shape)
    for step in steps:
        level = len(steps) - 1 - (step.bit_length() - 1)
        got = swap(held, axis, step)
        high = (me // step) % 2 == 1
        held = jnp.where(
            high,
            jnp.concatenate([got, held], axis=level),
            jnp.concatenate([held, got], axis=level),
        )
    return held.reshape((lax.axis_size(axis),) + array.shape)


def move_rows_plan(
    patches, gain, expand_weight, project_weight, counts, positions, text, cotangent
):
    sections = lax.axis_size("section")
    replicas = lax.axis_size("dp")
    devices = sections * replicas
    slot_count, features = patches.shape
    part = expand_weight.shape[0]
    capacity = slot_count // sections
    rows = devices * slot_count
    section_id = lax.axis_index("section")
    replica_id = lax.axis_index("dp")

    expand_slice = lax.all_to_all(expand_weight, "dp", split_axis=1, concat_axis=0, tiled=True)
    project_slice = lax.all_to_all(project_weight, "dp", split_axis=0, concat_axis=1, tiled=True)

    arrival = jnp.arange(slot_count, dtype=jnp.int32)
    slot_index = section_id * capacity + arrival % capacity
    is_live = slot_index < jnp.repeat(counts[0], capacity)
    spots = jnp.arange(text.shape[0], dtype=jnp.int32)
    lands = (positions[0][:, None] == spots[None, :]) & is_live[:, None]
    chooser = lands.astype(jnp.bfloat16)
    picked = jnp.dot(chooser, cotangent, preferred_element_type=jnp.float32).astype(jnp.bfloat16)

    pair = jnp.concatenate([patches, picked], axis=0)
    over_dp = doubling_gather(pair, "dp", exchange_bits(replicas)[::-1])
    over_all = doubling_gather(over_dp, "section", exchange_bits(sections)[::-1])
    over_all = over_all.reshape(sections, replicas, 2, slot_count, features)
    inputs_all = over_all[:, :, 0].transpose(1, 0, 2, 3).reshape(rows, features)
    grad_all = (
        over_all[:, :, 1]
        .reshape(sections, replicas, sections, capacity, features)
        .transpose(1, 2, 0, 3, 4)
        .reshape(rows, features)
    )

    wide = inputs_all.astype(jnp.float32)
    inv_rms_all = lax.rsqrt(jnp.mean(wide * wide, axis=-1, keepdims=True) + 1e-06)
    normed = (wide * inv_rms_all * gain).astype(jnp.bfloat16)

    preact = jnp.dot(normed, expand_slice, preferred_element_type=jnp.float32)
    activated, derivative = gelu_pair(preact)
    hidden_part = activated.astype(jnp.bfloat16)
    grad_hidden = lax.dot_general(
        grad_all, project_slice, (((1,), (1,)), ((), ())), preferred_element_type=jnp.float32
    )
    grad_pre_part = (grad_hidden * derivative).astype(jnp.bfloat16)

    both = jnp.stack([hidden_part, grad_pre_part])
    spread = doubling_gather(both, "dp", exchange_bits(replicas)[::-1])
    spread = spread.transpose(1, 2, 0, 3).reshape(2, rows, -1)
    hidden, grad_pre = spread[0], spread[1]

    mixed_part = jnp.dot(hidden, project_weight, preferred_element_type=jnp.float32)
    grad_normed_part = lax.dot_general(
        grad_pre, expand_weight, (((1,), (1,)), ((), ())), preferred_element_type=jnp.float32
    )
    mixed_part = (
        mixed_part.astype(jnp.bfloat16)
        .reshape(replicas, sections, sections, capacity, part)
        .transpose(0, 2, 1, 3, 4)
        .reshape(devices, slot_count, part)
    )
    grad_normed_part = grad_normed_part.astype(jnp.bfloat16).reshape(devices, slot_count, part)
    tail = jnp.concatenate([mixed_part, grad_normed_part], axis=1)
    tail = lax.all_to_all(tail, ("dp", "section"), split_axis=0, concat_axis=0, tiled=True)
    tail = tail.reshape(replicas, sections, 2 * slot_count, part).astype(jnp.float32)
    tail = jnp.sum(tail, axis=1).transpose(1, 0, 2).reshape(2 * slot_count, features)
    mixed, grad_normed = tail[:slot_count], tail[slot_count:]

    expand_grad = lax.dot_general(
        normed, grad_pre, (((0,), (0,)), ((), ())), preferred_element_type=jnp.float32
    ).astype(jnp.bfloat16)
    project_grad = lax.dot_general(
        hidden, grad_all, (((0,), (0,)), ((), ())), preferred_element_type=jnp.float32
    ).astype(jnp.bfloat16)

    group = sections * slot_count
    mine = lax.dynamic_slice_in_dim(inputs_all, replica_id * group, group, 0)
    mine = mine.reshape(sections, sections, capacity, features)
    coming = lax.dynamic_index_in_dim(mine, section_id, 1, keepdims=False)
    coming = coming.reshape(slot_count, features)
    out_rows = (coming.astype(jnp.float32) + mixed).astype(jnp.bfloat16)
    placed = lax.dot_general(
        chooser, out_rows, (((0,), (0,)), ((), ())), preferred_element_type=jnp.float32
    ).astype(jnp.bfloat16)
    taken = jnp.any(lands, axis=0)[:, None]
    embedded = jnp.where(taken, placed, text)

    inputs = patches.astype(jnp.float32)
    inv_rms = lax.rsqrt(jnp.mean(inputs * inputs, axis=-1, keepdims=True) + 1e-06)
    grad_own = lax.dynamic_slice_in_dim(
        grad_all, (replica_id * sections + section_id) * slot_count, slot_count, 0
    ).astype(jnp.float32)
    scaled_grad = grad_normed * gain
    centred = jnp.mean(scaled_grad * inputs, axis=-1, keepdims=True)
    grad_rows = (grad_own + inv_rms * scaled_grad - inputs * inv_rms**3 * centred).astype(
        jnp.bfloat16
    )
    return (embedded, grad_rows, expand_grad, project_grad)


def shards(patches, gain, expand_weight, project_weight, counts, positions, text, cotangent):
    replicas, sections = lax.axis_size("dp"), lax.axis_size("section")
    slot_count, features = patches.shape
    units = expand_weight.shape[1]
    rows = replicas * sections * slot_count
    powers = replicas & (replicas - 1) == 0 and sections & (sections - 1) == 0
    if powers and units % replicas == 0 and rows * (features + units) <= features * units:
        plan = move_rows_plan
    else:
        plan = gather_weights_plan
    return plan(
        patches, gain, expand_weight, project_weight, counts, positions, text, cotangent
    )


def solution(mesh):
    return jax.shard_map(
        shards,
        mesh=mesh,
        in_specs=(
            P(("dp", "section"), None),
            P(),
            P("dp", "section"),
            P("section", "dp"),
            P("dp", None),
            P(("dp", "section"), None),
            P(("dp", "section"), None),
            P(("dp", "section"), None),
        ),
        out_specs=(
            P(("dp", "section"), None),
            P(("dp", "section"), None),
            P(None, "section"),
            P("section", None),
        ),
        check_vma=False,
    )
```

```python
import functools

import jax
import jax.numpy as jnp
from jax import lax
from jax.experimental import pallas as pl
from jax.experimental.pallas import tpu as pltpu
from jax.sharding import PartitionSpec as P


def gelu_pair(values):
    coeff = 0.7978845608
    inner = coeff * (values + 0.044715 * values * values * values)
    tangent = jnp.tanh(inner)
    activated = 0.5 * values * (1.0 + tangent)
    derivative = 0.5 * (1.0 + tangent) + 0.5 * values * (1.0 - tangent * tangent) * coeff * (
        1.0 + 3.0 * 0.044715 * values * values
    )
    return (activated, derivative)


def gather_weights_plan(
    patches, gain, expand_weight, project_weight, counts, positions, text, cotangent
):
    sections = lax.axis_size("section")
    slot_count = patches.shape[0]
    features = patches.shape[1]
    capacity = slot_count // sections
    inputs = patches.astype(jnp.float32)
    inv_rms = lax.rsqrt(jnp.mean(inputs * inputs, axis=-1, keepdims=True) + 1e-06)
    normed = (inputs * inv_rms * gain).astype(jnp.bfloat16)
    gathered = lax.all_gather(normed, "section", axis=0, tiled=True)
    expand_full, project_full = (
        lax.all_gather(expand_weight, "dp", axis=0, tiled=True),
        lax.all_gather(project_weight, "dp", axis=1, tiled=True),
    )
    preact = jnp.dot(gathered, expand_full, preferred_element_type=jnp.float32)
    activated, derivative = gelu_pair(preact)
    hidden = activated.astype(jnp.bfloat16)
    row_block = hidden
    mixed = lax.psum_scatter(
        jnp.dot(row_block, project_full, preferred_element_type=jnp.float32).astype(jnp.bfloat16),
        "section",
        scatter_dimension=0,
        tiled=True,
    ).astype(jnp.float32)
    out_rows = (inputs + mixed).astype(jnp.bfloat16)
    arrived = lax.all_to_all(out_rows, "section", split_axis=0, concat_axis=0, tiled=True)
    section_id = lax.axis_index("section")
    arrival = jnp.arange(slot_count, dtype=jnp.int32)
    source = arrival // capacity
    slot_index = section_id * capacity + arrival % capacity
    is_live = (slot_index < counts[0][source])[:, None]
    targets = positions[0]
    current = text[targets]
    embedded = text.at[targets].set(jnp.where(is_live, arrived, current))
    picked = jnp.where(is_live, cotangent[targets], jnp.zeros_like(current))
    collected = lax.all_gather(picked, "section", axis=0, tiled=True)
    grad_all = (
        collected.reshape(sections, sections, capacity, features)
        .transpose(1, 0, 2, 3)
        .reshape(sections * slot_count, features)
    )
    returned = lax.dynamic_slice_in_dim(grad_all, section_id * slot_count, slot_count, 0)
    grad_own = returned.astype(jnp.float32)
    project_local = lax.dot_general(
        hidden, grad_all, (((0,), (0,)), ((), ())), preferred_element_type=jnp.float32
    )
    grad_hidden = lax.dot_general(
        grad_all, project_full, (((1,), (1,)), ((), ())), preferred_element_type=jnp.float32
    )
    grad_pre = (grad_hidden * derivative).astype(jnp.bfloat16)
    row_block = grad_pre
    grad_normed = lax.psum_scatter(
        lax.dot_general(
            row_block, expand_full, (((1,), (1,)), ((), ())), preferred_element_type=jnp.float32
        ).astype(jnp.bfloat16),
        "section",
        scatter_dimension=0,
        tiled=True,
    ).astype(jnp.float32)
    expand_local = lax.dot_general(
        gathered, grad_pre, (((0,), (0,)), ((), ())), preferred_element_type=jnp.float32
    )
    project_total, expand_total = (
        lax.psum(project_local.astype(jnp.bfloat16), "dp").astype(jnp.float32),
        lax.psum(expand_local.astype(jnp.bfloat16), "dp").astype(jnp.float32),
    )
    scaled_grad = grad_normed * gain
    centred = jnp.mean(scaled_grad * inputs, axis=-1, keepdims=True)
    grad_rows = (grad_own + inv_rms * scaled_grad - inputs * inv_rms**3 * centred).astype(
        jnp.bfloat16
    )
    return (
        embedded,
        grad_rows,
        expand_total.astype(jnp.bfloat16),
        project_total.astype(jnp.bfloat16),
    )


def bit_steps(size):
    steps = []
    step = size // 2
    while step >= 1:
        steps.append(step)
        step //= 2
    return steps


def swap(array, axis, step):
    size = lax.axis_size(axis)
    return lax.ppermute(array, axis, [(i, i ^ step) for i in range(size)])


def masked_steps(index, steps):
    mask = 0
    for place, step in enumerate(steps):
        mask = mask + ((index >> place) & 1) * step
    return mask


VMEM_SPEC = pl.BlockSpec(memory_space=pltpu.VMEM)
SMEM_SPEC = pl.BlockSpec(memory_space=pltpu.SMEM)


def log2(value):
    return value.bit_length() - 1


def landing(place_ref, count_ref, section, slots, capacity, length):
    row = lax.broadcasted_iota(jnp.int32, (slots, length), 0)
    column = lax.broadcasted_iota(jnp.int32, (slots, length), 1)
    spot = jnp.full((slots, length), -1, jnp.int32)
    for q in range(slots):
        live = section * capacity + q % capacity < count_ref[0, q // capacity]
        spot = jnp.where(row == q, jnp.where(live, place_ref[0, q], -1), spot)
    return (spot == column).astype(jnp.float32)


def pick_kernel(capacity, me_ref, count_ref, place_ref, patch_ref, cotangent_ref, pair_ref):
    slots = patch_ref.shape[0]
    chooser = landing(
        place_ref, count_ref, me_ref[1], slots, capacity, cotangent_ref.shape[0]
    ).astype(jnp.bfloat16)
    picked = jnp.dot(chooser, cotangent_ref[...], preferred_element_type=jnp.float32)
    pair_ref[0] = jnp.concatenate(
        [patch_ref[...].astype(jnp.float32), picked], axis=0
    ).astype(jnp.bfloat16)


def repack_kernel(expand_ref, project_ref, out_ref):
    units = out_ref.shape[3]
    for d in range(out_ref.shape[0]):
        out_ref[d, 0] = expand_ref[:, d * units : (d + 1) * units]
        out_ref[d, 1] = project_ref[:, d * units : (d + 1) * units]


def order_kernel(
    sections, capacity, dp_steps, section_steps,
    me_ref, near_ref, far_ref, gain_ref, normed_ref, grad_ref, extra_ref,
):
    rows = normed_ref.shape[0]
    slots = sections * capacity
    half = near_ref.shape[0] * near_ref.shape[1]
    me_dp, me_section = me_ref[0], me_ref[1]
    column = lax.broadcasted_iota(jnp.int32, (8, half), 1)
    row = lax.broadcasted_iota(jnp.int32, (rows, half), 0)
    kind = column & (2 * slots - 1)
    slot = kind & (slots - 1)
    inputs = grad = None
    for side, ref in enumerate((near_ref, far_ref)):
        block = (column >> log2(2 * slots)) + side * (half // (2 * slots))
        source_dp = me_dp ^ masked_steps(block, dp_steps)
        source_section = me_section ^ masked_steps(block >> len(dp_steps), section_steps)
        patch_at = (source_dp * sections + source_section) * slots + slot
        grad_at = (
            (source_dp * sections + (slot >> log2(capacity))) * slots
            + source_section * capacity
            + (slot & (capacity - 1))
        )
        patch_at = jnp.where(kind < slots, patch_at, -1)[:1]
        grad_at = jnp.where(kind >= slots, grad_at, -1)[:1]
        values = ref[...].reshape(half, ref.shape[2])
        chosen = (row == patch_at).astype(jnp.float32).astype(jnp.bfloat16)
        found = jnp.dot(chosen, values, preferred_element_type=jnp.float32)
        inputs = found if inputs is None else inputs + found
        chosen = (row == grad_at).astype(jnp.float32).astype(jnp.bfloat16)
        found = jnp.dot(chosen, values, preferred_element_type=jnp.float32)
        grad = found if grad is None else grad + found
    inv_rms = lax.rsqrt(jnp.mean(inputs * inputs, axis=-1, keepdims=True) + 1e-06)
    normed_ref[...] = (inputs * inv_rms * gain_ref[...]).astype(jnp.bfloat16)
    grad = grad.astype(jnp.bfloat16)
    grad_ref[...] = grad
    mine = lax.broadcasted_iota(jnp.int32, (slots, rows), 0)
    every = lax.broadcasted_iota(jnp.int32, (slots, rows), 1)
    coming_at = (
        (me_dp * sections + (mine >> log2(capacity))) * slots
        + me_section * capacity
        + (mine & (capacity - 1))
    )
    own_at = (me_dp * sections + me_section) * slots + mine
    coming = jnp.dot(
        (every == coming_at).astype(jnp.float32).astype(jnp.bfloat16),
        inputs.astype(jnp.bfloat16),
        preferred_element_type=jnp.float32,
    )
    own = jnp.dot(
        (every == own_at).astype(jnp.float32).astype(jnp.bfloat16),
        grad,
        preferred_element_type=jnp.float32,
    )
    extra_ref[...] = jnp.concatenate([coming, own], axis=0)


def hidden_kernel(normed_ref, grad_ref, turned_ref, both_ref, expand_ref, project_ref):
    part = turned_ref.shape[2]
    for d in range(turned_ref.shape[0]):
        expand_ref[d * part : (d + 1) * part, :] = turned_ref[d, 0]
        project_ref[d * part : (d + 1) * part, :] = turned_ref[d, 1]
    preact = jnp.dot(normed_ref[...], expand_ref[...], preferred_element_type=jnp.float32)
    activated, derivative = gelu_pair(preact)
    both_ref[0] = activated.astype(jnp.bfloat16)
    grad_hidden = jnp.dot(grad_ref[...], project_ref[...], preferred_element_type=jnp.float32)
    both_ref[1] = (grad_hidden * derivative).astype(jnp.bfloat16)


def share_kernel(
    sections, capacity, dp_steps, me_ref, near_ref, far_ref, expand_ref, project_ref, out_ref
):
    blocks, _, rows, units = near_ref.shape
    devices, _, part = out_ref.shape
    slots = sections * capacity
    mixed = jnp.zeros((rows, part), jnp.float32)
    grad_normed = jnp.zeros((rows, part), jnp.float32)
    for side, ref in enumerate((near_ref, far_ref)):
        for i in range(blocks):
            source = me_ref[0] ^ masked_steps(side * blocks + i, dp_steps)
            columns = pl.ds(pl.multiple_of(source * units, 128), units)
            mixed += lax.dot_general(
                ref[i, 0], project_ref[:, columns],
                (((1,), (1,)), ((), ())), preferred_element_type=jnp.float32,
            )
            grad_normed += lax.dot_general(
                ref[i, 1], expand_ref[:, columns],
                (((1,), (1,)), ((), ())), preferred_element_type=jnp.float32,
            )
    row = lax.broadcasted_iota(jnp.int32, (rows, rows), 0)
    column = lax.broadcasted_iota(jnp.int32, (rows, rows), 1)
    inside = row & (slots - 1)
    text_section = (row >> log2(slots)) & (sections - 1)
    source_row = (
        (row >> log2(slots * sections)) * (slots * sections)
        + (inside >> log2(capacity)) * slots
        + text_section * capacity
        + (inside & (capacity - 1))
    )
    turn = (column == source_row).astype(jnp.float32).astype(jnp.bfloat16)
    mixed = jnp.dot(turn, mixed.astype(jnp.bfloat16), preferred_element_type=jnp.float32)
    out_ref[:, :slots, :] = mixed.reshape(devices, slots, part).astype(jnp.bfloat16)
    out_ref[:, slots:, :] = grad_normed.reshape(devices, slots, part).astype(jnp.bfloat16)


def weight_grad_kernel(me_ref, block_ref, normed_ref, grad_ref, *refs):
    expand_ref, project_ref = refs[-2:]
    contract = (((0,), (0,)), ((), ()))
    expand_ref[...] = lax.dot_general(
        normed_ref[...], block_ref[0, 1], contract, preferred_element_type=jnp.float32
    ).astype(jnp.bfloat16)
    project_ref[...] = lax.dot_general(
        grad_ref[...], block_ref[0, 0], contract, preferred_element_type=jnp.float32
    ).astype(jnp.bfloat16)


def finish_kernel(
    sections, capacity,
    me_ref, count_ref, place_ref, tail_ref, extra_ref, patch_ref, text_ref, gain_ref,
    embedded_ref, grad_rows_ref, sum_ref,
):
    devices, _, part = tail_ref.shape
    slots = patch_ref.shape[0]
    for d in range(devices // sections):
        total = tail_ref[d * sections].astype(jnp.float32)
        for s in range(1, sections):
            total += tail_ref[d * sections + s].astype(jnp.float32)
        sum_ref[:, d * part : (d + 1) * part] = total
    mixed, grad_normed = sum_ref[:slots, :], sum_ref[slots:, :]
    out_rows = (extra_ref[:slots, :] + mixed).astype(jnp.bfloat16)
    length = text_ref.shape[0]
    chooser = landing(place_ref, count_ref, me_ref[1], slots, capacity, length)
    contract = (((0,), (0,)), ((), ()))
    placed = lax.dot_general(
        chooser.astype(jnp.bfloat16), out_rows, contract, preferred_element_type=jnp.float32
    )
    taken = lax.dot_general(
        chooser.astype(jnp.bfloat16), jnp.ones((slots, 128), jnp.bfloat16),
        contract, preferred_element_type=jnp.float32,
    )[:, :1]
    embedded_ref[...] = jnp.where(
        taken > 0.5, placed, text_ref[...].astype(jnp.float32)
    ).astype(jnp.bfloat16)
    inputs = patch_ref[...].astype(jnp.float32)
    inv_rms = lax.rsqrt(jnp.mean(inputs * inputs, axis=-1, keepdims=True) + 1e-06)
    scaled_grad = grad_normed * gain_ref[...]
    centred = jnp.mean(scaled_grad * inputs, axis=-1, keepdims=True)
    grad_rows_ref[...] = (
        extra_ref[slots:, :] + inv_rms * scaled_grad - inputs * (inv_rms**3 * centred)
    ).astype(jnp.bfloat16)


def weight_grads(me, blocks, first_index, dp_steps, normed, grad_all, width, before):
    count, _, rows, units = blocks.shape
    features = normed.shape[1]

    def where_to(i, me_ref):
        return me_ref[0] ^ masked_steps(first_index + i, dp_steps)

    whole = pl.BlockSpec((rows, features), lambda i, me_ref: (0, 0))
    in_specs = [
        pl.BlockSpec((1, 2, rows, units), lambda i, me_ref: (i, 0, 0, 0)), whole, whole
    ] + [pl.BlockSpec(memory_space=pl.ANY)] * len(before)
    return pl.pallas_call(
        weight_grad_kernel,
        grid_spec=pltpu.PrefetchScalarGridSpec(
            num_scalar_prefetch=1,
            grid=(count,),
            in_specs=in_specs,
            out_specs=[
                pl.BlockSpec((features, units), lambda i, me_ref: (0, where_to(i, me_ref)))
            ] * 2,
        ),
        out_shape=[jax.ShapeDtypeStruct((features, width), jnp.bfloat16)] * 2,
        input_output_aliases={4: 0, 5: 1} if before else {},
        compiler_params=pltpu.CompilerParams(
            dimension_semantics=("arbitrary",), vmem_limit_bytes=24 << 20
        ),
        cost_estimate=pl.CostEstimate(
            flops=4 * count * rows * features * units,
            bytes_accessed=4 * count * units * features + 4 * rows * features,
            transcendentals=0,
        ),
    )(me, blocks, normed, grad_all, *before)


def call(kernel, out_shape, smem, vmem, scratch=()):
    single = not isinstance(out_shape, (list, tuple))
    return pl.pallas_call(
        kernel,
        out_shape=out_shape,
        in_specs=[SMEM_SPEC] * len(smem) + [VMEM_SPEC] * len(vmem),
        out_specs=VMEM_SPEC if single else [VMEM_SPEC] * len(out_shape),
        scratch_shapes=scratch,
        compiler_params=pltpu.CompilerParams(vmem_limit_bytes=24 << 20),
    )(*smem, *vmem)


def move_rows_plan(
    patches, gain, expand_weight, project_weight, counts, positions, text, cotangent
):
    sections = lax.axis_size("section")
    replicas = lax.axis_size("dp")
    devices = sections * replicas
    slots, features = patches.shape
    part, width = expand_weight.shape
    units = width // replicas
    capacity = slots // sections
    rows = devices * slots
    dp_steps, section_steps = bit_steps(replicas), bit_steps(sections)
    me = jnp.stack([lax.axis_index("dp"), lax.axis_index("section")]).astype(jnp.int32)
    gain = gain.reshape(1, features)
    project_turned = project_weight.T
    kept, wide = jnp.bfloat16, jnp.float32
    shape = jax.ShapeDtypeStruct

    stacked = call(
        repack_kernel,
        shape((replicas, 2, part, units), kept),
        (), (expand_weight, project_turned),
    )
    turned = lax.all_to_all(stacked, "dp", split_axis=0, concat_axis=0, tiled=True)

    held = call(
        functools.partial(pick_kernel, capacity),
        shape((1, 2 * slots, features), kept),
        (me, counts, positions), (patches, cotangent),
    )
    for axis, step in [("dp", s) for s in dp_steps] + [("section", s) for s in section_steps]:
        got = swap(held, axis, step)
        if held.shape[0] < devices // 2:
            held = jnp.concatenate([held, got], axis=0)
    normed, grad_all, extra = call(
        functools.partial(order_kernel, sections, capacity, dp_steps, section_steps),
        [shape((rows, features), kept), shape((rows, features), kept), shape((2 * slots, features), wide)],
        (me,), (held, got, gain),
    )

    both = call(
        hidden_kernel,
        shape((2, rows, units), kept),
        (), (normed, grad_all, turned),
        [pltpu.VMEM((features, units), kept)] * 2,
    )

    near = both[None]
    for step in dp_steps:
        far = swap(near, "dp", step)
        if near.shape[0] < replicas // 2:
            near = jnp.concatenate([near, far], axis=0)

    grads = weight_grads(me, near, 0, dp_steps, normed, grad_all, width, ())
    tail = call(
        functools.partial(share_kernel, sections, capacity, dp_steps),
        shape((devices, 2 * slots, part), kept),
        (me,), (near, far, expand_weight, project_turned),
    )
    tail = lax.all_to_all(
        tail, ("dp", "section"), split_axis=0, concat_axis=0, tiled=True
    )
    expand_grad, project_grad = weight_grads(
        me, far, replicas // 2, dp_steps, normed, grad_all, width, grads
    )
    embedded, grad_rows = call(
        functools.partial(finish_kernel, sections, capacity),
        [shape(text.shape, kept), shape(patches.shape, kept)],
        (me, counts, positions), (tail, extra, patches, text, gain),
        [pltpu.VMEM((2 * slots, features), wide)],
    )
    return (embedded, grad_rows, expand_grad, project_grad.T)


def power_of_two(value):
    return value > 0 and value & (value - 1) == 0


def shards(patches, gain, expand_weight, project_weight, counts, positions, text, cotangent):
    replicas, sections = lax.axis_size("dp"), lax.axis_size("section")
    slots, features = patches.shape
    width = expand_weight.shape[1]
    rows = replicas * sections * slots
    fits = rows * (features + width) <= features * width
    even = (
        all(power_of_two(n) for n in (replicas, sections, slots))
        and replicas > 1
        and sections > 1
        and slots % 8 == 0
        and width % (128 * replicas) == 0
    )
    if fits and even:
        plan = move_rows_plan
    else:
        plan = gather_weights_plan
    return plan(
        patches, gain, expand_weight, project_weight, counts, positions, text, cotangent
    )


def solution(mesh):
    return jax.shard_map(
        shards,
        mesh=mesh,
        in_specs=(
            P(("dp", "section"), None),
            P(),
            P("dp", "section"),
            P("section", "dp"),
            P("dp", None),
            P(("dp", "section"), None),
            P(("dp", "section"), None),
            P(("dp", "section"), None),
        ),
        out_specs=(
            P(("dp", "section"), None),
            P(("dp", "section"), None),
            P(None, "section"),
            P("section", None),
        ),
        check_vma=False,
    )
```

```python
import functools

import jax
import jax.numpy as jnp
from jax import lax
from jax.experimental import pallas as pl
from jax.experimental.pallas import tpu as pltpu
from jax.sharding import PartitionSpec as P


def gelu_pair(values):
    coeff = 0.7978845608
    inner = coeff * (values + 0.044715 * values * values * values)
    tangent = jnp.tanh(inner)
    activated = 0.5 * values * (1.0 + tangent)
    derivative = 0.5 * (1.0 + tangent) + 0.5 * values * (1.0 - tangent * tangent) * coeff * (
        1.0 + 3.0 * 0.044715 * values * values
    )
    return (activated, derivative)


def gather_weights_plan(
    patches, gain, expand_weight, project_weight, counts, positions, text, cotangent
):
    sections = lax.axis_size("section")
    slot_count = patches.shape[0]
    features = patches.shape[1]
    capacity = slot_count // sections
    inputs = patches.astype(jnp.float32)
    inv_rms = lax.rsqrt(jnp.mean(inputs * inputs, axis=-1, keepdims=True) + 1e-06)
    normed = (inputs * inv_rms * gain).astype(jnp.bfloat16)
    gathered = lax.all_gather(normed, "section", axis=0, tiled=True)
    expand_full, project_full = (
        lax.all_gather(expand_weight, "dp", axis=0, tiled=True),
        lax.all_gather(project_weight, "dp", axis=1, tiled=True),
    )
    preact = jnp.dot(gathered, expand_full, preferred_element_type=jnp.float32)
    activated, derivative = gelu_pair(preact)
    hidden = activated.astype(jnp.bfloat16)
    row_block = hidden
    mixed = lax.psum_scatter(
        jnp.dot(row_block, project_full, preferred_element_type=jnp.float32).astype(jnp.bfloat16),
        "section",
        scatter_dimension=0,
        tiled=True,
    ).astype(jnp.float32)
    out_rows = (inputs + mixed).astype(jnp.bfloat16)
    arrived = lax.all_to_all(out_rows, "section", split_axis=0, concat_axis=0, tiled=True)
    section_id = lax.axis_index("section")
    arrival = jnp.arange(slot_count, dtype=jnp.int32)
    source = arrival // capacity
    slot_index = section_id * capacity + arrival % capacity
    is_live = (slot_index < counts[0][source])[:, None]
    targets = positions[0]
    current = text[targets]
    embedded = text.at[targets].set(jnp.where(is_live, arrived, current))
    picked = jnp.where(is_live, cotangent[targets], jnp.zeros_like(current))
    collected = lax.all_gather(picked, "section", axis=0, tiled=True)
    grad_all = (
        collected.reshape(sections, sections, capacity, features)
        .transpose(1, 0, 2, 3)
        .reshape(sections * slot_count, features)
    )
    returned = lax.dynamic_slice_in_dim(grad_all, section_id * slot_count, slot_count, 0)
    grad_own = returned.astype(jnp.float32)
    project_local = lax.dot_general(
        hidden, grad_all, (((0,), (0,)), ((), ())), preferred_element_type=jnp.float32
    )
    grad_hidden = lax.dot_general(
        grad_all, project_full, (((1,), (1,)), ((), ())), preferred_element_type=jnp.float32
    )
    grad_pre = (grad_hidden * derivative).astype(jnp.bfloat16)
    row_block = grad_pre
    grad_normed = lax.psum_scatter(
        lax.dot_general(
            row_block, expand_full, (((1,), (1,)), ((), ())), preferred_element_type=jnp.float32
        ).astype(jnp.bfloat16),
        "section",
        scatter_dimension=0,
        tiled=True,
    ).astype(jnp.float32)
    expand_local = lax.dot_general(
        gathered, grad_pre, (((0,), (0,)), ((), ())), preferred_element_type=jnp.float32
    )
    project_total, expand_total = (
        lax.psum(project_local.astype(jnp.bfloat16), "dp").astype(jnp.float32),
        lax.psum(expand_local.astype(jnp.bfloat16), "dp").astype(jnp.float32),
    )
    scaled_grad = grad_normed * gain
    centred = jnp.mean(scaled_grad * inputs, axis=-1, keepdims=True)
    grad_rows = (grad_own + inv_rms * scaled_grad - inputs * inv_rms**3 * centred).astype(
        jnp.bfloat16
    )
    return (
        embedded,
        grad_rows,
        expand_total.astype(jnp.bfloat16),
        project_total.astype(jnp.bfloat16),
    )


def bit_steps(size):
    steps = []
    step = size // 2
    while step >= 1:
        steps.append(step)
        step //= 2
    return steps


def swap(array, axis, step):
    size = lax.axis_size(axis)
    return lax.ppermute(array, axis, [(i, i ^ step) for i in range(size)])


def masked_steps(index, steps):
    mask = 0
    for place, step in enumerate(steps):
        mask = mask + ((index >> place) & 1) * step
    return mask


VMEM_SPEC = pl.BlockSpec(memory_space=pltpu.VMEM)
SMEM_SPEC = pl.BlockSpec(memory_space=pltpu.SMEM)


def log2(value):
    return value.bit_length() - 1


def landing(place_ref, count_ref, section, slots, capacity, length):
    row = lax.broadcasted_iota(jnp.int32, (slots, length), 0)
    column = lax.broadcasted_iota(jnp.int32, (slots, length), 1)
    spot = jnp.full((slots, length), -1, jnp.int32)
    for q in range(slots):
        live = section * capacity + q % capacity < count_ref[0, q // capacity]
        spot = jnp.where(row == q, jnp.where(live, place_ref[0, q], -1), spot)
    return (spot == column).astype(jnp.float32)


def pick_kernel(capacity, me_ref, count_ref, place_ref, patch_ref, cotangent_ref, pair_ref):
    slots = patch_ref.shape[0]
    chooser = landing(
        place_ref, count_ref, me_ref[1], slots, capacity, cotangent_ref.shape[0]
    ).astype(jnp.bfloat16)
    picked = jnp.dot(chooser, cotangent_ref[...], preferred_element_type=jnp.float32)
    pair_ref[0] = jnp.concatenate(
        [patch_ref[...].astype(jnp.float32), picked], axis=0
    ).astype(jnp.bfloat16)


def repack_kernel(expand_ref, project_ref, out_ref):
    units = out_ref.shape[3]
    for d in range(out_ref.shape[0]):
        out_ref[d, 0] = expand_ref[:, d * units : (d + 1) * units]
        out_ref[d, 1] = project_ref[:, d * units : (d + 1) * units]


def order_kernel(
    sections, capacity, dp_steps, section_steps,
    me_ref, near_ref, far_ref, gain_ref, normed_ref, grad_ref, extra_ref,
):
    rows = normed_ref.shape[0]
    slots = sections * capacity
    half = near_ref.shape[0] * near_ref.shape[1]
    me_dp, me_section = me_ref[0], me_ref[1]
    column = lax.broadcasted_iota(jnp.int32, (8, half), 1)
    row = lax.broadcasted_iota(jnp.int32, (rows, half), 0)
    kind = column & (2 * slots - 1)
    slot = kind & (slots - 1)
    inputs = grad = None
    for side, ref in enumerate((near_ref, far_ref)):
        block = (column >> log2(2 * slots)) + side * (half // (2 * slots))
        source_dp = me_dp ^ masked_steps(block, dp_steps)
        source_section = me_section ^ masked_steps(block >> len(dp_steps), section_steps)
        patch_at = (source_dp * sections + source_section) * slots + slot
        grad_at = (
            (source_dp * sections + (slot >> log2(capacity))) * slots
            + source_section * capacity
            + (slot & (capacity - 1))
        )
        patch_at = jnp.where(kind < slots, patch_at, -1)[:1]
        grad_at = jnp.where(kind >= slots, grad_at, -1)[:1]
        values = ref[...].reshape(half, ref.shape[2])
        chosen = (row == patch_at).astype(jnp.float32).astype(jnp.bfloat16)
        found = jnp.dot(chosen, values, preferred_element_type=jnp.float32)
        inputs = found if inputs is None else inputs + found
        chosen = (row == grad_at).astype(jnp.float32).astype(jnp.bfloat16)
        found = jnp.dot(chosen, values, preferred_element_type=jnp.float32)
        grad = found if grad is None else grad + found
    inv_rms = lax.rsqrt(jnp.mean(inputs * inputs, axis=-1, keepdims=True) + 1e-06)
    normed_ref[...] = (inputs * inv_rms * gain_ref[...]).astype(jnp.bfloat16)
    grad = grad.astype(jnp.bfloat16)
    grad_ref[...] = grad
    mine = lax.broadcasted_iota(jnp.int32, (slots, rows), 0)
    every = lax.broadcasted_iota(jnp.int32, (slots, rows), 1)
    coming_at = (
        (me_dp * sections + (mine >> log2(capacity))) * slots
        + me_section * capacity
        + (mine & (capacity - 1))
    )
    own_at = (me_dp * sections + me_section) * slots + mine
    coming = jnp.dot(
        (every == coming_at).astype(jnp.float32).astype(jnp.bfloat16),
        inputs.astype(jnp.bfloat16),
        preferred_element_type=jnp.float32,
    )
    own = jnp.dot(
        (every == own_at).astype(jnp.float32).astype(jnp.bfloat16),
        grad,
        preferred_element_type=jnp.float32,
    )
    extra_ref[...] = jnp.concatenate([coming, own], axis=0)


def hidden_kernel(
    normed_ref, grad_ref, turned_ref, hidden_ref, pre_ref, expand_ref, project_ref
):
    part = turned_ref.shape[2]
    for d in range(turned_ref.shape[0]):
        expand_ref[d * part : (d + 1) * part, :] = turned_ref[d, 0]
        project_ref[d * part : (d + 1) * part, :] = turned_ref[d, 1]
    preact = jnp.dot(normed_ref[...], expand_ref[...], preferred_element_type=jnp.float32)
    activated, derivative = gelu_pair(preact)
    hidden_ref[0] = activated.astype(jnp.bfloat16)
    grad_hidden = jnp.dot(grad_ref[...], project_ref[...], preferred_element_type=jnp.float32)
    pre_ref[0] = (grad_hidden * derivative).astype(jnp.bfloat16)


def share_kernel(
    sections, capacity, hidden_steps, pre_steps,
    me_ref, hidden_near_ref, hidden_far_ref, pre_near_ref, pre_far_ref,
    expand_ref, project_ref, out_ref,
):
    blocks, rows, units = hidden_near_ref.shape
    devices, _, part = out_ref.shape
    slots = sections * capacity

    def product(near_ref, far_ref, weight_ref, steps):
        total = jnp.zeros((rows, part), jnp.float32)
        for side, ref in enumerate((near_ref, far_ref)):
            for i in range(blocks):
                source = me_ref[0] ^ masked_steps(side * blocks + i, steps)
                columns = pl.ds(pl.multiple_of(source * units, 128), units)
                total += lax.dot_general(
                    ref[i], weight_ref[:, columns],
                    (((1,), (1,)), ((), ())), preferred_element_type=jnp.float32,
                )
        return total

    mixed = product(hidden_near_ref, hidden_far_ref, project_ref, hidden_steps)
    grad_normed = product(pre_near_ref, pre_far_ref, expand_ref, pre_steps)
    row = lax.broadcasted_iota(jnp.int32, (rows, rows), 0)
    column = lax.broadcasted_iota(jnp.int32, (rows, rows), 1)
    inside = row & (slots - 1)
    text_section = (row >> log2(slots)) & (sections - 1)
    source_row = (
        (row >> log2(slots * sections)) * (slots * sections)
        + (inside >> log2(capacity)) * slots
        + text_section * capacity
        + (inside & (capacity - 1))
    )
    turn = (column == source_row).astype(jnp.float32).astype(jnp.bfloat16)
    mixed = jnp.dot(turn, mixed.astype(jnp.bfloat16), preferred_element_type=jnp.float32)
    out_ref[:, :slots, :] = mixed.reshape(devices, slots, part).astype(jnp.bfloat16)
    out_ref[:, slots:, :] = grad_normed.reshape(devices, slots, part).astype(jnp.bfloat16)


def weight_grad_kernel(me_ref, hidden_ref, pre_ref, normed_ref, grad_ref, *refs):
    expand_ref, project_ref = refs[-2:]
    contract = (((0,), (0,)), ((), ()))
    expand_ref[...] = lax.dot_general(
        normed_ref[...], pre_ref[0], contract, preferred_element_type=jnp.float32
    ).astype(jnp.bfloat16)
    project_ref[...] = lax.dot_general(
        grad_ref[...], hidden_ref[0], contract, preferred_element_type=jnp.float32
    ).astype(jnp.bfloat16)


def finish_kernel(
    sections, capacity,
    me_ref, count_ref, place_ref, tail_ref, extra_ref, patch_ref, text_ref, gain_ref,
    embedded_ref, grad_rows_ref, sum_ref,
):
    devices, _, part = tail_ref.shape
    slots = patch_ref.shape[0]
    for d in range(devices // sections):
        total = tail_ref[d * sections].astype(jnp.float32)
        for s in range(1, sections):
            total += tail_ref[d * sections + s].astype(jnp.float32)
        sum_ref[:, d * part : (d + 1) * part] = total
    mixed, grad_normed = sum_ref[:slots, :], sum_ref[slots:, :]
    out_rows = (extra_ref[:slots, :] + mixed).astype(jnp.bfloat16)
    length = text_ref.shape[0]
    chooser = landing(place_ref, count_ref, me_ref[1], slots, capacity, length)
    contract = (((0,), (0,)), ((), ()))
    placed = lax.dot_general(
        chooser.astype(jnp.bfloat16), out_rows, contract, preferred_element_type=jnp.float32
    )
    taken = lax.dot_general(
        chooser.astype(jnp.bfloat16), jnp.ones((slots, 128), jnp.bfloat16),
        contract, preferred_element_type=jnp.float32,
    )[:, :1]
    embedded_ref[...] = jnp.where(
        taken > 0.5, placed, text_ref[...].astype(jnp.float32)
    ).astype(jnp.bfloat16)
    inputs = patch_ref[...].astype(jnp.float32)
    inv_rms = lax.rsqrt(jnp.mean(inputs * inputs, axis=-1, keepdims=True) + 1e-06)
    scaled_grad = grad_normed * gain_ref[...]
    centred = jnp.mean(scaled_grad * inputs, axis=-1, keepdims=True)
    grad_rows_ref[...] = (
        extra_ref[slots:, :] + inv_rms * scaled_grad - inputs * (inv_rms**3 * centred)
    ).astype(jnp.bfloat16)


def weight_grads(
    me, hidden, pre, first_index, hidden_steps, pre_steps, normed, grad_all, width, before
):
    count, rows, units = hidden.shape
    features = normed.shape[1]

    def column(steps):
        return lambda i, me_ref: (0, me_ref[0] ^ masked_steps(first_index + i, steps))

    whole = pl.BlockSpec((rows, features), lambda i, me_ref: (0, 0))
    block = pl.BlockSpec((1, rows, units), lambda i, me_ref: (i, 0, 0))
    return pl.pallas_call(
        weight_grad_kernel,
        grid_spec=pltpu.PrefetchScalarGridSpec(
            num_scalar_prefetch=1,
            grid=(count,),
            in_specs=[block, block, whole, whole]
            + [pl.BlockSpec(memory_space=pl.ANY)] * len(before),
            out_specs=[
                pl.BlockSpec((features, units), column(pre_steps)),
                pl.BlockSpec((features, units), column(hidden_steps)),
            ],
        ),
        out_shape=[jax.ShapeDtypeStruct((features, width), jnp.bfloat16)] * 2,
        input_output_aliases={5: 0, 6: 1} if before else {},
        compiler_params=pltpu.CompilerParams(
            dimension_semantics=("arbitrary",), vmem_limit_bytes=24 << 20
        ),
        cost_estimate=pl.CostEstimate(
            flops=4 * count * rows * features * units,
            bytes_accessed=4 * count * units * features + 4 * rows * features,
            transcendentals=0,
        ),
    )(me, hidden, pre, normed, grad_all, *before)


def call(kernel, out_shape, smem, vmem, scratch=()):
    single = not isinstance(out_shape, (list, tuple))
    return pl.pallas_call(
        kernel,
        out_shape=out_shape,
        in_specs=[SMEM_SPEC] * len(smem) + [VMEM_SPEC] * len(vmem),
        out_specs=VMEM_SPEC if single else [VMEM_SPEC] * len(out_shape),
        scratch_shapes=scratch,
        compiler_params=pltpu.CompilerParams(vmem_limit_bytes=24 << 20),
    )(*smem, *vmem)


def move_rows_plan(
    patches, gain, expand_weight, project_weight, counts, positions, text, cotangent
):
    sections = lax.axis_size("section")
    replicas = lax.axis_size("dp")
    devices = sections * replicas
    slots, features = patches.shape
    part, width = expand_weight.shape
    units = width // replicas
    capacity = slots // sections
    rows = devices * slots
    dp_steps, section_steps = bit_steps(replicas), bit_steps(sections)
    me = jnp.stack([lax.axis_index("dp"), lax.axis_index("section")]).astype(jnp.int32)
    gain = gain.reshape(1, features)
    project_turned = project_weight.T
    kept, wide = jnp.bfloat16, jnp.float32
    shape = jax.ShapeDtypeStruct

    stacked = call(
        repack_kernel,
        shape((replicas, 2, part, units), kept),
        (), (expand_weight, project_turned),
    )
    turned = lax.all_to_all(stacked, "dp", split_axis=0, concat_axis=0, tiled=True)

    held = call(
        functools.partial(pick_kernel, capacity),
        shape((1, 2 * slots, features), kept),
        (me, counts, positions), (patches, cotangent),
    )
    exchanges = [("dp", step) for step in dp_steps] + [("section", step) for step in section_steps]
    for axis, step in exchanges:
        got = swap(held, axis, step)
        if held.shape[0] < devices // 2:
            held = jnp.concatenate([held, got], axis=0)
    normed, grad_all, extra = call(
        functools.partial(order_kernel, sections, capacity, dp_steps, section_steps),
        [shape((rows, features), kept), shape((rows, features), kept), shape((2 * slots, features), wide)],
        (me,), (held, got, gain),
    )

    hidden_near, pre_near = call(
        hidden_kernel,
        [shape((1, rows, units), kept)] * 2,
        (), (normed, grad_all, turned),
        [pltpu.VMEM((features, units), kept)] * 2,
    )

    hidden_steps, pre_steps = dp_steps, dp_steps[-1:] + dp_steps[:-1]
    for hidden_step, pre_step in zip(hidden_steps, pre_steps):
        hidden_far = swap(hidden_near, "dp", hidden_step)
        pre_far = swap(pre_near, "dp", pre_step)
        if hidden_near.shape[0] < replicas // 2:
            hidden_near = jnp.concatenate([hidden_near, hidden_far], axis=0)
            pre_near = jnp.concatenate([pre_near, pre_far], axis=0)

    grads = weight_grads(
        me, hidden_near, pre_near, 0,
        hidden_steps, pre_steps, normed, grad_all, width, (),
    )
    tail = call(
        functools.partial(share_kernel, sections, capacity, hidden_steps, pre_steps),
        shape((devices, 2 * slots, part), kept),
        (me,), (hidden_near, hidden_far, pre_near, pre_far, expand_weight, project_turned),
    )
    tail = lax.all_to_all(
        tail, ("dp", "section"), split_axis=0, concat_axis=0, tiled=True
    )
    expand_grad, project_grad = weight_grads(
        me, hidden_far, pre_far, replicas // 2,
        hidden_steps, pre_steps, normed, grad_all, width, grads,
    )
    embedded, grad_rows = call(
        functools.partial(finish_kernel, sections, capacity),
        [shape(text.shape, kept), shape(patches.shape, kept)],
        (me, counts, positions), (tail, extra, patches, text, gain),
        [pltpu.VMEM((2 * slots, features), wide)],
    )
    return (embedded, grad_rows, expand_grad, project_grad.T)


def power_of_two(value):
    return value > 0 and value & (value - 1) == 0


def shards(patches, gain, expand_weight, project_weight, counts, positions, text, cotangent):
    replicas, sections = lax.axis_size("dp"), lax.axis_size("section")
    slots, features = patches.shape
    width = expand_weight.shape[1]
    rows = replicas * sections * slots
    fits = rows * (features + width) <= features * width
    even = (
        all(power_of_two(n) for n in (replicas, sections, slots))
        and replicas > 1
        and sections > 1
        and slots % 8 == 0
        and width % (128 * replicas) == 0
    )
    if fits and even:
        plan = move_rows_plan
    else:
        plan = gather_weights_plan
    return plan(
        patches, gain, expand_weight, project_weight, counts, positions, text, cotangent
    )


def solution(mesh):
    return jax.shard_map(
        shards,
        mesh=mesh,
        in_specs=(
            P(("dp", "section"), None),
            P(),
            P("dp", "section"),
            P("section", "dp"),
            P("dp", None),
            P(("dp", "section"), None),
            P(("dp", "section"), None),
            P(("dp", "section"), None),
        ),
        out_specs=(
            P(("dp", "section"), None),
            P(("dp", "section"), None),
            P(None, "section"),
            P("section", None),
        ),
        check_vma=False,
    )
```

```python
import functools

import jax
import jax.numpy as jnp
from jax import lax
from jax.experimental import pallas as pl
from jax.experimental.pallas import tpu as pltpu
from jax.sharding import PartitionSpec as P


def gelu_pair(values):
    coeff = 0.7978845608
    inner = coeff * (values + 0.044715 * values * values * values)
    tangent = jnp.tanh(inner)
    activated = 0.5 * values * (1.0 + tangent)
    derivative = 0.5 * (1.0 + tangent) + 0.5 * values * (1.0 - tangent * tangent) * coeff * (
        1.0 + 3.0 * 0.044715 * values * values
    )
    return (activated, derivative)


def gather_weights_plan(
    patches, gain, expand_weight, project_weight, counts, positions, text, cotangent
):
    sections = lax.axis_size("section")
    slot_count = patches.shape[0]
    features = patches.shape[1]
    capacity = slot_count // sections
    inputs = patches.astype(jnp.float32)
    inv_rms = lax.rsqrt(jnp.mean(inputs * inputs, axis=-1, keepdims=True) + 1e-06)
    normed = (inputs * inv_rms * gain).astype(jnp.bfloat16)
    gathered = lax.all_gather(normed, "section", axis=0, tiled=True)
    expand_full, project_full = (
        lax.all_gather(expand_weight, "dp", axis=0, tiled=True),
        lax.all_gather(project_weight, "dp", axis=1, tiled=True),
    )
    preact = jnp.dot(gathered, expand_full, preferred_element_type=jnp.float32)
    activated, derivative = gelu_pair(preact)
    hidden = activated.astype(jnp.bfloat16)
    row_block = hidden
    mixed = lax.psum_scatter(
        jnp.dot(row_block, project_full, preferred_element_type=jnp.float32).astype(jnp.bfloat16),
        "section",
        scatter_dimension=0,
        tiled=True,
    ).astype(jnp.float32)
    out_rows = (inputs + mixed).astype(jnp.bfloat16)
    arrived = lax.all_to_all(out_rows, "section", split_axis=0, concat_axis=0, tiled=True)
    section_id = lax.axis_index("section")
    arrival = jnp.arange(slot_count, dtype=jnp.int32)
    source = arrival // capacity
    slot_index = section_id * capacity + arrival % capacity
    is_live = (slot_index < counts[0][source])[:, None]
    targets = positions[0]
    current = text[targets]
    embedded = text.at[targets].set(jnp.where(is_live, arrived, current))
    picked = jnp.where(is_live, cotangent[targets], jnp.zeros_like(current))
    collected = lax.all_gather(picked, "section", axis=0, tiled=True)
    grad_all = (
        collected.reshape(sections, sections, capacity, features)
        .transpose(1, 0, 2, 3)
        .reshape(sections * slot_count, features)
    )
    returned = lax.dynamic_slice_in_dim(grad_all, section_id * slot_count, slot_count, 0)
    grad_own = returned.astype(jnp.float32)
    project_local = lax.dot_general(
        hidden, grad_all, (((0,), (0,)), ((), ())), preferred_element_type=jnp.float32
    )
    grad_hidden = lax.dot_general(
        grad_all, project_full, (((1,), (1,)), ((), ())), preferred_element_type=jnp.float32
    )
    grad_pre = (grad_hidden * derivative).astype(jnp.bfloat16)
    row_block = grad_pre
    grad_normed = lax.psum_scatter(
        lax.dot_general(
            row_block, expand_full, (((1,), (1,)), ((), ())), preferred_element_type=jnp.float32
        ).astype(jnp.bfloat16),
        "section",
        scatter_dimension=0,
        tiled=True,
    ).astype(jnp.float32)
    expand_local = lax.dot_general(
        gathered, grad_pre, (((0,), (0,)), ((), ())), preferred_element_type=jnp.float32
    )
    project_total, expand_total = (
        lax.psum(project_local.astype(jnp.bfloat16), "dp").astype(jnp.float32),
        lax.psum(expand_local.astype(jnp.bfloat16), "dp").astype(jnp.float32),
    )
    scaled_grad = grad_normed * gain
    centred = jnp.mean(scaled_grad * inputs, axis=-1, keepdims=True)
    grad_rows = (grad_own + inv_rms * scaled_grad - inputs * inv_rms**3 * centred).astype(
        jnp.bfloat16
    )
    return (
        embedded,
        grad_rows,
        expand_total.astype(jnp.bfloat16),
        project_total.astype(jnp.bfloat16),
    )


def bit_steps(size):
    steps = []
    step = size // 2
    while step >= 1:
        steps.append(step)
        step //= 2
    return steps


def swap(array, axis, step):
    size = lax.axis_size(axis)
    return lax.ppermute(array, axis, [(i, i ^ step) for i in range(size)])


def masked_steps(index, steps):
    mask = 0
    for place, step in enumerate(steps):
        mask = mask + ((index >> place) & 1) * step
    return mask


VMEM_SPEC = pl.BlockSpec(memory_space=pltpu.VMEM)
SMEM_SPEC = pl.BlockSpec(memory_space=pltpu.SMEM)


def log2(value):
    return value.bit_length() - 1


def landing(place_ref, count_ref, section, slots, capacity, length):
    row = lax.broadcasted_iota(jnp.int32, (slots, length), 0)
    column = lax.broadcasted_iota(jnp.int32, (slots, length), 1)
    spot = jnp.full((slots, length), -1, jnp.int32)
    for q in range(slots):
        live = section * capacity + q % capacity < count_ref[0, q // capacity]
        spot = jnp.where(row == q, jnp.where(live, place_ref[0, q], -1), spot)
    return (spot == column).astype(jnp.float32)


def fetch(copies):
    for copy in copies:
        copy.start()
    for copy in copies:
        copy.wait()


def pick_kernel(
    capacity, counts_at, places_at, patches_at, cotangent_at, pair_ref,
    count_ref, place_ref, patch_ref, cotangent_ref, sems,
):
    ends = (
        (counts_at, count_ref), (places_at, place_ref),
        (patches_at, patch_ref), (cotangent_at, cotangent_ref),
    )
    fetch([pltpu.make_async_copy(a, b, sems.at[i]) for i, (a, b) in enumerate(ends)])
    slots = patch_ref.shape[0]
    section = lax.axis_index("section")
    chooser = landing(
        place_ref, count_ref, section, slots, capacity, cotangent_ref.shape[0]
    ).astype(jnp.bfloat16)
    picked = jnp.dot(chooser, cotangent_ref[...], preferred_element_type=jnp.float32)
    pair_ref[0] = jnp.concatenate(
        [patch_ref[...].astype(jnp.float32), picked], axis=0
    ).astype(jnp.bfloat16)


def repack_kernel(expand_at, project_at, *refs):
    blocks, sems = refs[:-1], refs[-1]
    units = blocks[0].shape[2]
    copies = []
    for i, block in enumerate(blocks):
        start = pl.multiple_of((lax.axis_index("dp") ^ (i + 1)) * units, 128)
        for k, source in enumerate((expand_at, project_at)):
            copies.append(
                pltpu.make_async_copy(
                    source.at[:, pl.ds(start, units)], block.at[k], sems.at[2 * i + k]
                )
            )
    fetch(copies)


def order_kernel(
    sections, capacity, dp_steps, section_steps,
    me_ref, near_ref, far_ref, gain_ref, normed_ref, grad_ref, extra_ref,
):
    rows = normed_ref.shape[0]
    slots = sections * capacity
    half = near_ref.shape[0] * near_ref.shape[1]
    me_dp, me_section = me_ref[0], me_ref[1]
    column = lax.broadcasted_iota(jnp.int32, (8, half), 1)
    row = lax.broadcasted_iota(jnp.int32, (rows, half), 0)
    kind = column & (2 * slots - 1)
    slot = kind & (slots - 1)
    inputs = grad = None
    for side, ref in enumerate((near_ref, far_ref)):
        block = (column >> log2(2 * slots)) + side * (half // (2 * slots))
        source_dp = me_dp ^ masked_steps(block, dp_steps)
        source_section = me_section ^ masked_steps(block >> len(dp_steps), section_steps)
        patch_at = (source_dp * sections + source_section) * slots + slot
        grad_at = (
            (source_dp * sections + (slot >> log2(capacity))) * slots
            + source_section * capacity
            + (slot & (capacity - 1))
        )
        patch_at = jnp.where(kind < slots, patch_at, -1)[:1]
        grad_at = jnp.where(kind >= slots, grad_at, -1)[:1]
        values = ref[...].reshape(half, ref.shape[2])
        chosen = (row == patch_at).astype(jnp.float32).astype(jnp.bfloat16)
        found = jnp.dot(chosen, values, preferred_element_type=jnp.float32)
        inputs = found if inputs is None else inputs + found
        chosen = (row == grad_at).astype(jnp.float32).astype(jnp.bfloat16)
        found = jnp.dot(chosen, values, preferred_element_type=jnp.float32)
        grad = found if grad is None else grad + found
    inv_rms = lax.rsqrt(jnp.mean(inputs * inputs, axis=-1, keepdims=True) + 1e-06)
    normed_ref[...] = (inputs * inv_rms * gain_ref[...]).astype(jnp.bfloat16)
    grad = grad.astype(jnp.bfloat16)
    grad_ref[...] = grad
    mine = lax.broadcasted_iota(jnp.int32, (slots, rows), 0)
    every = lax.broadcasted_iota(jnp.int32, (slots, rows), 1)
    coming_at = (
        (me_dp * sections + (mine >> log2(capacity))) * slots
        + me_section * capacity
        + (mine & (capacity - 1))
    )
    own_at = (me_dp * sections + me_section) * slots + mine
    coming = jnp.dot(
        (every == coming_at).astype(jnp.float32).astype(jnp.bfloat16),
        inputs.astype(jnp.bfloat16),
        preferred_element_type=jnp.float32,
    )
    own = jnp.dot(
        (every == own_at).astype(jnp.float32).astype(jnp.bfloat16),
        grad,
        preferred_element_type=jnp.float32,
    )
    extra_ref[...] = jnp.concatenate([coming, own], axis=0)


def hidden_kernel(normed_ref, grad_ref, expand_at, project_at, *refs):
    blocks = refs[:-5]
    hidden_ref, pre_ref, expand_ref, project_ref, sems = refs[-5:]
    part = expand_at.shape[0]
    units = hidden_ref.shape[2]
    me = lax.axis_index("dp")
    copies = []
    for k, (source, whole) in enumerate(((expand_at, expand_ref), (project_at, project_ref))):
        own = source.at[:, pl.ds(pl.multiple_of(me * units, 128), units)]
        for i, block in enumerate((own, *(block.at[k] for block in blocks))):
            at = pl.ds(pl.multiple_of((me ^ i) * part, 8), part)
            copies.append(
                pltpu.make_async_copy(
                    block, whole.at[at, :], sems.at[k * (len(blocks) + 1) + i]
                )
            )
    fetch(copies)
    preact = jnp.dot(normed_ref[...], expand_ref[...], preferred_element_type=jnp.float32)
    activated, derivative = gelu_pair(preact)
    hidden_ref[0] = activated.astype(jnp.bfloat16)
    grad_hidden = jnp.dot(grad_ref[...], project_ref[...], preferred_element_type=jnp.float32)
    pre_ref[0] = (grad_hidden * derivative).astype(jnp.bfloat16)


def share_kernel(
    sections, capacity, steps,
    me_ref, hidden_ref, pre_ref, expand_ref, project_ref, keep_ref, send_ref,
):
    rows = hidden_ref.shape[1]
    slots = sections * capacity
    row = lax.broadcasted_iota(jnp.int32, (rows, rows), 0)
    column = lax.broadcasted_iota(jnp.int32, (rows, rows), 1)
    inside = row & (slots - 1)
    replica = (row >> log2(slots)) & (rows // (sections * slots) - 1)
    away = row >> log2(rows // sections)
    goal = me_ref[1] ^ masked_steps(away, steps[::-1])
    base = replica * (slots * sections)
    mixed_from = (
        base + (inside >> log2(capacity)) * slots + goal * capacity + (inside & (capacity - 1))
    )
    normed_from = base + goal * slots + inside
    for k, (ref, source, weight_ref) in enumerate(
        ((hidden_ref, mixed_from, project_ref), (pre_ref, normed_from, expand_ref))
    ):
        turn = (column == source).astype(jnp.float32).astype(jnp.bfloat16)
        turned = jnp.dot(turn, ref[0], preferred_element_type=jnp.float32).astype(jnp.bfloat16)
        share = lax.dot_general(
            turned, weight_ref[...], (((1,), (1,)), ((), ())), preferred_element_type=jnp.float32
        )
        share = share.reshape(2, *keep_ref.shape[1:])
        keep_ref[k] = share[0]
        send_ref[k] = share[1].astype(jnp.bfloat16)


def halve_kernel(keep_ref, got_ref, next_keep_ref, next_send_ref):
    half = next_keep_ref.shape[1]
    total = keep_ref[...] + got_ref[...].astype(jnp.float32)
    next_keep_ref[...] = total[:, :half]
    next_send_ref[...] = total[:, half:].astype(jnp.bfloat16)


def address_kernel(keep_ref, got_ref, out_ref):
    total = keep_ref[...] + got_ref[...].astype(jnp.float32)
    for d in range(out_ref.shape[0]):
        out_ref[d] = jnp.concatenate([total[0, d], total[1, d]], axis=0).astype(jnp.bfloat16)


def weight_grad_kernel(me_ref, hidden_ref, pre_ref, normed_ref, grad_ref, *refs):
    expand_ref, project_ref = refs[-2:]
    contract = (((0,), (0,)), ((), ()))
    expand_ref[...] = lax.dot_general(
        normed_ref[...], pre_ref[0], contract, preferred_element_type=jnp.float32
    ).astype(jnp.bfloat16)
    project_ref[...] = lax.dot_general(
        grad_ref[...], hidden_ref[0], contract, preferred_element_type=jnp.float32
    ).astype(jnp.bfloat16)


def finish_kernel(
    capacity,
    me_ref, count_ref, place_ref, tail_ref, extra_ref, patch_ref, text_ref, gain_ref,
    embedded_ref, grad_rows_ref,
):
    slots = patch_ref.shape[0]
    total = tail_ref[0].astype(jnp.float32)
    for d in range(1, tail_ref.shape[0]):
        total += tail_ref[d].astype(jnp.float32)
    mixed, grad_normed = total[:slots], total[slots:]
    out_rows = (extra_ref[:slots, :] + mixed).astype(jnp.bfloat16)
    length = text_ref.shape[0]
    chooser = landing(place_ref, count_ref, me_ref[1], slots, capacity, length)
    contract = (((0,), (0,)), ((), ()))
    placed = lax.dot_general(
        chooser.astype(jnp.bfloat16), out_rows, contract, preferred_element_type=jnp.float32
    )
    taken = lax.dot_general(
        chooser.astype(jnp.bfloat16), jnp.ones((slots, 128), jnp.bfloat16),
        contract, preferred_element_type=jnp.float32,
    )[:, :1]
    embedded_ref[...] = jnp.where(
        taken > 0.5, placed, text_ref[...].astype(jnp.float32)
    ).astype(jnp.bfloat16)
    inputs = patch_ref[...].astype(jnp.float32)
    inv_rms = lax.rsqrt(jnp.mean(inputs * inputs, axis=-1, keepdims=True) + 1e-06)
    scaled_grad = grad_normed * gain_ref[...]
    centred = jnp.mean(scaled_grad * inputs, axis=-1, keepdims=True)
    grad_rows_ref[...] = (
        extra_ref[slots:, :] + inv_rms * scaled_grad - inputs * (inv_rms**3 * centred)
    ).astype(jnp.bfloat16)


def weight_grads(
    me, hidden, pre, first_index, hidden_steps, pre_steps, normed, grad_all, width, before
):
    count, rows, units = hidden.shape
    features = normed.shape[1]

    def column(steps):
        return lambda i, me_ref: (0, me_ref[0] ^ masked_steps(first_index + i, steps))

    whole = pl.BlockSpec((rows, features), lambda i, me_ref: (0, 0))
    block = pl.BlockSpec((1, rows, units), lambda i, me_ref: (i, 0, 0))
    return pl.pallas_call(
        weight_grad_kernel,
        grid_spec=pltpu.PrefetchScalarGridSpec(
            num_scalar_prefetch=1,
            grid=(count,),
            in_specs=[block, block, whole, whole]
            + [pl.BlockSpec(memory_space=pl.ANY)] * len(before),
            out_specs=[
                pl.BlockSpec((features, units), column(pre_steps)),
                pl.BlockSpec((features, units), column(hidden_steps)),
            ],
        ),
        out_shape=[jax.ShapeDtypeStruct((features, width), jnp.bfloat16)] * 2,
        input_output_aliases={5: 0, 6: 1} if before else {},
        compiler_params=pltpu.CompilerParams(
            dimension_semantics=("arbitrary",), vmem_limit_bytes=12 << 20
        ),
        cost_estimate=pl.CostEstimate(
            flops=4 * count * rows * features * units,
            bytes_accessed=4 * count * units * features + 4 * rows * features,
            transcendentals=0,
        ),
    )(me, hidden, pre, normed, grad_all, *before)


def call(kernel, out_shape, smem, vmem, scratch=()):
    single = not isinstance(out_shape, (list, tuple))
    return pl.pallas_call(
        kernel,
        out_shape=out_shape,
        in_specs=[SMEM_SPEC] * len(smem) + [VMEM_SPEC] * len(vmem),
        out_specs=VMEM_SPEC if single else [VMEM_SPEC] * len(out_shape),
        scratch_shapes=scratch,
        compiler_params=pltpu.CompilerParams(vmem_limit_bytes=12 << 20),
    )(*smem, *vmem)


def move_rows_plan(
    patches, gain, expand_weight, project_weight, counts, positions, text, cotangent
):
    sections = lax.axis_size("section")
    replicas = lax.axis_size("dp")
    devices = sections * replicas
    slots, features = patches.shape
    part, width = expand_weight.shape
    units = width // replicas
    capacity = slots // sections
    rows = devices * slots
    dp_steps, section_steps = bit_steps(replicas), bit_steps(sections)
    me = jnp.stack([lax.axis_index("dp"), lax.axis_index("section")]).astype(jnp.int32)
    gain = gain.reshape(1, features)
    project_turned = project_weight.T
    kept, wide = jnp.bfloat16, jnp.float32
    shape = jax.ShapeDtypeStruct

    hbm = pl.BlockSpec(memory_space=pltpu.HBM)

    def in_hbm(*arrays):
        return [pltpu.with_memory_space_constraint(array, pltpu.HBM) for array in arrays]

    held = pl.pallas_call(
        functools.partial(pick_kernel, capacity),
        out_shape=shape((1, 2 * slots, features), kept),
        in_specs=[hbm] * 4,
        out_specs=VMEM_SPEC,
        scratch_shapes=[
            pltpu.SMEM(counts.shape, counts.dtype),
            pltpu.SMEM(positions.shape, positions.dtype),
            pltpu.VMEM(patches.shape, kept),
            pltpu.VMEM(cotangent.shape, kept),
            pltpu.SemaphoreType.DMA((4,)),
        ],
        compiler_params=pltpu.CompilerParams(vmem_limit_bytes=12 << 20),
    )(*in_hbm(counts, positions, patches, cotangent))
    blocks = pl.pallas_call(
        repack_kernel,
        out_shape=[shape((2, part, units), kept)] * (replicas - 1),
        in_specs=[hbm] * 2,
        out_specs=[VMEM_SPEC] * (replicas - 1),
        scratch_shapes=[pltpu.SemaphoreType.DMA((2 * replicas - 2,))],
        compiler_params=pltpu.CompilerParams(vmem_limit_bytes=12 << 20),
    )(*in_hbm(expand_weight, project_turned))
    arrived = []
    for distance in range(1, replicas):
        arrived.append(swap(blocks[distance - 1], "dp", distance))

    exchanges = [("dp", step) for step in dp_steps] + [("section", step) for step in section_steps]
    for axis, step in exchanges:
        got = swap(held, axis, step)
        if held.shape[0] < devices // 2:
            held = jnp.concatenate([held, got], axis=0)
    normed, grad_all, extra = call(
        functools.partial(order_kernel, sections, capacity, dp_steps, section_steps),
        [shape((rows, features), kept), shape((rows, features), kept), shape((2 * slots, features), wide)],
        (me,), (held, got, gain),
    )

    hidden_near, pre_near, expand_slice, project_slice = pl.pallas_call(
        hidden_kernel,
        out_shape=[shape((1, rows, units), kept)] * 2 + [shape((features, units), kept)] * 2,
        in_specs=[VMEM_SPEC] * 2 + [hbm] * 2 + [pl.BlockSpec(memory_space=pl.ANY)] * len(arrived),
        out_specs=[VMEM_SPEC] * 4,
        scratch_shapes=[pltpu.SemaphoreType.DMA((2 * replicas,))],
        compiler_params=pltpu.CompilerParams(vmem_limit_bytes=12 << 20),
    )(normed, grad_all, *in_hbm(expand_weight, project_turned), *arrived)

    tail_steps = section_steps[::-1]
    keep, send = call(
        functools.partial(share_kernel, sections, capacity, tail_steps),
        [shape((2, devices // 2, slots, features), kind) for kind in (wide, kept)],
        (me,), (hidden_near, pre_near, expand_slice, project_slice),
    )
    for place, step in enumerate(tail_steps):
        got = swap(send, "section", step)
        if place < len(tail_steps) - 1:
            half = (2, send.shape[1] // 2, slots, features)
            keep, send = call(
                halve_kernel, [shape(half, wide), shape(half, kept)], (), (keep, got)
            )
    tail = call(address_kernel, shape((replicas, 2 * slots, features), kept), (), (keep, got))
    tail = lax.all_to_all(tail, "dp", split_axis=0, concat_axis=0, tiled=True)

    hidden_steps, pre_steps = dp_steps, dp_steps[-1:] + dp_steps[:-1]
    for hidden_step, pre_step in zip(hidden_steps, pre_steps):
        hidden_far = swap(hidden_near, "dp", hidden_step)
        pre_far = swap(pre_near, "dp", pre_step)
        if hidden_near.shape[0] < replicas // 2:
            hidden_near = jnp.concatenate([hidden_near, hidden_far], axis=0)
            pre_near = jnp.concatenate([pre_near, pre_far], axis=0)

    grads = weight_grads(
        me, hidden_near, pre_near, 0,
        hidden_steps, pre_steps, normed, grad_all, width, (),
    )
    expand_grad, project_grad = weight_grads(
        me, hidden_far, pre_far, replicas // 2,
        hidden_steps, pre_steps, normed, grad_all, width, grads,
    )
    embedded, grad_rows = call(
        functools.partial(finish_kernel, capacity),
        [shape(text.shape, kept), shape(patches.shape, kept)],
        (me, counts, positions), (tail, extra, patches, text, gain),
    )
    return (embedded, grad_rows, expand_grad, project_grad.T)


def power_of_two(value):
    return value > 0 and value & (value - 1) == 0


def shards(patches, gain, expand_weight, project_weight, counts, positions, text, cotangent):
    replicas, sections = lax.axis_size("dp"), lax.axis_size("section")
    slots, features = patches.shape
    width = expand_weight.shape[1]
    rows = replicas * sections * slots
    fits = rows * (features + width) <= features * width
    even = (
        all(power_of_two(n) for n in (replicas, sections, slots))
        and replicas > 1
        and sections > 1
        and slots % 8 == 0
        and width % (128 * replicas) == 0
    )
    if fits and even:
        plan = move_rows_plan
    else:
        plan = gather_weights_plan
    return plan(
        patches, gain, expand_weight, project_weight, counts, positions, text, cotangent
    )


def solution(mesh):
    return jax.shard_map(
        shards,
        mesh=mesh,
        in_specs=(
            P(("dp", "section"), None),
            P(),
            P("dp", "section"),
            P("section", "dp"),
            P("dp", None),
            P(("dp", "section"), None),
            P(("dp", "section"), None),
            P(("dp", "section"), None),
        ),
        out_specs=(
            P(("dp", "section"), None),
            P(("dp", "section"), None),
            P(None, "section"),
            P("section", None),
        ),
        check_vma=False,
    )
```

```python
import functools

import jax
import jax.numpy as jnp
from jax import lax
from jax.experimental import pallas as pl
from jax.experimental.pallas import tpu as pltpu
from jax.sharding import PartitionSpec as P


def gelu_pair(values):
    coeff = 0.7978845608
    inner = coeff * (values + 0.044715 * values * values * values)
    tangent = jnp.tanh(inner)
    activated = 0.5 * values * (1.0 + tangent)
    derivative = 0.5 * (1.0 + tangent) + 0.5 * values * (1.0 - tangent * tangent) * coeff * (
        1.0 + 3.0 * 0.044715 * values * values
    )
    return (activated, derivative)


def gather_weights_plan(
    patches, gain, expand_weight, project_weight, counts, positions, text, cotangent
):
    sections = lax.axis_size("section")
    slot_count = patches.shape[0]
    features = patches.shape[1]
    capacity = slot_count // sections
    inputs = patches.astype(jnp.float32)
    inv_rms = lax.rsqrt(jnp.mean(inputs * inputs, axis=-1, keepdims=True) + 1e-06)
    normed = (inputs * inv_rms * gain).astype(jnp.bfloat16)
    gathered = lax.all_gather(normed, "section", axis=0, tiled=True)
    expand_full, project_full = (
        lax.all_gather(expand_weight, "dp", axis=0, tiled=True),
        lax.all_gather(project_weight, "dp", axis=1, tiled=True),
    )
    preact = jnp.dot(gathered, expand_full, preferred_element_type=jnp.float32)
    activated, derivative = gelu_pair(preact)
    hidden = activated.astype(jnp.bfloat16)
    row_block = hidden
    mixed = lax.psum_scatter(
        jnp.dot(row_block, project_full, preferred_element_type=jnp.float32).astype(jnp.bfloat16),
        "section",
        scatter_dimension=0,
        tiled=True,
    ).astype(jnp.float32)
    out_rows = (inputs + mixed).astype(jnp.bfloat16)
    arrived = lax.all_to_all(out_rows, "section", split_axis=0, concat_axis=0, tiled=True)
    section_id = lax.axis_index("section")
    arrival = jnp.arange(slot_count, dtype=jnp.int32)
    source = arrival // capacity
    slot_index = section_id * capacity + arrival % capacity
    is_live = (slot_index < counts[0][source])[:, None]
    targets = positions[0]
    current = text[targets]
    embedded = text.at[targets].set(jnp.where(is_live, arrived, current))
    picked = jnp.where(is_live, cotangent[targets], jnp.zeros_like(current))
    collected = lax.all_gather(picked, "section", axis=0, tiled=True)
    grad_all = (
        collected.reshape(sections, sections, capacity, features)
        .transpose(1, 0, 2, 3)
        .reshape(sections * slot_count, features)
    )
    returned = lax.dynamic_slice_in_dim(grad_all, section_id * slot_count, slot_count, 0)
    grad_own = returned.astype(jnp.float32)
    project_local = lax.dot_general(
        hidden, grad_all, (((0,), (0,)), ((), ())), preferred_element_type=jnp.float32
    )
    grad_hidden = lax.dot_general(
        grad_all, project_full, (((1,), (1,)), ((), ())), preferred_element_type=jnp.float32
    )
    grad_pre = (grad_hidden * derivative).astype(jnp.bfloat16)
    row_block = grad_pre
    grad_normed = lax.psum_scatter(
        lax.dot_general(
            row_block, expand_full, (((1,), (1,)), ((), ())), preferred_element_type=jnp.float32
        ).astype(jnp.bfloat16),
        "section",
        scatter_dimension=0,
        tiled=True,
    ).astype(jnp.float32)
    expand_local = lax.dot_general(
        gathered, grad_pre, (((0,), (0,)), ((), ())), preferred_element_type=jnp.float32
    )
    project_total, expand_total = (
        lax.psum(project_local.astype(jnp.bfloat16), "dp").astype(jnp.float32),
        lax.psum(expand_local.astype(jnp.bfloat16), "dp").astype(jnp.float32),
    )
    scaled_grad = grad_normed * gain
    centred = jnp.mean(scaled_grad * inputs, axis=-1, keepdims=True)
    grad_rows = (grad_own + inv_rms * scaled_grad - inputs * inv_rms**3 * centred).astype(
        jnp.bfloat16
    )
    return (
        embedded,
        grad_rows,
        expand_total.astype(jnp.bfloat16),
        project_total.astype(jnp.bfloat16),
    )


def bit_steps(size):
    steps = []
    step = size // 2
    while step >= 1:
        steps.append(step)
        step //= 2
    return steps


def swap(array, axis, step):
    size = lax.axis_size(axis)
    return lax.ppermute(array, axis, [(i, i ^ step) for i in range(size)])


def masked_steps(index, steps):
    mask = 0
    for place, step in enumerate(steps):
        mask = mask + ((index >> place) & 1) * step
    return mask


VMEM_SPEC = pl.BlockSpec(memory_space=pltpu.VMEM)
SMEM_SPEC = pl.BlockSpec(memory_space=pltpu.SMEM)


def log2(value):
    return value.bit_length() - 1


def landing(place_ref, count_ref, section, slots, capacity, length):
    row = lax.broadcasted_iota(jnp.int32, (slots, length), 0)
    column = lax.broadcasted_iota(jnp.int32, (slots, length), 1)
    spot = jnp.full((slots, length), -1, jnp.int32)
    for q in range(slots):
        live = section * capacity + q % capacity < count_ref[0, q // capacity]
        spot = jnp.where(row == q, jnp.where(live, place_ref[0, q], -1), spot)
    return (spot == column).astype(jnp.float32)


def fetch(copies):
    for copy in copies:
        copy.start()
    for copy in copies:
        copy.wait()


def pick_kernel(
    capacity, counts_at, places_at, patches_at, cotangent_at, pair_ref,
    count_ref, place_ref, patch_ref, cotangent_ref, sems,
):
    ends = (
        (counts_at, count_ref), (places_at, place_ref),
        (patches_at, patch_ref), (cotangent_at, cotangent_ref),
    )
    fetch([pltpu.make_async_copy(a, b, sems.at[i]) for i, (a, b) in enumerate(ends)])
    slots = patch_ref.shape[0]
    section = lax.axis_index("section")
    chooser = landing(
        place_ref, count_ref, section, slots, capacity, cotangent_ref.shape[0]
    ).astype(jnp.bfloat16)
    picked = jnp.dot(chooser, cotangent_ref[...], preferred_element_type=jnp.float32)
    pair_ref[0] = jnp.concatenate(
        [patch_ref[...].astype(jnp.float32), picked], axis=0
    ).astype(jnp.bfloat16)


def repack_kernel(expand_at, project_at, *refs):
    blocks, sems = refs[:-1], refs[-1]
    units = blocks[0].shape[2]
    copies = []
    for i, block in enumerate(blocks):
        start = pl.multiple_of((lax.axis_index("dp") ^ (i + 1)) * units, 128)
        for k, source in enumerate((expand_at, project_at)):
            copies.append(
                pltpu.make_async_copy(
                    source.at[:, pl.ds(start, units)], block.at[k], sems.at[2 * i + k]
                )
            )
    fetch(copies)


def join_kernel(first_ref, second_ref, out_ref):
    count = first_ref.shape[0]
    out_ref[:count] = first_ref[...]
    out_ref[count:] = second_ref[...]


def order_kernel(
    sections, capacity, dp_steps, section_steps,
    me_ref, near_ref, far_ref, gain_ref, normed_ref, grad_ref, extra_ref,
):
    rows = normed_ref.shape[0]
    slots = sections * capacity
    half = near_ref.shape[0] * near_ref.shape[1]
    me_dp, me_section = me_ref[0], me_ref[1]
    column = lax.broadcasted_iota(jnp.int32, (8, half), 1)
    row = lax.broadcasted_iota(jnp.int32, (rows, half), 0)
    kind = column & (2 * slots - 1)
    slot = kind & (slots - 1)
    inputs = grad = None
    for side, ref in enumerate((near_ref, far_ref)):
        block = (column >> log2(2 * slots)) + side * (half // (2 * slots))
        source_dp = me_dp ^ masked_steps(block, dp_steps)
        source_section = me_section ^ masked_steps(block >> len(dp_steps), section_steps)
        patch_at = (source_dp * sections + source_section) * slots + slot
        grad_at = (
            (source_dp * sections + (slot >> log2(capacity))) * slots
            + source_section * capacity
            + (slot & (capacity - 1))
        )
        patch_at = jnp.where(kind < slots, patch_at, -1)[:1]
        grad_at = jnp.where(kind >= slots, grad_at, -1)[:1]
        values = ref[...].reshape(half, ref.shape[2])
        chosen = (row == patch_at).astype(jnp.float32).astype(jnp.bfloat16)
        found = jnp.dot(chosen, values, preferred_element_type=jnp.float32)
        inputs = found if inputs is None else inputs + found
        chosen = (row == grad_at).astype(jnp.float32).astype(jnp.bfloat16)
        found = jnp.dot(chosen, values, preferred_element_type=jnp.float32)
        grad = found if grad is None else grad + found
    inv_rms = lax.rsqrt(jnp.mean(inputs * inputs, axis=-1, keepdims=True) + 1e-06)
    normed_ref[...] = (inputs * inv_rms * gain_ref[...]).astype(jnp.bfloat16)
    grad = grad.astype(jnp.bfloat16)
    grad_ref[...] = grad
    mine = lax.broadcasted_iota(jnp.int32, (slots, rows), 0)
    every = lax.broadcasted_iota(jnp.int32, (slots, rows), 1)
    coming_at = (
        (me_dp * sections + (mine >> log2(capacity))) * slots
        + me_section * capacity
        + (mine & (capacity - 1))
    )
    own_at = (me_dp * sections + me_section) * slots + mine
    coming = jnp.dot(
        (every == coming_at).astype(jnp.float32).astype(jnp.bfloat16),
        inputs.astype(jnp.bfloat16),
        preferred_element_type=jnp.float32,
    )
    own = jnp.dot(
        (every == own_at).astype(jnp.float32).astype(jnp.bfloat16),
        grad,
        preferred_element_type=jnp.float32,
    )
    extra_ref[...] = jnp.concatenate([coming, own], axis=0)


def hidden_kernel(normed_ref, grad_ref, expand_at, project_at, *refs):
    blocks = refs[:-5]
    hidden_ref, pre_ref, expand_ref, project_ref, sems = refs[-5:]
    part = expand_at.shape[0]
    units = hidden_ref.shape[2]
    me = lax.axis_index("dp")
    copies = []
    for k, (source, whole) in enumerate(((expand_at, expand_ref), (project_at, project_ref))):
        own = source.at[:, pl.ds(pl.multiple_of(me * units, 128), units)]
        for i, block in enumerate((own, *(block.at[k] for block in blocks))):
            at = pl.ds(pl.multiple_of((me ^ i) * part, 8), part)
            copies.append(
                pltpu.make_async_copy(
                    block, whole.at[at, :], sems.at[k * (len(blocks) + 1) + i]
                )
            )
    fetch(copies)
    preact = jnp.dot(normed_ref[...], expand_ref[...], preferred_element_type=jnp.float32)
    activated, derivative = gelu_pair(preact)
    hidden_ref[0] = activated.astype(jnp.bfloat16)
    grad_hidden = jnp.dot(grad_ref[...], project_ref[...], preferred_element_type=jnp.float32)
    pre_ref[0] = (grad_hidden * derivative).astype(jnp.bfloat16)


def share_kernel(
    sections, capacity, steps,
    me_ref, hidden_ref, pre_ref, expand_ref, project_ref, keep_ref, send_ref,
):
    rows = hidden_ref.shape[1]
    slots = sections * capacity
    row = lax.broadcasted_iota(jnp.int32, (rows, rows), 0)
    column = lax.broadcasted_iota(jnp.int32, (rows, rows), 1)
    inside = row & (slots - 1)
    replica = (row >> log2(slots)) & (rows // (sections * slots) - 1)
    away = row >> log2(rows // sections)
    goal = me_ref[1] ^ masked_steps(away, steps[::-1])
    base = replica * (slots * sections)
    mixed_from = (
        base + (inside >> log2(capacity)) * slots + goal * capacity + (inside & (capacity - 1))
    )
    normed_from = base + goal * slots + inside
    for k, (ref, source, weight_ref) in enumerate(
        ((hidden_ref, mixed_from, project_ref), (pre_ref, normed_from, expand_ref))
    ):
        turn = (column == source).astype(jnp.float32).astype(jnp.bfloat16)
        turned = jnp.dot(turn, ref[0], preferred_element_type=jnp.float32).astype(jnp.bfloat16)
        share = lax.dot_general(
            turned, weight_ref[...], (((1,), (1,)), ((), ())), preferred_element_type=jnp.float32
        )
        share = share.reshape(2, *keep_ref.shape[1:])
        keep_ref[k] = share[0]
        send_ref[k] = share[1].astype(jnp.bfloat16)


def halve_kernel(keep_ref, got_ref, next_keep_ref, next_send_ref):
    half = next_keep_ref.shape[1]
    total = keep_ref[...] + got_ref[...].astype(jnp.float32)
    next_keep_ref[...] = total[:, :half]
    next_send_ref[...] = total[:, half:].astype(jnp.bfloat16)


def address_kernel(keep_ref, got_ref, out_ref):
    total = keep_ref[...] + got_ref[...].astype(jnp.float32)
    for d in range(out_ref.shape[0]):
        out_ref[d] = jnp.concatenate([total[0, d], total[1, d]], axis=0).astype(jnp.bfloat16)


def weight_grad_kernel(me_ref, hidden_ref, pre_ref, normed_ref, grad_ref, *refs):
    expand_ref, project_ref = refs[-2:]
    contract = (((0,), (0,)), ((), ()))
    expand_ref[...] = lax.dot_general(
        normed_ref[...], pre_ref[0], contract, preferred_element_type=jnp.float32
    ).astype(jnp.bfloat16)
    project_ref[...] = lax.dot_general(
        grad_ref[...], hidden_ref[0], contract, preferred_element_type=jnp.float32
    ).astype(jnp.bfloat16)


def finish_kernel(
    capacity,
    me_ref, count_ref, place_ref, tail_ref, extra_ref, patch_ref, text_ref, gain_ref,
    embedded_ref, grad_rows_ref,
):
    slots = patch_ref.shape[0]
    total = tail_ref[0].astype(jnp.float32)
    for d in range(1, tail_ref.shape[0]):
        total += tail_ref[d].astype(jnp.float32)
    mixed, grad_normed = total[:slots], total[slots:]
    out_rows = (extra_ref[:slots, :] + mixed).astype(jnp.bfloat16)
    length = text_ref.shape[0]
    chooser = landing(place_ref, count_ref, me_ref[1], slots, capacity, length)
    contract = (((0,), (0,)), ((), ()))
    placed = lax.dot_general(
        chooser.astype(jnp.bfloat16), out_rows, contract, preferred_element_type=jnp.float32
    )
    taken = lax.dot_general(
        chooser.astype(jnp.bfloat16), jnp.ones((slots, 128), jnp.bfloat16),
        contract, preferred_element_type=jnp.float32,
    )[:, :1]
    embedded_ref[...] = jnp.where(
        taken > 0.5, placed, text_ref[...].astype(jnp.float32)
    ).astype(jnp.bfloat16)
    inputs = patch_ref[...].astype(jnp.float32)
    inv_rms = lax.rsqrt(jnp.mean(inputs * inputs, axis=-1, keepdims=True) + 1e-06)
    scaled_grad = grad_normed * gain_ref[...]
    centred = jnp.mean(scaled_grad * inputs, axis=-1, keepdims=True)
    grad_rows_ref[...] = (
        extra_ref[slots:, :] + inv_rms * scaled_grad - inputs * (inv_rms**3 * centred)
    ).astype(jnp.bfloat16)


def weight_grads(
    me, hidden, pre, first_index, hidden_steps, pre_steps, normed, grad_all, width, before
):
    count, rows, units = hidden.shape
    features = normed.shape[1]

    def column(steps):
        return lambda i, me_ref: (0, me_ref[0] ^ masked_steps(first_index + i, steps))

    whole = pl.BlockSpec((rows, features), lambda i, me_ref: (0, 0))
    block = pl.BlockSpec((1, rows, units), lambda i, me_ref: (i, 0, 0))
    return pl.pallas_call(
        weight_grad_kernel,
        grid_spec=pltpu.PrefetchScalarGridSpec(
            num_scalar_prefetch=1,
            grid=(count,),
            in_specs=[block, block, whole, whole]
            + [pl.BlockSpec(memory_space=pl.ANY)] * len(before),
            out_specs=[
                pl.BlockSpec((features, units), column(pre_steps)),
                pl.BlockSpec((features, units), column(hidden_steps)),
            ],
        ),
        out_shape=[jax.ShapeDtypeStruct((features, width), jnp.bfloat16)] * 2,
        input_output_aliases={5: 0, 6: 1} if before else {},
        compiler_params=pltpu.CompilerParams(
            dimension_semantics=("arbitrary",), vmem_limit_bytes=12 << 20
        ),
        cost_estimate=pl.CostEstimate(
            flops=4 * count * rows * features * units,
            bytes_accessed=4 * count * units * features + 4 * rows * features,
            transcendentals=0,
        ),
    )(me, hidden, pre, normed, grad_all, *before)


def call(kernel, out_shape, smem, vmem, scratch=()):
    single = not isinstance(out_shape, (list, tuple))
    return pl.pallas_call(
        kernel,
        out_shape=out_shape,
        in_specs=[SMEM_SPEC] * len(smem) + [VMEM_SPEC] * len(vmem),
        out_specs=VMEM_SPEC if single else [VMEM_SPEC] * len(out_shape),
        scratch_shapes=scratch,
        compiler_params=pltpu.CompilerParams(vmem_limit_bytes=12 << 20),
    )(*smem, *vmem)


def join(first, second):
    both = (first.shape[0] + second.shape[0], *first.shape[1:])
    return call(join_kernel, jax.ShapeDtypeStruct(both, first.dtype), (), (first, second))


def move_rows_plan(
    patches, gain, expand_weight, project_weight, counts, positions, text, cotangent
):
    sections = lax.axis_size("section")
    replicas = lax.axis_size("dp")
    devices = sections * replicas
    slots, features = patches.shape
    part, width = expand_weight.shape
    units = width // replicas
    capacity = slots // sections
    rows = devices * slots
    dp_steps, section_steps = bit_steps(replicas), bit_steps(sections)
    me = jnp.stack([lax.axis_index("dp"), lax.axis_index("section")]).astype(jnp.int32)
    gain = gain.reshape(1, features)
    project_turned = project_weight.T
    kept, wide = jnp.bfloat16, jnp.float32
    shape = jax.ShapeDtypeStruct

    hbm = pl.BlockSpec(memory_space=pltpu.HBM)

    def in_hbm(*arrays):
        return [pltpu.with_memory_space_constraint(array, pltpu.HBM) for array in arrays]

    held = pl.pallas_call(
        functools.partial(pick_kernel, capacity),
        out_shape=shape((1, 2 * slots, features), kept),
        in_specs=[hbm] * 4,
        out_specs=VMEM_SPEC,
        scratch_shapes=[
            pltpu.SMEM(counts.shape, counts.dtype),
            pltpu.SMEM(positions.shape, positions.dtype),
            pltpu.VMEM(patches.shape, kept),
            pltpu.VMEM(cotangent.shape, kept),
            pltpu.SemaphoreType.DMA((4,)),
        ],
        compiler_params=pltpu.CompilerParams(vmem_limit_bytes=12 << 20),
    )(*in_hbm(counts, positions, patches, cotangent))
    blocks = pl.pallas_call(
        repack_kernel,
        out_shape=[shape((2, part, units), kept)] * (replicas - 1),
        in_specs=[hbm] * 2,
        out_specs=[VMEM_SPEC] * (replicas - 1),
        scratch_shapes=[pltpu.SemaphoreType.DMA((2 * replicas - 2,))],
        compiler_params=pltpu.CompilerParams(vmem_limit_bytes=12 << 20),
    )(*in_hbm(expand_weight, project_turned))
    arrived = []
    for distance in range(1, replicas):
        arrived.append(swap(blocks[distance - 1], "dp", distance))

    exchanges = [("dp", step) for step in dp_steps] + [("section", step) for step in section_steps]
    for axis, step in exchanges:
        got = swap(held, axis, step)
        if held.shape[0] < devices // 2:
            held = join(held, got)
    normed, grad_all, extra = call(
        functools.partial(order_kernel, sections, capacity, dp_steps, section_steps),
        [shape((rows, features), kept), shape((rows, features), kept), shape((2 * slots, features), wide)],
        (me,), (held, got, gain),
    )

    hidden_near, pre_near, expand_slice, project_slice = pl.pallas_call(
        hidden_kernel,
        out_shape=[shape((1, rows, units), kept)] * 2 + [shape((features, units), kept)] * 2,
        in_specs=[VMEM_SPEC] * 2 + [hbm] * 2 + [pl.BlockSpec(memory_space=pl.ANY)] * len(arrived),
        out_specs=[VMEM_SPEC] * 4,
        scratch_shapes=[pltpu.SemaphoreType.DMA((2 * replicas,))],
        compiler_params=pltpu.CompilerParams(vmem_limit_bytes=12 << 20),
    )(normed, grad_all, *in_hbm(expand_weight, project_turned), *arrived)

    tail_steps = section_steps[::-1]
    keep, send = call(
        functools.partial(share_kernel, sections, capacity, tail_steps),
        [shape((2, devices // 2, slots, features), kind) for kind in (wide, kept)],
        (me,), (hidden_near, pre_near, expand_slice, project_slice),
    )
    for place, step in enumerate(tail_steps):
        got = swap(send, "section", step)
        if place < len(tail_steps) - 1:
            half = (2, send.shape[1] // 2, slots, features)
            keep, send = call(
                halve_kernel, [shape(half, wide), shape(half, kept)], (), (keep, got)
            )
    tail = call(address_kernel, shape((replicas, 2 * slots, features), kept), (), (keep, got))
    tail = lax.all_to_all(tail, "dp", split_axis=0, concat_axis=0, tiled=True)

    hidden_steps, pre_steps = dp_steps, dp_steps[-1:] + dp_steps[:-1]
    for hidden_step, pre_step in zip(hidden_steps, pre_steps):
        hidden_far = swap(hidden_near, "dp", hidden_step)
        pre_far = swap(pre_near, "dp", pre_step)
        if hidden_near.shape[0] < replicas // 2:
            hidden_near = join(hidden_near, hidden_far)
            pre_near = join(pre_near, pre_far)

    grads = weight_grads(
        me, hidden_near, pre_near, 0,
        hidden_steps, pre_steps, normed, grad_all, width, (),
    )
    expand_grad, project_grad = weight_grads(
        me, hidden_far, pre_far, replicas // 2,
        hidden_steps, pre_steps, normed, grad_all, width, grads,
    )
    embedded, grad_rows = call(
        functools.partial(finish_kernel, capacity),
        [shape(text.shape, kept), shape(patches.shape, kept)],
        (me, counts, positions), (tail, extra, patches, text, gain),
    )
    return (embedded, grad_rows, expand_grad, project_grad.T)


def power_of_two(value):
    return value > 0 and value & (value - 1) == 0


def shards(patches, gain, expand_weight, project_weight, counts, positions, text, cotangent):
    replicas, sections = lax.axis_size("dp"), lax.axis_size("section")
    slots, features = patches.shape
    width = expand_weight.shape[1]
    rows = replicas * sections * slots
    fits = rows * (features + width) <= features * width
    even = (
        all(power_of_two(n) for n in (replicas, sections, slots))
        and replicas > 1
        and sections > 1
        and slots % 8 == 0
        and width % (128 * replicas) == 0
    )
    if fits and even:
        plan = move_rows_plan
    else:
        plan = gather_weights_plan
    return plan(
        patches, gain, expand_weight, project_weight, counts, positions, text, cotangent
    )


def solution(mesh):
    return jax.shard_map(
        shards,
        mesh=mesh,
        in_specs=(
            P(("dp", "section"), None),
            P(),
            P("dp", "section"),
            P("section", "dp"),
            P("dp", None),
            P(("dp", "section"), None),
            P(("dp", "section"), None),
            P(("dp", "section"), None),
        ),
        out_specs=(
            P(("dp", "section"), None),
            P(("dp", "section"), None),
            P(None, "section"),
            P("section", None),
        ),
        check_vma=False,
    )
```

```python
import functools

import jax
import jax.numpy as jnp
from jax import lax
from jax.experimental import pallas as pl
from jax.experimental.pallas import tpu as pltpu
from jax.sharding import PartitionSpec as P


def gelu_pair(values):
    coeff = 0.7978845608
    inner = coeff * (values + 0.044715 * values * values * values)
    tangent = jnp.tanh(inner)
    activated = 0.5 * values * (1.0 + tangent)
    derivative = 0.5 * (1.0 + tangent) + 0.5 * values * (1.0 - tangent * tangent) * coeff * (
        1.0 + 3.0 * 0.044715 * values * values
    )
    return (activated, derivative)


def gather_weights_plan(
    patches, gain, expand_weight, project_weight, counts, positions, text, cotangent
):
    sections = lax.axis_size("section")
    slot_count = patches.shape[0]
    features = patches.shape[1]
    capacity = slot_count // sections
    inputs = patches.astype(jnp.float32)
    inv_rms = lax.rsqrt(jnp.mean(inputs * inputs, axis=-1, keepdims=True) + 1e-06)
    normed = (inputs * inv_rms * gain).astype(jnp.bfloat16)
    gathered = lax.all_gather(normed, "section", axis=0, tiled=True)
    expand_full, project_full = (
        lax.all_gather(expand_weight, "dp", axis=0, tiled=True),
        lax.all_gather(project_weight, "dp", axis=1, tiled=True),
    )
    preact = jnp.dot(gathered, expand_full, preferred_element_type=jnp.float32)
    activated, derivative = gelu_pair(preact)
    hidden = activated.astype(jnp.bfloat16)
    row_block = hidden
    mixed = lax.psum_scatter(
        jnp.dot(row_block, project_full, preferred_element_type=jnp.float32).astype(jnp.bfloat16),
        "section",
        scatter_dimension=0,
        tiled=True,
    ).astype(jnp.float32)
    out_rows = (inputs + mixed).astype(jnp.bfloat16)
    arrived = lax.all_to_all(out_rows, "section", split_axis=0, concat_axis=0, tiled=True)
    section_id = lax.axis_index("section")
    arrival = jnp.arange(slot_count, dtype=jnp.int32)
    source = arrival // capacity
    slot_index = section_id * capacity + arrival % capacity
    is_live = (slot_index < counts[0][source])[:, None]
    targets = positions[0]
    current = text[targets]
    embedded = text.at[targets].set(jnp.where(is_live, arrived, current))
    picked = jnp.where(is_live, cotangent[targets], jnp.zeros_like(current))
    collected = lax.all_gather(picked, "section", axis=0, tiled=True)
    grad_all = (
        collected.reshape(sections, sections, capacity, features)
        .transpose(1, 0, 2, 3)
        .reshape(sections * slot_count, features)
    )
    returned = lax.dynamic_slice_in_dim(grad_all, section_id * slot_count, slot_count, 0)
    grad_own = returned.astype(jnp.float32)
    project_local = lax.dot_general(
        hidden, grad_all, (((0,), (0,)), ((), ())), preferred_element_type=jnp.float32
    )
    grad_hidden = lax.dot_general(
        grad_all, project_full, (((1,), (1,)), ((), ())), preferred_element_type=jnp.float32
    )
    grad_pre = (grad_hidden * derivative).astype(jnp.bfloat16)
    row_block = grad_pre
    grad_normed = lax.psum_scatter(
        lax.dot_general(
            row_block, expand_full, (((1,), (1,)), ((), ())), preferred_element_type=jnp.float32
        ).astype(jnp.bfloat16),
        "section",
        scatter_dimension=0,
        tiled=True,
    ).astype(jnp.float32)
    expand_local = lax.dot_general(
        gathered, grad_pre, (((0,), (0,)), ((), ())), preferred_element_type=jnp.float32
    )
    project_total, expand_total = (
        lax.psum(project_local.astype(jnp.bfloat16), "dp").astype(jnp.float32),
        lax.psum(expand_local.astype(jnp.bfloat16), "dp").astype(jnp.float32),
    )
    scaled_grad = grad_normed * gain
    centred = jnp.mean(scaled_grad * inputs, axis=-1, keepdims=True)
    grad_rows = (grad_own + inv_rms * scaled_grad - inputs * inv_rms**3 * centred).astype(
        jnp.bfloat16
    )
    return (
        embedded,
        grad_rows,
        expand_total.astype(jnp.bfloat16),
        project_total.astype(jnp.bfloat16),
    )


def bit_steps(size):
    steps = []
    step = size // 2
    while step >= 1:
        steps.append(step)
        step //= 2
    return steps


def swap(array, axis, step):
    size = lax.axis_size(axis)
    return lax.ppermute(array, axis, [(i, i ^ step) for i in range(size)])


def masked_steps(index, steps):
    mask = 0
    for place, step in enumerate(steps):
        mask = mask + ((index >> place) & 1) * step
    return mask


VMEM_SPEC = pl.BlockSpec(memory_space=pltpu.VMEM)
SMEM_SPEC = pl.BlockSpec(memory_space=pltpu.SMEM)


def log2(value):
    return value.bit_length() - 1


def landing(place_ref, count_ref, section, slots, capacity, length):
    row = lax.broadcasted_iota(jnp.int32, (slots, length), 0)
    column = lax.broadcasted_iota(jnp.int32, (slots, length), 1)
    spot = jnp.full((slots, length), -1, jnp.int32)
    for q in range(slots):
        live = section * capacity + q % capacity < count_ref[0, q // capacity]
        spot = jnp.where(row == q, jnp.where(live, place_ref[0, q], -1), spot)
    return (spot == column).astype(jnp.float32)


def fetch(copies):
    for copy in copies:
        copy.start()
    for copy in copies:
        copy.wait()


def pick_kernel(
    capacity, counts_at, places_at, patches_at, cotangent_at, pair_ref,
    count_ref, place_ref, patch_ref, cotangent_ref, sems,
):
    ends = (
        (counts_at, count_ref), (places_at, place_ref),
        (patches_at, patch_ref), (cotangent_at, cotangent_ref),
    )
    fetch([pltpu.make_async_copy(a, b, sems.at[i]) for i, (a, b) in enumerate(ends)])
    slots = patch_ref.shape[0]
    section = lax.axis_index("section")
    chooser = landing(
        place_ref, count_ref, section, slots, capacity, cotangent_ref.shape[0]
    ).astype(jnp.bfloat16)
    picked = jnp.dot(chooser, cotangent_ref[...], preferred_element_type=jnp.float32)
    pair_ref[0] = jnp.concatenate(
        [patch_ref[...].astype(jnp.float32), picked], axis=0
    ).astype(jnp.bfloat16)


def repack_kernel(expand_at, project_at, *refs):
    blocks, sems = refs[:-1], refs[-1]
    units = blocks[0].shape[2]
    copies = []
    for i, block in enumerate(blocks):
        start = pl.multiple_of((lax.axis_index("dp") ^ (i + 1)) * units, 128)
        for k, source in enumerate((expand_at, project_at)):
            copies.append(
                pltpu.make_async_copy(
                    source.at[:, pl.ds(start, units)], block.at[k], sems.at[2 * i + k]
                )
            )
    fetch(copies)


def join_kernel(first_ref, second_ref, out_ref):
    count = first_ref.shape[0]
    out_ref[:count] = first_ref[...]
    out_ref[count:] = second_ref[...]


def order_kernel(
    sections, capacity, dp_steps, section_steps,
    me_ref, near_ref, far_ref, gain_ref, normed_ref, grad_ref, extra_ref,
):
    rows = normed_ref.shape[0]
    slots = sections * capacity
    half = near_ref.shape[0] * near_ref.shape[1]
    me_dp, me_section = me_ref[0], me_ref[1]
    column = lax.broadcasted_iota(jnp.int32, (8, half), 1)
    row = lax.broadcasted_iota(jnp.int32, (rows, half), 0)
    kind = column & (2 * slots - 1)
    slot = kind & (slots - 1)
    inputs = grad = None
    for side, ref in enumerate((near_ref, far_ref)):
        block = (column >> log2(2 * slots)) + side * (half // (2 * slots))
        source_dp = me_dp ^ masked_steps(block, dp_steps)
        source_section = me_section ^ masked_steps(block >> len(dp_steps), section_steps)
        patch_at = (source_dp * sections + source_section) * slots + slot
        grad_at = (
            (source_dp * sections + (slot >> log2(capacity))) * slots
            + source_section * capacity
            + (slot & (capacity - 1))
        )
        patch_at = jnp.where(kind < slots, patch_at, -1)[:1]
        grad_at = jnp.where(kind >= slots, grad_at, -1)[:1]
        values = ref[...].reshape(half, ref.shape[2])
        chosen = (row == patch_at).astype(jnp.float32).astype(jnp.bfloat16)
        found = jnp.dot(chosen, values, preferred_element_type=jnp.float32)
        inputs = found if inputs is None else inputs + found
        chosen = (row == grad_at).astype(jnp.float32).astype(jnp.bfloat16)
        found = jnp.dot(chosen, values, preferred_element_type=jnp.float32)
        grad = found if grad is None else grad + found
    inv_rms = lax.rsqrt(jnp.mean(inputs * inputs, axis=-1, keepdims=True) + 1e-06)
    normed_ref[...] = (inputs * inv_rms * gain_ref[...]).astype(jnp.bfloat16)
    grad = grad.astype(jnp.bfloat16)
    grad_ref[...] = grad
    mine = lax.broadcasted_iota(jnp.int32, (slots, rows), 0)
    every = lax.broadcasted_iota(jnp.int32, (slots, rows), 1)
    coming_at = (
        (me_dp * sections + (mine >> log2(capacity))) * slots
        + me_section * capacity
        + (mine & (capacity - 1))
    )
    own_at = (me_dp * sections + me_section) * slots + mine
    coming = jnp.dot(
        (every == coming_at).astype(jnp.float32).astype(jnp.bfloat16),
        inputs.astype(jnp.bfloat16),
        preferred_element_type=jnp.float32,
    )
    own = jnp.dot(
        (every == own_at).astype(jnp.float32).astype(jnp.bfloat16),
        grad,
        preferred_element_type=jnp.float32,
    )
    extra_ref[...] = jnp.concatenate([coming, own], axis=0)


def hidden_kernel(normed_ref, grad_ref, expand_at, project_at, *refs):
    blocks = refs[:-4]
    both_ref, expand_ref, project_ref, sems = refs[-4:]
    part = expand_at.shape[0]
    units = both_ref.shape[2]
    me = lax.axis_index("dp")
    copies = []
    for k, (source, whole) in enumerate(((expand_at, expand_ref), (project_at, project_ref))):
        own = source.at[:, pl.ds(pl.multiple_of(me * units, 128), units)]
        for i, block in enumerate((own, *(block.at[k] for block in blocks))):
            at = pl.ds(pl.multiple_of((me ^ i) * part, 8), part)
            copies.append(
                pltpu.make_async_copy(
                    block, whole.at[at, :], sems.at[k * (len(blocks) + 1) + i]
                )
            )
    fetch(copies)
    preact = jnp.dot(normed_ref[...], expand_ref[...], preferred_element_type=jnp.float32)
    activated, derivative = gelu_pair(preact)
    both_ref[0] = activated.astype(jnp.bfloat16)
    grad_hidden = jnp.dot(grad_ref[...], project_ref[...], preferred_element_type=jnp.float32)
    both_ref[1] = (grad_hidden * derivative).astype(jnp.bfloat16)


def share_kernel(
    sections, capacity, steps,
    me_ref, both_ref, expand_ref, project_ref, keep_ref, send_ref,
):
    rows = both_ref.shape[1]
    slots = sections * capacity
    row = lax.broadcasted_iota(jnp.int32, (rows, rows), 0)
    column = lax.broadcasted_iota(jnp.int32, (rows, rows), 1)
    inside = row & (slots - 1)
    replica = (row >> log2(slots)) & (rows // (sections * slots) - 1)
    away = row >> log2(rows // sections)
    goal = me_ref[1] ^ masked_steps(away, steps[::-1])
    base = replica * (slots * sections)
    mixed_from = (
        base + (inside >> log2(capacity)) * slots + goal * capacity + (inside & (capacity - 1))
    )
    normed_from = base + goal * slots + inside
    for k, (source, weight_ref) in enumerate(
        ((mixed_from, project_ref), (normed_from, expand_ref))
    ):
        turn = (column == source).astype(jnp.float32).astype(jnp.bfloat16)
        turned = jnp.dot(turn, both_ref[k], preferred_element_type=jnp.float32).astype(jnp.bfloat16)
        share = lax.dot_general(
            turned, weight_ref[...], (((1,), (1,)), ((), ())), preferred_element_type=jnp.float32
        )
        share = share.reshape(2, *keep_ref.shape[1:])
        keep_ref[k] = share[0]
        send_ref[k] = share[1].astype(jnp.bfloat16)


def halve_kernel(keep_ref, got_ref, next_keep_ref, next_send_ref):
    half = next_keep_ref.shape[1]
    total = keep_ref[...] + got_ref[...].astype(jnp.float32)
    next_keep_ref[...] = total[:, :half]
    next_send_ref[...] = total[:, half:].astype(jnp.bfloat16)


def address_kernel(keep_ref, got_ref, out_ref):
    total = keep_ref[...] + got_ref[...].astype(jnp.float32)
    for d in range(out_ref.shape[0]):
        out_ref[d] = jnp.concatenate([total[0, d], total[1, d]], axis=0).astype(jnp.bfloat16)


def weight_grad_kernel(me_ref, block_ref, rows_ref, *refs):
    refs[-1][...] = lax.dot_general(
        rows_ref[...], block_ref[0], (((0,), (0,)), ((), ())), preferred_element_type=jnp.float32
    ).astype(jnp.bfloat16)


def finish_kernel(
    capacity,
    me_ref, count_ref, place_ref, tail_ref, extra_ref, patch_ref, text_ref, gain_ref,
    embedded_ref, grad_rows_ref,
):
    slots = patch_ref.shape[0]
    total = tail_ref[0].astype(jnp.float32)
    for d in range(1, tail_ref.shape[0]):
        total += tail_ref[d].astype(jnp.float32)
    mixed, grad_normed = total[:slots], total[slots:]
    out_rows = (extra_ref[:slots, :] + mixed).astype(jnp.bfloat16)
    length = text_ref.shape[0]
    chooser = landing(place_ref, count_ref, me_ref[1], slots, capacity, length)
    contract = (((0,), (0,)), ((), ()))
    placed = lax.dot_general(
        chooser.astype(jnp.bfloat16), out_rows, contract, preferred_element_type=jnp.float32
    )
    taken = lax.dot_general(
        chooser.astype(jnp.bfloat16), jnp.ones((slots, 128), jnp.bfloat16),
        contract, preferred_element_type=jnp.float32,
    )[:, :1]
    embedded_ref[...] = jnp.where(
        taken > 0.5, placed, text_ref[...].astype(jnp.float32)
    ).astype(jnp.bfloat16)
    inputs = patch_ref[...].astype(jnp.float32)
    inv_rms = lax.rsqrt(jnp.mean(inputs * inputs, axis=-1, keepdims=True) + 1e-06)
    scaled_grad = grad_normed * gain_ref[...]
    centred = jnp.mean(scaled_grad * inputs, axis=-1, keepdims=True)
    grad_rows_ref[...] = (
        extra_ref[slots:, :] + inv_rms * scaled_grad - inputs * (inv_rms**3 * centred)
    ).astype(jnp.bfloat16)


def weight_grads(me, blocks, first_index, steps, values, width, before=()):
    count, rows, units = blocks.shape
    features = values.shape[1]
    return pl.pallas_call(
        weight_grad_kernel,
        grid_spec=pltpu.PrefetchScalarGridSpec(
            num_scalar_prefetch=1,
            grid=(count,),
            in_specs=[
                pl.BlockSpec((1, rows, units), lambda i, me_ref: (i, 0, 0)),
                pl.BlockSpec((rows, features), lambda i, me_ref: (0, 0)),
            ]
            + [pl.BlockSpec(memory_space=pl.ANY)] * len(before),
            out_specs=pl.BlockSpec(
                (features, units),
                lambda i, me_ref: (0, me_ref[0] ^ masked_steps(first_index + i, steps)),
            ),
        ),
        out_shape=jax.ShapeDtypeStruct((features, width), jnp.bfloat16),
        input_output_aliases={3: 0} if before else {},
        compiler_params=pltpu.CompilerParams(
            dimension_semantics=("arbitrary",), vmem_limit_bytes=12 << 20
        ),
        cost_estimate=pl.CostEstimate(
            flops=2 * count * rows * features * units,
            bytes_accessed=2 * count * units * features + 2 * rows * features,
            transcendentals=0,
        ),
    )(me, blocks, values, *before)


def call(kernel, out_shape, smem, vmem, scratch=()):
    single = not isinstance(out_shape, (list, tuple))
    return pl.pallas_call(
        kernel,
        out_shape=out_shape,
        in_specs=[SMEM_SPEC] * len(smem) + [VMEM_SPEC] * len(vmem),
        out_specs=VMEM_SPEC if single else [VMEM_SPEC] * len(out_shape),
        scratch_shapes=scratch,
        compiler_params=pltpu.CompilerParams(vmem_limit_bytes=12 << 20),
    )(*smem, *vmem)


def join(first, second):
    both = (first.shape[0] + second.shape[0], *first.shape[1:])
    return call(join_kernel, jax.ShapeDtypeStruct(both, first.dtype), (), (first, second))


def join_pairs_kernel(first_ref, second_ref, hidden_ref, pre_ref):
    for k, out_ref in enumerate((hidden_ref, pre_ref)):
        out_ref[0] = first_ref[k]
        out_ref[1] = second_ref[k]


def join_pairs(first, second):
    out = jax.ShapeDtypeStruct(first.shape, first.dtype)
    return call(join_pairs_kernel, [out, out], (), (first, second))


def move_rows_plan(
    patches, gain, expand_weight, project_weight, counts, positions, text, cotangent
):
    sections = lax.axis_size("section")
    replicas = lax.axis_size("dp")
    devices = sections * replicas
    slots, features = patches.shape
    part, width = expand_weight.shape
    units = width // replicas
    capacity = slots // sections
    rows = devices * slots
    dp_steps, section_steps = bit_steps(replicas), bit_steps(sections)
    me = jnp.stack([lax.axis_index("dp"), lax.axis_index("section")]).astype(jnp.int32)
    gain = gain.reshape(1, features)
    project_turned = project_weight.T
    kept, wide = jnp.bfloat16, jnp.float32
    shape = jax.ShapeDtypeStruct

    hbm = pl.BlockSpec(memory_space=pltpu.HBM)

    def in_hbm(*arrays):
        return [pltpu.with_memory_space_constraint(array, pltpu.HBM) for array in arrays]

    held = pl.pallas_call(
        functools.partial(pick_kernel, capacity),
        out_shape=shape((1, 2 * slots, features), kept),
        in_specs=[hbm] * 4,
        out_specs=VMEM_SPEC,
        scratch_shapes=[
            pltpu.SMEM(counts.shape, counts.dtype),
            pltpu.SMEM(positions.shape, positions.dtype),
            pltpu.VMEM(patches.shape, kept),
            pltpu.VMEM(cotangent.shape, kept),
            pltpu.SemaphoreType.DMA((4,)),
        ],
        compiler_params=pltpu.CompilerParams(vmem_limit_bytes=12 << 20),
    )(*in_hbm(counts, positions, patches, cotangent))
    blocks = pl.pallas_call(
        repack_kernel,
        out_shape=[shape((2, part, units), kept)] * (replicas - 1),
        in_specs=[hbm] * 2,
        out_specs=[VMEM_SPEC] * (replicas - 1),
        scratch_shapes=[pltpu.SemaphoreType.DMA((2 * replicas - 2,))],
        compiler_params=pltpu.CompilerParams(vmem_limit_bytes=12 << 20),
    )(*in_hbm(expand_weight, project_turned))
    arrived = []
    for distance in range(1, replicas):
        arrived.append(swap(blocks[distance - 1], "dp", distance))

    exchanges = [("dp", step) for step in dp_steps] + [("section", step) for step in section_steps]
    for axis, step in exchanges:
        got = swap(held, axis, step)
        if held.shape[0] < devices // 2:
            held = join(held, got)
    normed, grad_all, extra = call(
        functools.partial(order_kernel, sections, capacity, dp_steps, section_steps),
        [shape((rows, features), kept), shape((rows, features), kept), shape((2 * slots, features), wide)],
        (me,), (held, got, gain),
    )

    both, expand_slice, project_slice = pl.pallas_call(
        hidden_kernel,
        out_shape=[shape((2, rows, units), kept)] + [shape((features, units), kept)] * 2,
        in_specs=[VMEM_SPEC] * 2 + [hbm] * 2 + [pl.BlockSpec(memory_space=pl.ANY)] * len(arrived),
        out_specs=[VMEM_SPEC] * 3,
        scratch_shapes=[pltpu.SemaphoreType.DMA((2 * replicas,))],
        compiler_params=pltpu.CompilerParams(vmem_limit_bytes=12 << 20),
    )(normed, grad_all, *in_hbm(expand_weight, project_turned), *arrived)

    tail_steps = section_steps[::-1]
    keep, send = call(
        functools.partial(share_kernel, sections, capacity, tail_steps),
        [shape((2, devices // 2, slots, features), kind) for kind in (wide, kept)],
        (me,), (both, expand_slice, project_slice),
    )
    for place, step in enumerate(tail_steps):
        got = swap(send, "section", step)
        if place < len(tail_steps) - 1:
            half = (2, send.shape[1] // 2, slots, features)
            keep, send = call(
                halve_kernel, [shape(half, wide), shape(half, kept)], (), (keep, got)
            )
    tail = call(address_kernel, shape((replicas, 2 * slots, features), kept), (), (keep, got))
    tail = lax.all_to_all(tail, "dp", split_axis=0, concat_axis=0, tiled=True)

    far_both = swap(both, "dp", dp_steps[0])
    hidden_steps, pre_steps = dp_steps, dp_steps[:1] + dp_steps[:0:-1]
    hidden, pre = join_pairs(both, far_both)
    for place, (hidden_step, pre_step) in enumerate(zip(hidden_steps[1:], pre_steps[1:]), 1):
        hidden_far = swap(hidden, "dp", hidden_step)
        pre_far = swap(pre, "dp", pre_step)
        if hidden.shape[0] < replicas // 2:
            hidden, pre = join(hidden, hidden_far), join(pre, pre_far)

    half = replicas // 2
    project_grad = weight_grads(me, hidden, 0, hidden_steps, grad_all, width)
    expand_grad = weight_grads(me, pre, 0, pre_steps, normed, width)
    project_grad = weight_grads(
        me, hidden_far, half, hidden_steps, grad_all, width, (project_grad,)
    )
    expand_grad = weight_grads(me, pre_far, half, pre_steps, normed, width, (expand_grad,))
    embedded, grad_rows = call(
        functools.partial(finish_kernel, capacity),
        [shape(text.shape, kept), shape(patches.shape, kept)],
        (me, counts, positions), (tail, extra, patches, text, gain),
    )
    return (embedded, grad_rows, expand_grad, project_grad.T)


def power_of_two(value):
    return value > 0 and value & (value - 1) == 0


def shards(patches, gain, expand_weight, project_weight, counts, positions, text, cotangent):
    replicas, sections = lax.axis_size("dp"), lax.axis_size("section")
    slots, features = patches.shape
    width = expand_weight.shape[1]
    rows = replicas * sections * slots
    fits = rows * (features + width) <= features * width
    even = (
        all(power_of_two(n) for n in (replicas, sections, slots))
        and replicas > 2
        and sections > 1
        and slots % 8 == 0
        and width % (128 * replicas) == 0
    )
    if fits and even:
        plan = move_rows_plan
    else:
        plan = gather_weights_plan
    return plan(
        patches, gain, expand_weight, project_weight, counts, positions, text, cotangent
    )


def solution(mesh):
    return jax.shard_map(
        shards,
        mesh=mesh,
        in_specs=(
            P(("dp", "section"), None),
            P(),
            P("dp", "section"),
            P("section", "dp"),
            P("dp", None),
            P(("dp", "section"), None),
            P(("dp", "section"), None),
            P(("dp", "section"), None),
        ),
        out_specs=(
            P(("dp", "section"), None),
            P(("dp", "section"), None),
            P(None, "section"),
            P("section", None),
        ),
        check_vma=False,
    )
```

```python
import functools

import jax
import jax.numpy as jnp
from jax import lax
from jax.experimental import pallas as pl
from jax.experimental.pallas import tpu as pltpu
from jax.sharding import PartitionSpec as P


def gelu_pair(values):
    coeff = 0.7978845608
    inner = coeff * (values + 0.044715 * values * values * values)
    tangent = jnp.tanh(inner)
    activated = 0.5 * values * (1.0 + tangent)
    derivative = 0.5 * (1.0 + tangent) + 0.5 * values * (1.0 - tangent * tangent) * coeff * (
        1.0 + 3.0 * 0.044715 * values * values
    )
    return (activated, derivative)


def gather_weights_plan(
    patches, gain, expand_weight, project_weight, counts, positions, text, cotangent
):
    sections = lax.axis_size("section")
    slot_count = patches.shape[0]
    features = patches.shape[1]
    capacity = slot_count // sections
    inputs = patches.astype(jnp.float32)
    inv_rms = lax.rsqrt(jnp.mean(inputs * inputs, axis=-1, keepdims=True) + 1e-06)
    normed = (inputs * inv_rms * gain).astype(jnp.bfloat16)
    gathered = lax.all_gather(normed, "section", axis=0, tiled=True)
    expand_full, project_full = (
        lax.all_gather(expand_weight, "dp", axis=0, tiled=True),
        lax.all_gather(project_weight, "dp", axis=1, tiled=True),
    )
    preact = jnp.dot(gathered, expand_full, preferred_element_type=jnp.float32)
    activated, derivative = gelu_pair(preact)
    hidden = activated.astype(jnp.bfloat16)
    row_block = hidden
    mixed = lax.psum_scatter(
        jnp.dot(row_block, project_full, preferred_element_type=jnp.float32).astype(jnp.bfloat16),
        "section",
        scatter_dimension=0,
        tiled=True,
    ).astype(jnp.float32)
    out_rows = (inputs + mixed).astype(jnp.bfloat16)
    arrived = lax.all_to_all(out_rows, "section", split_axis=0, concat_axis=0, tiled=True)
    section_id = lax.axis_index("section")
    arrival = jnp.arange(slot_count, dtype=jnp.int32)
    source = arrival // capacity
    slot_index = section_id * capacity + arrival % capacity
    is_live = (slot_index < counts[0][source])[:, None]
    targets = positions[0]
    current = text[targets]
    embedded = text.at[targets].set(jnp.where(is_live, arrived, current))
    picked = jnp.where(is_live, cotangent[targets], jnp.zeros_like(current))
    collected = lax.all_gather(picked, "section", axis=0, tiled=True)
    grad_all = (
        collected.reshape(sections, sections, capacity, features)
        .transpose(1, 0, 2, 3)
        .reshape(sections * slot_count, features)
    )
    returned = lax.dynamic_slice_in_dim(grad_all, section_id * slot_count, slot_count, 0)
    grad_own = returned.astype(jnp.float32)
    project_local = lax.dot_general(
        hidden, grad_all, (((0,), (0,)), ((), ())), preferred_element_type=jnp.float32
    )
    grad_hidden = lax.dot_general(
        grad_all, project_full, (((1,), (1,)), ((), ())), preferred_element_type=jnp.float32
    )
    grad_pre = (grad_hidden * derivative).astype(jnp.bfloat16)
    row_block = grad_pre
    grad_normed = lax.psum_scatter(
        lax.dot_general(
            row_block, expand_full, (((1,), (1,)), ((), ())), preferred_element_type=jnp.float32
        ).astype(jnp.bfloat16),
        "section",
        scatter_dimension=0,
        tiled=True,
    ).astype(jnp.float32)
    expand_local = lax.dot_general(
        gathered, grad_pre, (((0,), (0,)), ((), ())), preferred_element_type=jnp.float32
    )
    project_total, expand_total = (
        lax.psum(project_local.astype(jnp.bfloat16), "dp").astype(jnp.float32),
        lax.psum(expand_local.astype(jnp.bfloat16), "dp").astype(jnp.float32),
    )
    scaled_grad = grad_normed * gain
    centred = jnp.mean(scaled_grad * inputs, axis=-1, keepdims=True)
    grad_rows = (grad_own + inv_rms * scaled_grad - inputs * inv_rms**3 * centred).astype(
        jnp.bfloat16
    )
    return (
        embedded,
        grad_rows,
        expand_total.astype(jnp.bfloat16),
        project_total.astype(jnp.bfloat16),
    )


def bit_steps(size):
    steps = []
    step = size // 2
    while step >= 1:
        steps.append(step)
        step //= 2
    return steps


def swap(array, axis, step):
    size = lax.axis_size(axis)
    return lax.ppermute(array, axis, [(i, i ^ step) for i in range(size)])


def masked_steps(index, steps):
    mask = 0
    for place, step in enumerate(steps):
        mask = mask + ((index >> place) & 1) * step
    return mask


VMEM_SPEC = pl.BlockSpec(memory_space=pltpu.VMEM)
SMEM_SPEC = pl.BlockSpec(memory_space=pltpu.SMEM)


def log2(value):
    return value.bit_length() - 1


def landing(place_ref, count_ref, section, slots, capacity, length):
    row = lax.broadcasted_iota(jnp.int32, (slots, length), 0)
    column = lax.broadcasted_iota(jnp.int32, (slots, length), 1)
    spot = jnp.full((slots, length), -1, jnp.int32)
    for q in range(slots):
        live = section * capacity + q % capacity < count_ref[0, q // capacity]
        spot = jnp.where(row == q, jnp.where(live, place_ref[0, q], -1), spot)
    return (spot == column).astype(jnp.float32)


def fetch(copies):
    for copy in copies:
        copy.start()
    for copy in copies:
        copy.wait()


def weight_copies(expand_at, project_at, distance, block, sems, first):
    units = block.shape[2]
    start = pl.multiple_of((lax.axis_index("dp") ^ distance) * units, 128)
    return [
        pltpu.make_async_copy(source.at[:, pl.ds(start, units)], block.at[k], sems.at[first + k])
        for k, source in enumerate((expand_at, project_at))
    ]


def pick_kernel(
    capacity, distance, counts_at, places_at, patches_at, cotangent_at, expand_at, project_at,
    pair_ref, block_ref, count_ref, place_ref, patch_ref, cotangent_ref, sems,
):
    ends = (
        (counts_at, count_ref), (places_at, place_ref),
        (patches_at, patch_ref), (cotangent_at, cotangent_ref),
    )
    fetch(
        [pltpu.make_async_copy(a, b, sems.at[i]) for i, (a, b) in enumerate(ends)]
        + weight_copies(expand_at, project_at, distance, block_ref, sems, 4)
    )
    slots = patch_ref.shape[0]
    section = lax.axis_index("section")
    chooser = landing(
        place_ref, count_ref, section, slots, capacity, cotangent_ref.shape[0]
    ).astype(jnp.bfloat16)
    picked = jnp.dot(chooser, cotangent_ref[...], preferred_element_type=jnp.float32)
    pair_ref[0] = jnp.concatenate(
        [patch_ref[...].astype(jnp.float32), picked], axis=0
    ).astype(jnp.bfloat16)


def repack_kernel(distances, expand_at, project_at, *refs):
    blocks, sems = refs[:-1], refs[-1]
    copies = []
    for i, (distance, block) in enumerate(zip(distances, blocks)):
        copies += weight_copies(expand_at, project_at, distance, block, sems, 2 * i)
    fetch(copies)


def turn_kernel(normed_ref, grad_ref, normed_turned_ref, grad_turned_ref):
    normed_turned_ref[...] = normed_ref[...].T
    grad_turned_ref[...] = grad_ref[...].T


def join_kernel(first_ref, second_ref, out_ref):
    count = first_ref.shape[0]
    out_ref[:count] = first_ref[...]
    out_ref[count:] = second_ref[...]


def order_kernel(
    sections, capacity, dp_steps, section_steps,
    me_ref, near_ref, far_ref, gain_ref, normed_ref, grad_ref, extra_ref,
):
    rows = normed_ref.shape[0]
    slots = sections * capacity
    half = near_ref.shape[0] * near_ref.shape[1]
    me_dp, me_section = me_ref[0], me_ref[1]
    column = lax.broadcasted_iota(jnp.int32, (8, half), 1)
    row = lax.broadcasted_iota(jnp.int32, (rows, half), 0)
    kind = column & (2 * slots - 1)
    slot = kind & (slots - 1)
    inputs = grad = None
    for side, ref in enumerate((near_ref, far_ref)):
        block = (column >> log2(2 * slots)) + side * (half // (2 * slots))
        source_dp = me_dp ^ masked_steps(block, dp_steps)
        source_section = me_section ^ masked_steps(block >> len(dp_steps), section_steps)
        patch_at = (source_dp * sections + source_section) * slots + slot
        grad_at = (
            (source_dp * sections + (slot >> log2(capacity))) * slots
            + source_section * capacity
            + (slot & (capacity - 1))
        )
        patch_at = jnp.where(kind < slots, patch_at, -1)[:1]
        grad_at = jnp.where(kind >= slots, grad_at, -1)[:1]
        values = ref[...].reshape(half, ref.shape[2])
        chosen = (row == patch_at).astype(jnp.float32).astype(jnp.bfloat16)
        found = jnp.dot(chosen, values, preferred_element_type=jnp.float32)
        inputs = found if inputs is None else inputs + found
        chosen = (row == grad_at).astype(jnp.float32).astype(jnp.bfloat16)
        found = jnp.dot(chosen, values, preferred_element_type=jnp.float32)
        grad = found if grad is None else grad + found
    inv_rms = lax.rsqrt(jnp.mean(inputs * inputs, axis=-1, keepdims=True) + 1e-06)
    normed_ref[...] = (inputs * inv_rms * gain_ref[...]).astype(jnp.bfloat16)
    grad = grad.astype(jnp.bfloat16)
    grad_ref[...] = grad
    mine = lax.broadcasted_iota(jnp.int32, (slots, rows), 0)
    every = lax.broadcasted_iota(jnp.int32, (slots, rows), 1)
    coming_at = (
        (me_dp * sections + (mine >> log2(capacity))) * slots
        + me_section * capacity
        + (mine & (capacity - 1))
    )
    own_at = (me_dp * sections + me_section) * slots + mine
    coming = jnp.dot(
        (every == coming_at).astype(jnp.float32).astype(jnp.bfloat16),
        inputs.astype(jnp.bfloat16),
        preferred_element_type=jnp.float32,
    )
    own = jnp.dot(
        (every == own_at).astype(jnp.float32).astype(jnp.bfloat16),
        grad,
        preferred_element_type=jnp.float32,
    )
    extra_ref[...] = jnp.concatenate([coming, own], axis=0)


def hidden_kernel(normed_ref, grad_ref, expand_at, project_at, *refs):
    blocks = refs[:-4]
    both_ref, expand_ref, project_ref, sems = refs[-4:]
    part = expand_at.shape[0]
    units = both_ref.shape[2]
    me = lax.axis_index("dp")
    copies = []
    for k, (source, whole) in enumerate(((expand_at, expand_ref), (project_at, project_ref))):
        own = source.at[:, pl.ds(pl.multiple_of(me * units, 128), units)]
        for i, block in enumerate((own, *(block.at[k] for block in blocks))):
            at = pl.ds(pl.multiple_of((me ^ i) * part, 8), part)
            copies.append(
                pltpu.make_async_copy(
                    block, whole.at[at, :], sems.at[k * (len(blocks) + 1) + i]
                )
            )
    fetch(copies)
    preact = jnp.dot(normed_ref[...], expand_ref[...], preferred_element_type=jnp.float32)
    activated, derivative = gelu_pair(preact)
    both_ref[0] = activated.astype(jnp.bfloat16)
    grad_hidden = jnp.dot(grad_ref[...], project_ref[...], preferred_element_type=jnp.float32)
    both_ref[1] = (grad_hidden * derivative).astype(jnp.bfloat16)


def share_kernel(
    sections, capacity, steps,
    me_ref, both_ref, expand_ref, project_ref, keep_ref, send_ref,
):
    rows = both_ref.shape[1]
    slots = sections * capacity
    row = lax.broadcasted_iota(jnp.int32, (rows, rows), 0)
    column = lax.broadcasted_iota(jnp.int32, (rows, rows), 1)
    inside = row & (slots - 1)
    replica = (row >> log2(slots)) & (rows // (sections * slots) - 1)
    away = row >> log2(rows // sections)
    goal = me_ref[1] ^ masked_steps(away, steps[::-1])
    base = replica * (slots * sections)
    mixed_from = (
        base + (inside >> log2(capacity)) * slots + goal * capacity + (inside & (capacity - 1))
    )
    normed_from = base + goal * slots + inside
    for k, (source, weight_ref) in enumerate(
        ((mixed_from, project_ref), (normed_from, expand_ref))
    ):
        turn = (column == source).astype(jnp.float32).astype(jnp.bfloat16)
        turned = jnp.dot(turn, both_ref[k], preferred_element_type=jnp.float32).astype(jnp.bfloat16)
        share = lax.dot_general(
            turned, weight_ref[...], (((1,), (1,)), ((), ())), preferred_element_type=jnp.float32
        )
        share = share.reshape(2, *keep_ref.shape[1:])
        keep_ref[k] = share[0]
        send_ref[k] = share[1].astype(jnp.bfloat16)


def halve_kernel(keep_ref, got_ref, next_keep_ref, next_send_ref):
    half = next_keep_ref.shape[1]
    total = keep_ref[...] + got_ref[...].astype(jnp.float32)
    next_keep_ref[...] = total[:, :half]
    next_send_ref[...] = total[:, half:].astype(jnp.bfloat16)


def address_kernel(keep_ref, got_ref, out_ref):
    total = keep_ref[...] + got_ref[...].astype(jnp.float32)
    for d in range(out_ref.shape[0]):
        out_ref[d] = jnp.concatenate([total[0, d], total[1, d]], axis=0).astype(jnp.bfloat16)


def weight_grad_kernel(me_ref, block_ref, rows_ref, *refs):
    refs[-1][...] = jnp.dot(
        rows_ref[...], block_ref[0], preferred_element_type=jnp.float32
    ).astype(jnp.bfloat16)


def finish_kernel(
    capacity,
    me_ref, count_ref, place_ref, tail_ref, extra_ref, patch_ref, text_ref, gain_ref,
    embedded_ref, grad_rows_ref,
):
    slots = patch_ref.shape[0]
    total = tail_ref[0].astype(jnp.float32)
    for d in range(1, tail_ref.shape[0]):
        total += tail_ref[d].astype(jnp.float32)
    mixed, grad_normed = total[:slots], total[slots:]
    out_rows = (extra_ref[:slots, :] + mixed).astype(jnp.bfloat16)
    length = text_ref.shape[0]
    chooser = landing(place_ref, count_ref, me_ref[1], slots, capacity, length)
    contract = (((0,), (0,)), ((), ()))
    placed = lax.dot_general(
        chooser.astype(jnp.bfloat16), out_rows, contract, preferred_element_type=jnp.float32
    )
    taken = lax.dot_general(
        chooser.astype(jnp.bfloat16), jnp.ones((slots, 128), jnp.bfloat16),
        contract, preferred_element_type=jnp.float32,
    )[:, :1]
    embedded_ref[...] = jnp.where(
        taken > 0.5, placed, text_ref[...].astype(jnp.float32)
    ).astype(jnp.bfloat16)
    inputs = patch_ref[...].astype(jnp.float32)
    inv_rms = lax.rsqrt(jnp.mean(inputs * inputs, axis=-1, keepdims=True) + 1e-06)
    scaled_grad = grad_normed * gain_ref[...]
    centred = jnp.mean(scaled_grad * inputs, axis=-1, keepdims=True)
    grad_rows_ref[...] = (
        extra_ref[slots:, :] + inv_rms * scaled_grad - inputs * (inv_rms**3 * centred)
    ).astype(jnp.bfloat16)


def weight_grads(me, blocks, first_index, steps, values, width, before=()):
    count, rows, units = blocks.shape
    features = values.shape[0]
    return pl.pallas_call(
        weight_grad_kernel,
        grid_spec=pltpu.PrefetchScalarGridSpec(
            num_scalar_prefetch=1,
            grid=(count,),
            in_specs=[
                pl.BlockSpec((1, rows, units), lambda i, me_ref: (i, 0, 0)),
                pl.BlockSpec((features, rows), lambda i, me_ref: (0, 0)),
            ]
            + [pl.BlockSpec(memory_space=pl.ANY)] * len(before),
            out_specs=pl.BlockSpec(
                (features, units),
                lambda i, me_ref: (0, me_ref[0] ^ masked_steps(first_index + i, steps)),
            ),
        ),
        out_shape=jax.ShapeDtypeStruct((features, width), jnp.bfloat16),
        input_output_aliases={3: 0} if before else {},
        compiler_params=pltpu.CompilerParams(
            dimension_semantics=("arbitrary",), vmem_limit_bytes=12 << 20
        ),
        cost_estimate=pl.CostEstimate(
            flops=2 * count * rows * features * units,
            bytes_accessed=2 * count * units * features + 2 * rows * features,
            transcendentals=0,
        ),
    )(me, blocks, values, *before)


def call(kernel, out_shape, smem, vmem, scratch=()):
    single = not isinstance(out_shape, (list, tuple))
    return pl.pallas_call(
        kernel,
        out_shape=out_shape,
        in_specs=[SMEM_SPEC] * len(smem) + [VMEM_SPEC] * len(vmem),
        out_specs=VMEM_SPEC if single else [VMEM_SPEC] * len(out_shape),
        scratch_shapes=scratch,
        compiler_params=pltpu.CompilerParams(vmem_limit_bytes=12 << 20),
    )(*smem, *vmem)


def join(first, second):
    both = (first.shape[0] + second.shape[0], *first.shape[1:])
    return call(join_kernel, jax.ShapeDtypeStruct(both, first.dtype), (), (first, second))


def join_pairs_kernel(first_ref, second_ref, hidden_ref, pre_ref):
    for k, out_ref in enumerate((hidden_ref, pre_ref)):
        out_ref[0] = first_ref[k]
        out_ref[1] = second_ref[k]


def join_pairs(first, second):
    out = jax.ShapeDtypeStruct(first.shape, first.dtype)
    return call(join_pairs_kernel, [out, out], (), (first, second))


def move_rows_plan(
    patches, gain, expand_weight, project_weight, counts, positions, text, cotangent
):
    sections = lax.axis_size("section")
    replicas = lax.axis_size("dp")
    devices = sections * replicas
    slots, features = patches.shape
    part, width = expand_weight.shape
    units = width // replicas
    capacity = slots // sections
    rows = devices * slots
    dp_steps, section_steps = bit_steps(replicas), bit_steps(sections)
    me = jnp.stack([lax.axis_index("dp"), lax.axis_index("section")]).astype(jnp.int32)
    gain = gain.reshape(1, features)
    project_turned = project_weight.T
    kept, wide = jnp.bfloat16, jnp.float32
    shape = jax.ShapeDtypeStruct

    hbm = pl.BlockSpec(memory_space=pltpu.HBM)

    def in_hbm(*arrays):
        return [pltpu.with_memory_space_constraint(array, pltpu.HBM) for array in arrays]

    first = dp_steps[0]
    others = [distance for distance in range(1, replicas) if distance != first]
    sources = in_hbm(expand_weight, project_turned)
    held, block = pl.pallas_call(
        functools.partial(pick_kernel, capacity, first),
        out_shape=[shape((1, 2 * slots, features), kept), shape((2, part, units), kept)],
        in_specs=[hbm] * 6,
        out_specs=[VMEM_SPEC] * 2,
        scratch_shapes=[
            pltpu.SMEM(counts.shape, counts.dtype),
            pltpu.SMEM(positions.shape, positions.dtype),
            pltpu.VMEM(patches.shape, kept),
            pltpu.VMEM(cotangent.shape, kept),
            pltpu.SemaphoreType.DMA((6,)),
        ],
        compiler_params=pltpu.CompilerParams(vmem_limit_bytes=12 << 20),
    )(*in_hbm(counts, positions, patches, cotangent), *sources)
    rest = pl.pallas_call(
        functools.partial(repack_kernel, others),
        out_shape=[shape((2, part, units), kept)] * len(others),
        in_specs=[hbm] * 2,
        out_specs=[VMEM_SPEC] * len(others),
        scratch_shapes=[pltpu.SemaphoreType.DMA((2 * len(others),))],
        compiler_params=pltpu.CompilerParams(vmem_limit_bytes=12 << 20),
    )(*sources)
    blocks = dict(zip([first, *others], [block, *rest]))
    arrived = []
    for distance in range(1, replicas):
        arrived.append(swap(blocks[distance], "dp", distance))

    exchanges = [("dp", step) for step in dp_steps] + [("section", step) for step in section_steps]
    for axis, step in exchanges:
        got = swap(held, axis, step)
        if held.shape[0] < devices // 2:
            held = join(held, got)
    normed, grad_all, extra = call(
        functools.partial(order_kernel, sections, capacity, dp_steps, section_steps),
        [shape((rows, features), kept), shape((rows, features), kept), shape((2 * slots, features), wide)],
        (me,), (held, got, gain),
    )

    normed_turned, grad_turned = call(
        turn_kernel, [shape((features, rows), kept)] * 2, (), (normed, grad_all)
    )
    both, expand_slice, project_slice = pl.pallas_call(
        hidden_kernel,
        out_shape=[shape((2, rows, units), kept)] + [shape((features, units), kept)] * 2,
        in_specs=[VMEM_SPEC] * 2 + [hbm] * 2 + [pl.BlockSpec(memory_space=pl.ANY)] * len(arrived),
        out_specs=[VMEM_SPEC] * 3,
        scratch_shapes=[pltpu.SemaphoreType.DMA((2 * replicas,))],
        compiler_params=pltpu.CompilerParams(vmem_limit_bytes=12 << 20),
    )(normed, grad_all, *sources, *arrived)

    tail_steps = section_steps[::-1]
    keep, send = call(
        functools.partial(share_kernel, sections, capacity, tail_steps),
        [shape((2, devices // 2, slots, features), kind) for kind in (wide, kept)],
        (me,), (both, expand_slice, project_slice),
    )
    for place, step in enumerate(tail_steps):
        got = swap(send, "section", step)
        if place < len(tail_steps) - 1:
            half = (2, send.shape[1] // 2, slots, features)
            keep, send = call(
                halve_kernel, [shape(half, wide), shape(half, kept)], (), (keep, got)
            )
    tail = call(address_kernel, shape((replicas, 2 * slots, features), kept), (), (keep, got))
    tail = lax.all_to_all(tail, "dp", split_axis=0, concat_axis=0, tiled=True)

    far_both = swap(both, "dp", dp_steps[0])
    hidden_steps, pre_steps = dp_steps, dp_steps[:1] + dp_steps[:0:-1]
    hidden, pre = join_pairs(both, far_both)
    hidden_new, pre_new, new_at = hidden, pre, 0
    project_grad = expand_grad = ()
    for place in range(1, len(dp_steps) + 1):
        project_grad = (
            weight_grads(me, hidden_new, new_at, hidden_steps, grad_turned, width, project_grad),
        )
        expand_grad = (
            weight_grads(me, pre_new, new_at, pre_steps, normed_turned, width, expand_grad),
        )
        if place == len(dp_steps):
            break
        new_at = hidden.shape[0]
        hidden_new = swap(hidden, "dp", hidden_steps[place])
        pre_new = swap(pre, "dp", pre_steps[place])
        if place < len(dp_steps) - 1:
            hidden, pre = join(hidden, hidden_new), join(pre, pre_new)
    embedded, grad_rows = call(
        functools.partial(finish_kernel, capacity),
        [shape(text.shape, kept), shape(patches.shape, kept)],
        (me, counts, positions), (tail, extra, patches, text, gain),
    )
    return (embedded, grad_rows, expand_grad[0], project_grad[0].T)


def power_of_two(value):
    return value > 0 and value & (value - 1) == 0


def shards(patches, gain, expand_weight, project_weight, counts, positions, text, cotangent):
    replicas, sections = lax.axis_size("dp"), lax.axis_size("section")
    slots, features = patches.shape
    width = expand_weight.shape[1]
    rows = replicas * sections * slots
    fits = rows * (features + width) <= features * width
    even = (
        all(power_of_two(n) for n in (replicas, sections, slots))
        and replicas > 2
        and sections > 1
        and slots % 8 == 0
        and width % (128 * replicas) == 0
    )
    if fits and even:
        plan = move_rows_plan
    else:
        plan = gather_weights_plan
    return plan(
        patches, gain, expand_weight, project_weight, counts, positions, text, cotangent
    )


def solution(mesh):
    return jax.shard_map(
        shards,
        mesh=mesh,
        in_specs=(
            P(("dp", "section"), None),
            P(),
            P("dp", "section"),
            P("section", "dp"),
            P("dp", None),
            P(("dp", "section"), None),
            P(("dp", "section"), None),
            P(("dp", "section"), None),
        ),
        out_specs=(
            P(("dp", "section"), None),
            P(("dp", "section"), None),
            P(None, "section"),
            P("section", None),
        ),
        check_vma=False,
    )
```

```python
import functools

import jax
import jax.numpy as jnp
from jax import lax
from jax.experimental import pallas as pl
from jax.experimental.pallas import tpu as pltpu
from jax.sharding import PartitionSpec as P


def gelu_pair(values):
    coeff = 0.7978845608
    inner = coeff * (values + 0.044715 * values * values * values)
    tangent = jnp.tanh(inner)
    activated = 0.5 * values * (1.0 + tangent)
    derivative = 0.5 * (1.0 + tangent) + 0.5 * values * (1.0 - tangent * tangent) * coeff * (
        1.0 + 3.0 * 0.044715 * values * values
    )
    return (activated, derivative)


def gather_weights_plan(
    patches, gain, expand_weight, project_weight, counts, positions, text, cotangent
):
    sections = lax.axis_size("section")
    slot_count = patches.shape[0]
    features = patches.shape[1]
    capacity = slot_count // sections
    inputs = patches.astype(jnp.float32)
    inv_rms = lax.rsqrt(jnp.mean(inputs * inputs, axis=-1, keepdims=True) + 1e-06)
    normed = (inputs * inv_rms * gain).astype(jnp.bfloat16)
    gathered = lax.all_gather(normed, "section", axis=0, tiled=True)
    expand_full, project_full = (
        lax.all_gather(expand_weight, "dp", axis=0, tiled=True),
        lax.all_gather(project_weight, "dp", axis=1, tiled=True),
    )
    preact = jnp.dot(gathered, expand_full, preferred_element_type=jnp.float32)
    activated, derivative = gelu_pair(preact)
    hidden = activated.astype(jnp.bfloat16)
    row_block = hidden
    mixed = lax.psum_scatter(
        jnp.dot(row_block, project_full, preferred_element_type=jnp.float32).astype(jnp.bfloat16),
        "section",
        scatter_dimension=0,
        tiled=True,
    ).astype(jnp.float32)
    out_rows = (inputs + mixed).astype(jnp.bfloat16)
    arrived = lax.all_to_all(out_rows, "section", split_axis=0, concat_axis=0, tiled=True)
    section_id = lax.axis_index("section")
    arrival = jnp.arange(slot_count, dtype=jnp.int32)
    source = arrival // capacity
    slot_index = section_id * capacity + arrival % capacity
    is_live = (slot_index < counts[0][source])[:, None]
    targets = positions[0]
    current = text[targets]
    embedded = text.at[targets].set(jnp.where(is_live, arrived, current))
    picked = jnp.where(is_live, cotangent[targets], jnp.zeros_like(current))
    collected = lax.all_gather(picked, "section", axis=0, tiled=True)
    grad_all = (
        collected.reshape(sections, sections, capacity, features)
        .transpose(1, 0, 2, 3)
        .reshape(sections * slot_count, features)
    )
    returned = lax.dynamic_slice_in_dim(grad_all, section_id * slot_count, slot_count, 0)
    grad_own = returned.astype(jnp.float32)
    project_local = lax.dot_general(
        hidden, grad_all, (((0,), (0,)), ((), ())), preferred_element_type=jnp.float32
    )
    grad_hidden = lax.dot_general(
        grad_all, project_full, (((1,), (1,)), ((), ())), preferred_element_type=jnp.float32
    )
    grad_pre = (grad_hidden * derivative).astype(jnp.bfloat16)
    row_block = grad_pre
    grad_normed = lax.psum_scatter(
        lax.dot_general(
            row_block, expand_full, (((1,), (1,)), ((), ())), preferred_element_type=jnp.float32
        ).astype(jnp.bfloat16),
        "section",
        scatter_dimension=0,
        tiled=True,
    ).astype(jnp.float32)
    expand_local = lax.dot_general(
        gathered, grad_pre, (((0,), (0,)), ((), ())), preferred_element_type=jnp.float32
    )
    project_total, expand_total = (
        lax.psum(project_local.astype(jnp.bfloat16), "dp").astype(jnp.float32),
        lax.psum(expand_local.astype(jnp.bfloat16), "dp").astype(jnp.float32),
    )
    scaled_grad = grad_normed * gain
    centred = jnp.mean(scaled_grad * inputs, axis=-1, keepdims=True)
    grad_rows = (grad_own + inv_rms * scaled_grad - inputs * inv_rms**3 * centred).astype(
        jnp.bfloat16
    )
    return (
        embedded,
        grad_rows,
        expand_total.astype(jnp.bfloat16),
        project_total.astype(jnp.bfloat16),
    )


def bit_steps(size):
    steps = []
    step = size // 2
    while step >= 1:
        steps.append(step)
        step //= 2
    return steps


def swap(array, axis, step):
    size = lax.axis_size(axis)
    return lax.ppermute(array, axis, [(i, i ^ step) for i in range(size)])


def masked_steps(index, steps):
    mask = 0
    for place, step in enumerate(steps):
        mask = mask + ((index >> place) & 1) * step
    return mask


VMEM_SPEC = pl.BlockSpec(memory_space=pltpu.VMEM)
SMEM_SPEC = pl.BlockSpec(memory_space=pltpu.SMEM)


def log2(value):
    return value.bit_length() - 1


def landing(place_ref, count_ref, section, slots, capacity, length):
    row = lax.broadcasted_iota(jnp.int32, (slots, length), 0)
    column = lax.broadcasted_iota(jnp.int32, (slots, length), 1)
    spot = jnp.full((slots, length), -1, jnp.int32)
    for q in range(slots):
        live = section * capacity + q % capacity < count_ref[0, q // capacity]
        spot = jnp.where(row == q, jnp.where(live, place_ref[0, q], -1), spot)
    return (spot == column).astype(jnp.float32)


def fetch(copies):
    for copy in copies:
        copy.start()
    for copy in copies:
        copy.wait()


def pick_kernel(
    capacity, counts_at, places_at, patches_at, cotangent_at, pair_ref,
    count_ref, place_ref, patch_ref, cotangent_ref, sems,
):
    ends = (
        (counts_at, count_ref), (places_at, place_ref),
        (patches_at, patch_ref), (cotangent_at, cotangent_ref),
    )
    fetch([pltpu.make_async_copy(a, b, sems.at[i]) for i, (a, b) in enumerate(ends)])
    slots = patch_ref.shape[0]
    section = lax.axis_index("section")
    chooser = landing(
        place_ref, count_ref, section, slots, capacity, cotangent_ref.shape[0]
    ).astype(jnp.bfloat16)
    picked = jnp.dot(chooser, cotangent_ref[...], preferred_element_type=jnp.float32)
    pair_ref[0] = jnp.concatenate(
        [patch_ref[...].astype(jnp.float32), picked], axis=0
    ).astype(jnp.bfloat16)


def repack_kernel(expand_at, project_at, *refs):
    blocks, sems = refs[:-1], refs[-1]
    units = blocks[0].shape[2]
    copies = []
    for i, block in enumerate(blocks):
        start = pl.multiple_of((lax.axis_index("dp") ^ (i + 1)) * units, 128)
        for k, source in enumerate((expand_at, project_at)):
            copies.append(
                pltpu.make_async_copy(
                    source.at[:, pl.ds(start, units)], block.at[k], sems.at[2 * i + k]
                )
            )
    fetch(copies)


def turn_kernel(normed_ref, grad_ref, normed_turned_ref, grad_turned_ref):
    normed_turned_ref[...] = normed_ref[...].T
    grad_turned_ref[...] = grad_ref[...].T


def join_kernel(first_ref, second_ref, out_ref):
    count = first_ref.shape[0]
    out_ref[:count] = first_ref[...]
    out_ref[count:] = second_ref[...]


def order_kernel(
    sections, capacity, dp_steps, section_steps,
    me_ref, near_ref, far_ref, gain_ref, normed_ref, grad_ref, extra_ref,
):
    rows = normed_ref.shape[0]
    slots = sections * capacity
    half = near_ref.shape[0] * near_ref.shape[1]
    me_dp, me_section = me_ref[0], me_ref[1]
    column = lax.broadcasted_iota(jnp.int32, (8, half), 1)
    row = lax.broadcasted_iota(jnp.int32, (rows, half), 0)
    kind = column & (2 * slots - 1)
    slot = kind & (slots - 1)
    inputs = grad = None
    for side, ref in enumerate((near_ref, far_ref)):
        block = (column >> log2(2 * slots)) + side * (half // (2 * slots))
        source_dp = me_dp ^ masked_steps(block, dp_steps)
        source_section = me_section ^ masked_steps(block >> len(dp_steps), section_steps)
        patch_at = (source_dp * sections + source_section) * slots + slot
        grad_at = (
            (source_dp * sections + (slot >> log2(capacity))) * slots
            + source_section * capacity
            + (slot & (capacity - 1))
        )
        patch_at = jnp.where(kind < slots, patch_at, -1)[:1]
        grad_at = jnp.where(kind >= slots, grad_at, -1)[:1]
        values = ref[...].reshape(half, ref.shape[2])
        chosen = (row == patch_at).astype(jnp.float32).astype(jnp.bfloat16)
        found = jnp.dot(chosen, values, preferred_element_type=jnp.float32)
        inputs = found if inputs is None else inputs + found
        chosen = (row == grad_at).astype(jnp.float32).astype(jnp.bfloat16)
        found = jnp.dot(chosen, values, preferred_element_type=jnp.float32)
        grad = found if grad is None else grad + found
    inv_rms = lax.rsqrt(jnp.mean(inputs * inputs, axis=-1, keepdims=True) + 1e-06)
    normed_ref[...] = (inputs * inv_rms * gain_ref[...]).astype(jnp.bfloat16)
    grad = grad.astype(jnp.bfloat16)
    grad_ref[...] = grad
    mine = lax.broadcasted_iota(jnp.int32, (slots, rows), 0)
    every = lax.broadcasted_iota(jnp.int32, (slots, rows), 1)
    coming_at = (
        (me_dp * sections + (mine >> log2(capacity))) * slots
        + me_section * capacity
        + (mine & (capacity - 1))
    )
    own_at = (me_dp * sections + me_section) * slots + mine
    coming = jnp.dot(
        (every == coming_at).astype(jnp.float32).astype(jnp.bfloat16),
        inputs.astype(jnp.bfloat16),
        preferred_element_type=jnp.float32,
    )
    own = jnp.dot(
        (every == own_at).astype(jnp.float32).astype(jnp.bfloat16),
        grad,
        preferred_element_type=jnp.float32,
    )
    extra_ref[...] = jnp.concatenate([coming, own], axis=0)


def hidden_kernel(normed_ref, grad_ref, expand_at, project_at, *refs):
    blocks = refs[:-4]
    both_ref, expand_ref, project_ref, sems = refs[-4:]
    part = expand_at.shape[0]
    units = both_ref.shape[2]
    me = lax.axis_index("dp")
    copies = []
    for k, (source, whole) in enumerate(((expand_at, expand_ref), (project_at, project_ref))):
        own = source.at[:, pl.ds(pl.multiple_of(me * units, 128), units)]
        for i, block in enumerate((own, *(block.at[k] for block in blocks))):
            at = pl.ds(pl.multiple_of((me ^ i) * part, 8), part)
            copies.append(
                pltpu.make_async_copy(
                    block, whole.at[at, :], sems.at[k * (len(blocks) + 1) + i]
                )
            )
    fetch(copies)
    preact = jnp.dot(normed_ref[...], expand_ref[...], preferred_element_type=jnp.float32)
    activated, derivative = gelu_pair(preact)
    both_ref[0] = activated.astype(jnp.bfloat16)
    grad_hidden = jnp.dot(grad_ref[...], project_ref[...], preferred_element_type=jnp.float32)
    both_ref[1] = (grad_hidden * derivative).astype(jnp.bfloat16)


def share_kernel(
    sections, capacity, steps,
    me_ref, both_ref, expand_ref, project_ref, keep_ref, send_ref,
):
    rows = both_ref.shape[1]
    slots = sections * capacity
    row = lax.broadcasted_iota(jnp.int32, (rows, rows), 0)
    column = lax.broadcasted_iota(jnp.int32, (rows, rows), 1)
    inside = row & (slots - 1)
    replica = (row >> log2(slots)) & (rows // (sections * slots) - 1)
    away = row >> log2(rows // sections)
    goal = me_ref[1] ^ masked_steps(away, steps[::-1])
    base = replica * (slots * sections)
    mixed_from = (
        base + (inside >> log2(capacity)) * slots + goal * capacity + (inside & (capacity - 1))
    )
    normed_from = base + goal * slots + inside
    for k, (source, weight_ref) in enumerate(
        ((mixed_from, project_ref), (normed_from, expand_ref))
    ):
        turn = (column == source).astype(jnp.float32).astype(jnp.bfloat16)
        turned = jnp.dot(turn, both_ref[k], preferred_element_type=jnp.float32).astype(jnp.bfloat16)
        share = lax.dot_general(
            turned, weight_ref[...], (((1,), (1,)), ((), ())), preferred_element_type=jnp.float32
        )
        share = share.reshape(2, *keep_ref.shape[1:])
        keep_ref[k] = share[0]
        send_ref[k] = share[1].astype(jnp.bfloat16)


def halve_kernel(keep_ref, got_ref, next_keep_ref, next_send_ref):
    half = next_keep_ref.shape[1]
    total = keep_ref[...] + got_ref[...].astype(jnp.float32)
    next_keep_ref[...] = total[:, :half]
    next_send_ref[...] = total[:, half:].astype(jnp.bfloat16)


def address_kernel(keep_ref, got_ref, out_ref):
    total = keep_ref[...] + got_ref[...].astype(jnp.float32)
    for d in range(out_ref.shape[0]):
        out_ref[d] = jnp.concatenate([total[0, d], total[1, d]], axis=0).astype(jnp.bfloat16)


def weight_grad_kernel(distances, block_ref, rows_ref, *refs):
    out_at, result_ref, sems = refs[-3:]
    count, features, units = result_ref.shape
    piece = features // sems.shape[1]
    copies = []
    for i in range(count):
        result_ref[i] = jnp.dot(
            rows_ref[...], block_ref[i], preferred_element_type=jnp.float32
        ).astype(jnp.bfloat16)
        source = lax.axis_index("dp") ^ distances[i]
        columns = pl.ds(pl.multiple_of(source * units, 128), units)
        for k in range(sems.shape[1]):
            at = pl.ds(k * piece, piece)
            copies.append(
                pltpu.make_async_copy(
                    result_ref.at[i, at, :], out_at.at[at, columns], sems.at[i, k]
                )
            )
            copies[-1].start()
    for copy in copies:
        copy.wait()


def finish_kernel(
    capacity,
    me_ref, count_ref, place_ref, tail_ref, extra_ref, patch_ref, text_ref, gain_ref,
    embedded_ref, grad_rows_ref,
):
    slots = patch_ref.shape[0]
    total = tail_ref[0].astype(jnp.float32)
    for d in range(1, tail_ref.shape[0]):
        total += tail_ref[d].astype(jnp.float32)
    mixed, grad_normed = total[:slots], total[slots:]
    out_rows = (extra_ref[:slots, :] + mixed).astype(jnp.bfloat16)
    length = text_ref.shape[0]
    chooser = landing(place_ref, count_ref, me_ref[1], slots, capacity, length)
    contract = (((0,), (0,)), ((), ()))
    placed = lax.dot_general(
        chooser.astype(jnp.bfloat16), out_rows, contract, preferred_element_type=jnp.float32
    )
    taken = lax.dot_general(
        chooser.astype(jnp.bfloat16), jnp.ones((slots, 128), jnp.bfloat16),
        contract, preferred_element_type=jnp.float32,
    )[:, :1]
    embedded_ref[...] = jnp.where(
        taken > 0.5, placed, text_ref[...].astype(jnp.float32)
    ).astype(jnp.bfloat16)
    inputs = patch_ref[...].astype(jnp.float32)
    inv_rms = lax.rsqrt(jnp.mean(inputs * inputs, axis=-1, keepdims=True) + 1e-06)
    scaled_grad = grad_normed * gain_ref[...]
    centred = jnp.mean(scaled_grad * inputs, axis=-1, keepdims=True)
    grad_rows_ref[...] = (
        extra_ref[slots:, :] + inv_rms * scaled_grad - inputs * (inv_rms**3 * centred)
    ).astype(jnp.bfloat16)


def weight_grads(blocks, distances, values, width, before=()):
    count, rows, units = blocks.shape
    features = values.shape[0]
    pieces = 4 if features % 64 == 0 else 1
    anywhere = pl.BlockSpec(memory_space=pl.ANY)
    return pl.pallas_call(
        functools.partial(weight_grad_kernel, distances),
        in_specs=[VMEM_SPEC] * 2 + [anywhere] * len(before),
        out_specs=anywhere,
        out_shape=jax.ShapeDtypeStruct((features, width), jnp.bfloat16),
        scratch_shapes=[
            pltpu.VMEM((count, features, units), jnp.bfloat16),
            pltpu.SemaphoreType.DMA((count, pieces)),
        ],
        input_output_aliases={2: 0} if before else {},
        compiler_params=pltpu.CompilerParams(vmem_limit_bytes=12 << 20),
        cost_estimate=pl.CostEstimate(
            flops=2 * count * rows * features * units,
            bytes_accessed=2 * count * units * features + 2 * rows * features,
            transcendentals=0,
        ),
    )(blocks, values, *before)


def call(kernel, out_shape, smem, vmem, scratch=()):
    single = not isinstance(out_shape, (list, tuple))
    return pl.pallas_call(
        kernel,
        out_shape=out_shape,
        in_specs=[SMEM_SPEC] * len(smem) + [VMEM_SPEC] * len(vmem),
        out_specs=VMEM_SPEC if single else [VMEM_SPEC] * len(out_shape),
        scratch_shapes=scratch,
        compiler_params=pltpu.CompilerParams(vmem_limit_bytes=12 << 20),
    )(*smem, *vmem)


def join(first, second):
    both = (first.shape[0] + second.shape[0], *first.shape[1:])
    return call(join_kernel, jax.ShapeDtypeStruct(both, first.dtype), (), (first, second))


def join_pairs_kernel(first_ref, second_ref, hidden_ref, pre_ref):
    for k, out_ref in enumerate((hidden_ref, pre_ref)):
        out_ref[0] = first_ref[k]
        out_ref[1] = second_ref[k]


def join_pairs(first, second):
    out = jax.ShapeDtypeStruct(first.shape, first.dtype)
    return call(join_pairs_kernel, [out, out], (), (first, second))


def move_rows_plan(
    patches, gain, expand_weight, project_weight, counts, positions, text, cotangent
):
    sections = lax.axis_size("section")
    replicas = lax.axis_size("dp")
    devices = sections * replicas
    slots, features = patches.shape
    part, width = expand_weight.shape
    units = width // replicas
    capacity = slots // sections
    rows = devices * slots
    dp_steps, section_steps = bit_steps(replicas), bit_steps(sections)
    me = jnp.stack([lax.axis_index("dp"), lax.axis_index("section")]).astype(jnp.int32)
    gain = gain.reshape(1, features)
    project_turned = project_weight.T
    kept, wide = jnp.bfloat16, jnp.float32
    shape = jax.ShapeDtypeStruct

    hbm = pl.BlockSpec(memory_space=pltpu.HBM)

    def in_hbm(*arrays):
        return [pltpu.with_memory_space_constraint(array, pltpu.HBM) for array in arrays]

    held = pl.pallas_call(
        functools.partial(pick_kernel, capacity),
        out_shape=shape((1, 2 * slots, features), kept),
        in_specs=[hbm] * 4,
        out_specs=VMEM_SPEC,
        scratch_shapes=[
            pltpu.SMEM(counts.shape, counts.dtype),
            pltpu.SMEM(positions.shape, positions.dtype),
            pltpu.VMEM(patches.shape, kept),
            pltpu.VMEM(cotangent.shape, kept),
            pltpu.SemaphoreType.DMA((4,)),
        ],
        compiler_params=pltpu.CompilerParams(vmem_limit_bytes=12 << 20),
    )(*in_hbm(counts, positions, patches, cotangent))
    blocks = pl.pallas_call(
        repack_kernel,
        out_shape=[shape((2, part, units), kept)] * (replicas - 1),
        in_specs=[hbm] * 2,
        out_specs=[VMEM_SPEC] * (replicas - 1),
        scratch_shapes=[pltpu.SemaphoreType.DMA((2 * replicas - 2,))],
        compiler_params=pltpu.CompilerParams(vmem_limit_bytes=12 << 20),
    )(*in_hbm(expand_weight, project_turned))
    arrived = []
    for distance in range(1, replicas):
        arrived.append(swap(blocks[distance - 1], "dp", distance))

    exchanges = [("dp", step) for step in dp_steps] + [("section", step) for step in section_steps]
    for axis, step in exchanges:
        got = swap(held, axis, step)
        if held.shape[0] < devices // 2:
            held = join(held, got)
    normed, grad_all, extra = call(
        functools.partial(order_kernel, sections, capacity, dp_steps, section_steps),
        [shape((rows, features), kept), shape((rows, features), kept), shape((2 * slots, features), wide)],
        (me,), (held, got, gain),
    )

    normed_turned, grad_turned = call(
        turn_kernel, [shape((features, rows), kept)] * 2, (), (normed, grad_all)
    )
    both, expand_slice, project_slice = pl.pallas_call(
        hidden_kernel,
        out_shape=[shape((2, rows, units), kept)] + [shape((features, units), kept)] * 2,
        in_specs=[VMEM_SPEC] * 2 + [hbm] * 2 + [pl.BlockSpec(memory_space=pl.ANY)] * len(arrived),
        out_specs=[VMEM_SPEC] * 3,
        scratch_shapes=[pltpu.SemaphoreType.DMA((2 * replicas,))],
        compiler_params=pltpu.CompilerParams(vmem_limit_bytes=12 << 20),
    )(normed, grad_all, *in_hbm(expand_weight, project_turned), *arrived)

    tail_steps = section_steps[::-1]
    keep, send = call(
        functools.partial(share_kernel, sections, capacity, tail_steps),
        [shape((2, devices // 2, slots, features), kind) for kind in (wide, kept)],
        (me,), (both, expand_slice, project_slice),
    )
    for place, step in enumerate(tail_steps):
        got = swap(send, "section", step)
        if place < len(tail_steps) - 1:
            half = (2, send.shape[1] // 2, slots, features)
            keep, send = call(
                halve_kernel, [shape(half, wide), shape(half, kept)], (), (keep, got)
            )
    tail = call(address_kernel, shape((replicas, 2 * slots, features), kept), (), (keep, got))
    tail = lax.all_to_all(tail, "dp", split_axis=0, concat_axis=0, tiled=True)

    far_both = swap(both, "dp", dp_steps[0])
    pairs = join_pairs(both, far_both)
    grads = []
    for pair, values, steps in (
        (pairs[0], grad_turned, dp_steps[1:]), (pairs[1], normed_turned, dp_steps[:0:-1])
    ):
        held_pairs = {0: pair}
        for step in steps:
            for mask, array in list(held_pairs.items()):
                held_pairs[mask ^ step] = swap(array, "dp", step)
        grad = ()
        for mask, array in held_pairs.items():
            grad = (weight_grads(array, (mask, mask ^ dp_steps[0]), values, width, grad),)
        grads += grad
    project_grad, expand_grad = grads
    embedded, grad_rows = call(
        functools.partial(finish_kernel, capacity),
        [shape(text.shape, kept), shape(patches.shape, kept)],
        (me, counts, positions), (tail, extra, patches, text, gain),
    )
    return (embedded, grad_rows, expand_grad, project_grad.T)


def power_of_two(value):
    return value > 0 and value & (value - 1) == 0


def shards(patches, gain, expand_weight, project_weight, counts, positions, text, cotangent):
    replicas, sections = lax.axis_size("dp"), lax.axis_size("section")
    slots, features = patches.shape
    width = expand_weight.shape[1]
    rows = replicas * sections * slots
    fits = rows * (features + width) <= features * width
    even = (
        all(power_of_two(n) for n in (replicas, sections, slots))
        and replicas > 2
        and sections > 1
        and slots % 8 == 0
        and width % (128 * replicas) == 0
    )
    if fits and even:
        plan = move_rows_plan
    else:
        plan = gather_weights_plan
    return plan(
        patches, gain, expand_weight, project_weight, counts, positions, text, cotangent
    )


def solution(mesh):
    return jax.shard_map(
        shards,
        mesh=mesh,
        in_specs=(
            P(("dp", "section"), None),
            P(),
            P("dp", "section"),
            P("section", "dp"),
            P("dp", None),
            P(("dp", "section"), None),
            P(("dp", "section"), None),
            P(("dp", "section"), None),
        ),
        out_specs=(
            P(("dp", "section"), None),
            P(("dp", "section"), None),
            P(None, "section"),
            P("section", None),
        ),
        check_vma=False,
    )
```

```python
import functools

import jax
import jax.numpy as jnp
from jax import lax
from jax.experimental import pallas as pl
from jax.experimental.pallas import tpu as pltpu
from jax.sharding import PartitionSpec as P


def gelu_pair(values):
    coeff = 0.7978845608
    inner = coeff * (values + 0.044715 * values * values * values)
    tangent = jnp.tanh(inner)
    activated = 0.5 * values * (1.0 + tangent)
    derivative = 0.5 * (1.0 + tangent) + 0.5 * values * (1.0 - tangent * tangent) * coeff * (
        1.0 + 3.0 * 0.044715 * values * values
    )
    return (activated, derivative)


def gather_weights_plan(
    patches, gain, expand_weight, project_weight, counts, positions, text, cotangent
):
    sections = lax.axis_size("section")
    slot_count = patches.shape[0]
    features = patches.shape[1]
    capacity = slot_count // sections
    inputs = patches.astype(jnp.float32)
    inv_rms = lax.rsqrt(jnp.mean(inputs * inputs, axis=-1, keepdims=True) + 1e-06)
    normed = (inputs * inv_rms * gain).astype(jnp.bfloat16)
    gathered = lax.all_gather(normed, "section", axis=0, tiled=True)
    expand_full, project_full = (
        lax.all_gather(expand_weight, "dp", axis=0, tiled=True),
        lax.all_gather(project_weight, "dp", axis=1, tiled=True),
    )
    preact = jnp.dot(gathered, expand_full, preferred_element_type=jnp.float32)
    activated, derivative = gelu_pair(preact)
    hidden = activated.astype(jnp.bfloat16)
    row_block = hidden
    mixed = lax.psum_scatter(
        jnp.dot(row_block, project_full, preferred_element_type=jnp.float32).astype(jnp.bfloat16),
        "section",
        scatter_dimension=0,
        tiled=True,
    ).astype(jnp.float32)
    out_rows = (inputs + mixed).astype(jnp.bfloat16)
    arrived = lax.all_to_all(out_rows, "section", split_axis=0, concat_axis=0, tiled=True)
    section_id = lax.axis_index("section")
    arrival = jnp.arange(slot_count, dtype=jnp.int32)
    source = arrival // capacity
    slot_index = section_id * capacity + arrival % capacity
    is_live = (slot_index < counts[0][source])[:, None]
    targets = positions[0]
    current = text[targets]
    embedded = text.at[targets].set(jnp.where(is_live, arrived, current))
    picked = jnp.where(is_live, cotangent[targets], jnp.zeros_like(current))
    collected = lax.all_gather(picked, "section", axis=0, tiled=True)
    grad_all = (
        collected.reshape(sections, sections, capacity, features)
        .transpose(1, 0, 2, 3)
        .reshape(sections * slot_count, features)
    )
    returned = lax.dynamic_slice_in_dim(grad_all, section_id * slot_count, slot_count, 0)
    grad_own = returned.astype(jnp.float32)
    project_local = lax.dot_general(
        hidden, grad_all, (((0,), (0,)), ((), ())), preferred_element_type=jnp.float32
    )
    grad_hidden = lax.dot_general(
        grad_all, project_full, (((1,), (1,)), ((), ())), preferred_element_type=jnp.float32
    )
    grad_pre = (grad_hidden * derivative).astype(jnp.bfloat16)
    row_block = grad_pre
    grad_normed = lax.psum_scatter(
        lax.dot_general(
            row_block, expand_full, (((1,), (1,)), ((), ())), preferred_element_type=jnp.float32
        ).astype(jnp.bfloat16),
        "section",
        scatter_dimension=0,
        tiled=True,
    ).astype(jnp.float32)
    expand_local = lax.dot_general(
        gathered, grad_pre, (((0,), (0,)), ((), ())), preferred_element_type=jnp.float32
    )
    project_total, expand_total = (
        lax.psum(project_local.astype(jnp.bfloat16), "dp").astype(jnp.float32),
        lax.psum(expand_local.astype(jnp.bfloat16), "dp").astype(jnp.float32),
    )
    scaled_grad = grad_normed * gain
    centred = jnp.mean(scaled_grad * inputs, axis=-1, keepdims=True)
    grad_rows = (grad_own + inv_rms * scaled_grad - inputs * inv_rms**3 * centred).astype(
        jnp.bfloat16
    )
    return (
        embedded,
        grad_rows,
        expand_total.astype(jnp.bfloat16),
        project_total.astype(jnp.bfloat16),
    )


def bit_steps(size):
    steps = []
    step = size // 2
    while step >= 1:
        steps.append(step)
        step //= 2
    return steps


def swap(array, axis, step):
    size = lax.axis_size(axis)
    return lax.ppermute(array, axis, [(i, i ^ step) for i in range(size)])


def masked_steps(index, steps):
    mask = 0
    for place, step in enumerate(steps):
        mask = mask + ((index >> place) & 1) * step
    return mask


VMEM_SPEC = pl.BlockSpec(memory_space=pltpu.VMEM)
SMEM_SPEC = pl.BlockSpec(memory_space=pltpu.SMEM)


def log2(value):
    return value.bit_length() - 1


def landing(place_ref, count_ref, section, slots, capacity, length):
    row = lax.broadcasted_iota(jnp.int32, (slots, length), 0)
    column = lax.broadcasted_iota(jnp.int32, (slots, length), 1)
    spot = jnp.full((slots, length), -1, jnp.int32)
    for q in range(slots):
        live = section * capacity + q % capacity < count_ref[0, q // capacity]
        spot = jnp.where(row == q, jnp.where(live, place_ref[0, q], -1), spot)
    return (spot == column).astype(jnp.float32)


def fetch(copies):
    for copy in copies:
        copy.start()
    for copy in copies:
        copy.wait()


def pick_kernel(
    capacity, counts_at, places_at, patches_at, cotangent_at, pair_ref,
    count_ref, place_ref, patch_ref, cotangent_ref, sems,
):
    ends = (
        (counts_at, count_ref), (places_at, place_ref),
        (patches_at, patch_ref), (cotangent_at, cotangent_ref),
    )
    fetch([pltpu.make_async_copy(a, b, sems.at[i]) for i, (a, b) in enumerate(ends)])
    slots = patch_ref.shape[0]
    section = lax.axis_index("section")
    chooser = landing(
        place_ref, count_ref, section, slots, capacity, cotangent_ref.shape[0]
    ).astype(jnp.bfloat16)
    picked = jnp.dot(chooser, cotangent_ref[...], preferred_element_type=jnp.float32)
    pair_ref[0] = jnp.concatenate(
        [patch_ref[...].astype(jnp.float32), picked], axis=0
    ).astype(jnp.bfloat16)


def repack_kernel(expand_at, project_at, *refs):
    blocks, sems = refs[:-1], refs[-1]
    units = blocks[0].shape[2]
    copies = []
    for i, block in enumerate(blocks):
        start = pl.multiple_of((lax.axis_index("dp") ^ (i + 1)) * units, 128)
        for k, source in enumerate((expand_at, project_at)):
            copies.append(
                pltpu.make_async_copy(
                    source.at[:, pl.ds(start, units)], block.at[k], sems.at[2 * i + k]
                )
            )
    fetch(copies)


def turn_kernel(normed_ref, grad_ref, normed_turned_ref, grad_turned_ref):
    normed_turned_ref[...] = normed_ref[...].T
    grad_turned_ref[...] = grad_ref[...].T


def join_kernel(first_ref, second_ref, out_ref):
    count = first_ref.shape[0]
    out_ref[:count] = first_ref[...]
    out_ref[count:] = second_ref[...]


def order_kernel(
    sections, capacity, dp_steps, section_steps,
    me_ref, near_ref, far_ref, gain_ref, normed_ref, grad_ref, extra_ref,
):
    rows = normed_ref.shape[0]
    slots = sections * capacity
    half = near_ref.shape[0] * near_ref.shape[1]
    me_dp, me_section = me_ref[0], me_ref[1]
    column = lax.broadcasted_iota(jnp.int32, (8, half), 1)
    row = lax.broadcasted_iota(jnp.int32, (rows, half), 0)
    kind = column & (2 * slots - 1)
    slot = kind & (slots - 1)
    inputs = grad = None
    for side, ref in enumerate((near_ref, far_ref)):
        block = (column >> log2(2 * slots)) + side * (half // (2 * slots))
        source_dp = me_dp ^ masked_steps(block, dp_steps)
        source_section = me_section ^ masked_steps(block >> len(dp_steps), section_steps)
        patch_at = (source_dp * sections + source_section) * slots + slot
        grad_at = (
            (source_dp * sections + (slot >> log2(capacity))) * slots
            + source_section * capacity
            + (slot & (capacity - 1))
        )
        patch_at = jnp.where(kind < slots, patch_at, -1)[:1]
        grad_at = jnp.where(kind >= slots, grad_at, -1)[:1]
        values = ref[...].reshape(half, ref.shape[2])
        chosen = (row == patch_at).astype(jnp.float32).astype(jnp.bfloat16)
        found = jnp.dot(chosen, values, preferred_element_type=jnp.float32)
        inputs = found if inputs is None else inputs + found
        chosen = (row == grad_at).astype(jnp.float32).astype(jnp.bfloat16)
        found = jnp.dot(chosen, values, preferred_element_type=jnp.float32)
        grad = found if grad is None else grad + found
    inv_rms = lax.rsqrt(jnp.mean(inputs * inputs, axis=-1, keepdims=True) + 1e-06)
    normed_ref[...] = (inputs * inv_rms * gain_ref[...]).astype(jnp.bfloat16)
    grad = grad.astype(jnp.bfloat16)
    grad_ref[...] = grad
    mine = lax.broadcasted_iota(jnp.int32, (slots, rows), 0)
    every = lax.broadcasted_iota(jnp.int32, (slots, rows), 1)
    coming_at = (
        (me_dp * sections + (mine >> log2(capacity))) * slots
        + me_section * capacity
        + (mine & (capacity - 1))
    )
    own_at = (me_dp * sections + me_section) * slots + mine
    coming = jnp.dot(
        (every == coming_at).astype(jnp.float32).astype(jnp.bfloat16),
        inputs.astype(jnp.bfloat16),
        preferred_element_type=jnp.float32,
    )
    own = jnp.dot(
        (every == own_at).astype(jnp.float32).astype(jnp.bfloat16),
        grad,
        preferred_element_type=jnp.float32,
    )
    extra_ref[...] = jnp.concatenate([coming, own], axis=0)


def hidden_kernel(normed_ref, grad_ref, expand_at, project_at, *refs):
    blocks = refs[:-4]
    both_ref, expand_ref, project_ref, sems = refs[-4:]
    part = expand_at.shape[0]
    units = both_ref.shape[2]
    me = lax.axis_index("dp")
    copies = []
    for k, (source, whole) in enumerate(((expand_at, expand_ref), (project_at, project_ref))):
        own = source.at[:, pl.ds(pl.multiple_of(me * units, 128), units)]
        for i, block in enumerate((own, *(block.at[k] for block in blocks))):
            at = pl.ds(pl.multiple_of((me ^ i) * part, 8), part)
            copies.append(
                pltpu.make_async_copy(
                    block, whole.at[at, :], sems.at[k * (len(blocks) + 1) + i]
                )
            )
    fetch(copies)
    preact = jnp.dot(normed_ref[...], expand_ref[...], preferred_element_type=jnp.float32)
    activated, derivative = gelu_pair(preact)
    both_ref[0] = activated.astype(jnp.bfloat16)
    grad_hidden = jnp.dot(grad_ref[...], project_ref[...], preferred_element_type=jnp.float32)
    both_ref[1] = (grad_hidden * derivative).astype(jnp.bfloat16)


def share_kernel(
    sections, capacity, steps,
    me_ref, both_ref, expand_ref, project_ref, keep_ref, send_ref,
):
    rows = both_ref.shape[1]
    slots = sections * capacity
    row = lax.broadcasted_iota(jnp.int32, (rows, rows), 0)
    column = lax.broadcasted_iota(jnp.int32, (rows, rows), 1)
    inside = row & (slots - 1)
    replica = (row >> log2(slots)) & (rows // (sections * slots) - 1)
    away = row >> log2(rows // sections)
    goal = me_ref[1] ^ masked_steps(away, steps[::-1])
    base = replica * (slots * sections)
    mixed_from = (
        base + (inside >> log2(capacity)) * slots + goal * capacity + (inside & (capacity - 1))
    )
    normed_from = base + goal * slots + inside
    for k, (source, weight_ref) in enumerate(
        ((mixed_from, project_ref), (normed_from, expand_ref))
    ):
        turn = (column == source).astype(jnp.float32).astype(jnp.bfloat16)
        turned = jnp.dot(turn, both_ref[k], preferred_element_type=jnp.float32).astype(jnp.bfloat16)
        share = lax.dot_general(
            turned, weight_ref[...], (((1,), (1,)), ((), ())), preferred_element_type=jnp.float32
        )
        share = share.reshape(2, *keep_ref.shape[1:])
        keep_ref[k] = share[0]
        send_ref[k] = share[1].astype(jnp.bfloat16)


def halve_kernel(keep_ref, got_ref, next_keep_ref, next_send_ref):
    half = next_keep_ref.shape[1]
    total = keep_ref[...] + got_ref[...].astype(jnp.float32)
    next_keep_ref[...] = total[:, :half]
    next_send_ref[...] = total[:, half:].astype(jnp.bfloat16)


def address_kernel(keep_ref, got_ref, out_ref):
    total = keep_ref[...] + got_ref[...].astype(jnp.float32)
    for d in range(out_ref.shape[0]):
        out_ref[d] = jnp.concatenate([total[0, d], total[1, d]], axis=0).astype(jnp.bfloat16)


def weight_grad_kernel(
    hidden_distances, pre_distances, hidden_ref, pre_ref, grad_ref, normed_ref, *refs
):
    project_at, expand_at, result_ref, sems = refs[-4:]
    _, count, features, units = result_ref.shape
    pieces = sems.shape[2]
    piece = features // pieces
    copies = []
    for i in range(count):
        for k, (block_ref, rows_ref, out_at, distances) in enumerate(
            (
                (pre_ref, normed_ref, expand_at, pre_distances),
                (hidden_ref, grad_ref, project_at, hidden_distances),
            )
        ):
            result_ref[k, i] = jnp.dot(
                rows_ref[...], block_ref[i], preferred_element_type=jnp.float32
            ).astype(jnp.bfloat16)
            source = lax.axis_index("dp") ^ distances[i]
            columns = pl.ds(pl.multiple_of(source * units, 128), units)
            for j in range(pieces):
                at = pl.ds(j * piece, piece)
                copies.append(
                    pltpu.make_async_copy(
                        result_ref.at[k, i, at, :], out_at.at[at, columns], sems.at[k, i, j]
                    )
                )
                copies[-1].start()
    for copy in copies:
        copy.wait()


def finish_kernel(
    capacity,
    me_ref, count_ref, place_ref, tail_ref, extra_ref, patch_ref, text_ref, gain_ref,
    embedded_ref, grad_rows_ref,
):
    slots = patch_ref.shape[0]
    total = tail_ref[0].astype(jnp.float32)
    for d in range(1, tail_ref.shape[0]):
        total += tail_ref[d].astype(jnp.float32)
    mixed, grad_normed = total[:slots], total[slots:]
    out_rows = (extra_ref[:slots, :] + mixed).astype(jnp.bfloat16)
    length = text_ref.shape[0]
    chooser = landing(place_ref, count_ref, me_ref[1], slots, capacity, length)
    contract = (((0,), (0,)), ((), ()))
    placed = lax.dot_general(
        chooser.astype(jnp.bfloat16), out_rows, contract, preferred_element_type=jnp.float32
    )
    taken = lax.dot_general(
        chooser.astype(jnp.bfloat16), jnp.ones((slots, 128), jnp.bfloat16),
        contract, preferred_element_type=jnp.float32,
    )[:, :1]
    embedded_ref[...] = jnp.where(
        taken > 0.5, placed, text_ref[...].astype(jnp.float32)
    ).astype(jnp.bfloat16)
    inputs = patch_ref[...].astype(jnp.float32)
    inv_rms = lax.rsqrt(jnp.mean(inputs * inputs, axis=-1, keepdims=True) + 1e-06)
    scaled_grad = grad_normed * gain_ref[...]
    centred = jnp.mean(scaled_grad * inputs, axis=-1, keepdims=True)
    grad_rows_ref[...] = (
        extra_ref[slots:, :] + inv_rms * scaled_grad - inputs * (inv_rms**3 * centred)
    ).astype(jnp.bfloat16)


def weight_grads(
    hidden, hidden_distances, pre, pre_distances, grad_turned, normed_turned, width, before
):
    count, rows, units = hidden.shape
    features = grad_turned.shape[0]
    pieces = 2 if features % 32 == 0 else 1
    anywhere = pl.BlockSpec(memory_space=pl.ANY)
    return pl.pallas_call(
        functools.partial(weight_grad_kernel, hidden_distances, pre_distances),
        in_specs=[VMEM_SPEC] * 4 + [anywhere] * len(before),
        out_specs=[anywhere] * 2,
        out_shape=[jax.ShapeDtypeStruct((features, width), jnp.bfloat16)] * 2,
        scratch_shapes=[
            pltpu.VMEM((2, count, features, units), jnp.bfloat16),
            pltpu.SemaphoreType.DMA((2, count, pieces)),
        ],
        input_output_aliases={4: 0, 5: 1} if before else {},
        compiler_params=pltpu.CompilerParams(vmem_limit_bytes=12 << 20),
        cost_estimate=pl.CostEstimate(
            flops=4 * count * rows * features * units,
            bytes_accessed=4 * count * units * features + 4 * rows * features,
            transcendentals=0,
        ),
    )(hidden, pre, grad_turned, normed_turned, *before)


def call(kernel, out_shape, smem, vmem, scratch=()):
    single = not isinstance(out_shape, (list, tuple))
    return pl.pallas_call(
        kernel,
        out_shape=out_shape,
        in_specs=[SMEM_SPEC] * len(smem) + [VMEM_SPEC] * len(vmem),
        out_specs=VMEM_SPEC if single else [VMEM_SPEC] * len(out_shape),
        scratch_shapes=scratch,
        compiler_params=pltpu.CompilerParams(vmem_limit_bytes=12 << 20),
    )(*smem, *vmem)


def join(first, second):
    both = (first.shape[0] + second.shape[0], *first.shape[1:])
    return call(join_kernel, jax.ShapeDtypeStruct(both, first.dtype), (), (first, second))


def join_pairs_kernel(first_ref, second_ref, hidden_ref, pre_ref):
    for k, out_ref in enumerate((hidden_ref, pre_ref)):
        out_ref[0] = first_ref[k]
        out_ref[1] = second_ref[k]


def join_pairs(first, second):
    out = jax.ShapeDtypeStruct(first.shape, first.dtype)
    return call(join_pairs_kernel, [out, out], (), (first, second))


def move_rows_plan(
    patches, gain, expand_weight, project_weight, counts, positions, text, cotangent
):
    sections = lax.axis_size("section")
    replicas = lax.axis_size("dp")
    devices = sections * replicas
    slots, features = patches.shape
    part, width = expand_weight.shape
    units = width // replicas
    capacity = slots // sections
    rows = devices * slots
    dp_steps, section_steps = bit_steps(replicas), bit_steps(sections)
    me = jnp.stack([lax.axis_index("dp"), lax.axis_index("section")]).astype(jnp.int32)
    gain = gain.reshape(1, features)
    project_turned = project_weight.T
    kept, wide = jnp.bfloat16, jnp.float32
    shape = jax.ShapeDtypeStruct

    hbm = pl.BlockSpec(memory_space=pltpu.HBM)

    def in_hbm(*arrays):
        return [pltpu.with_memory_space_constraint(array, pltpu.HBM) for array in arrays]

    held = pl.pallas_call(
        functools.partial(pick_kernel, capacity),
        out_shape=shape((1, 2 * slots, features), kept),
        in_specs=[hbm] * 4,
        out_specs=VMEM_SPEC,
        scratch_shapes=[
            pltpu.SMEM(counts.shape, counts.dtype),
            pltpu.SMEM(positions.shape, positions.dtype),
            pltpu.VMEM(patches.shape, kept),
            pltpu.VMEM(cotangent.shape, kept),
            pltpu.SemaphoreType.DMA((4,)),
        ],
        compiler_params=pltpu.CompilerParams(vmem_limit_bytes=12 << 20),
    )(*in_hbm(counts, positions, patches, cotangent))
    blocks = pl.pallas_call(
        repack_kernel,
        out_shape=[shape((2, part, units), kept)] * (replicas - 1),
        in_specs=[hbm] * 2,
        out_specs=[VMEM_SPEC] * (replicas - 1),
        scratch_shapes=[pltpu.SemaphoreType.DMA((2 * replicas - 2,))],
        compiler_params=pltpu.CompilerParams(vmem_limit_bytes=12 << 20),
    )(*in_hbm(expand_weight, project_turned))
    arrived = []
    for distance in range(1, replicas):
        arrived.append(swap(blocks[distance - 1], "dp", distance))

    exchanges = [("dp", step) for step in dp_steps] + [("section", step) for step in section_steps]
    for axis, step in exchanges:
        got = swap(held, axis, step)
        if held.shape[0] < devices // 2:
            held = join(held, got)
    normed, grad_all, extra = call(
        functools.partial(order_kernel, sections, capacity, dp_steps, section_steps),
        [shape((rows, features), kept), shape((rows, features), kept), shape((2 * slots, features), wide)],
        (me,), (held, got, gain),
    )

    normed_turned, grad_turned = call(
        turn_kernel, [shape((features, rows), kept)] * 2, (), (normed, grad_all)
    )
    both, expand_slice, project_slice = pl.pallas_call(
        hidden_kernel,
        out_shape=[shape((2, rows, units), kept)] + [shape((features, units), kept)] * 2,
        in_specs=[VMEM_SPEC] * 2 + [hbm] * 2 + [pl.BlockSpec(memory_space=pl.ANY)] * len(arrived),
        out_specs=[VMEM_SPEC] * 3,
        scratch_shapes=[pltpu.SemaphoreType.DMA((2 * replicas,))],
        compiler_params=pltpu.CompilerParams(vmem_limit_bytes=12 << 20),
    )(normed, grad_all, *in_hbm(expand_weight, project_turned), *arrived)

    tail_steps = section_steps[::-1]
    keep, send = call(
        functools.partial(share_kernel, sections, capacity, tail_steps),
        [shape((2, devices // 2, slots, features), kind) for kind in (wide, kept)],
        (me,), (both, expand_slice, project_slice),
    )
    for place, step in enumerate(tail_steps):
        got = swap(send, "section", step)
        if place < len(tail_steps) - 1:
            half = (2, send.shape[1] // 2, slots, features)
            keep, send = call(
                halve_kernel, [shape(half, wide), shape(half, kept)], (), (keep, got)
            )
    tail = call(address_kernel, shape((replicas, 2 * slots, features), kept), (), (keep, got))
    tail = lax.all_to_all(tail, "dp", split_axis=0, concat_axis=0, tiled=True)

    far_both = swap(both, "dp", dp_steps[0])
    pairs = join_pairs(both, far_both)
    gathered = []
    for pair, steps in ((pairs[0], dp_steps[1:]), (pairs[1], dp_steps[:0:-1])):
        held_pairs = {0: pair}
        for step in steps:
            for mask, array in list(held_pairs.items()):
                held_pairs[mask ^ step] = swap(array, "dp", step)
        gathered.append(held_pairs.items())
    grads = ()
    for (hidden_mask, hidden), (pre_mask, pre) in zip(*gathered):
        far = dp_steps[0]
        grads = weight_grads(
            hidden, (hidden_mask, hidden_mask ^ far), pre, (pre_mask, pre_mask ^ far),
            grad_turned, normed_turned, width, grads,
        )
    project_grad, expand_grad = grads
    embedded, grad_rows = call(
        functools.partial(finish_kernel, capacity),
        [shape(text.shape, kept), shape(patches.shape, kept)],
        (me, counts, positions), (tail, extra, patches, text, gain),
    )
    return (embedded, grad_rows, expand_grad, project_grad.T)


def power_of_two(value):
    return value > 0 and value & (value - 1) == 0


def shards(patches, gain, expand_weight, project_weight, counts, positions, text, cotangent):
    replicas, sections = lax.axis_size("dp"), lax.axis_size("section")
    slots, features = patches.shape
    width = expand_weight.shape[1]
    rows = replicas * sections * slots
    fits = rows * (features + width) <= features * width
    even = (
        all(power_of_two(n) for n in (replicas, sections, slots))
        and replicas > 2
        and sections > 1
        and slots % 8 == 0
        and width % (128 * replicas) == 0
    )
    if fits and even:
        plan = move_rows_plan
    else:
        plan = gather_weights_plan
    return plan(
        patches, gain, expand_weight, project_weight, counts, positions, text, cotangent
    )


def solution(mesh):
    return jax.shard_map(
        shards,
        mesh=mesh,
        in_specs=(
            P(("dp", "section"), None),
            P(),
            P("dp", "section"),
            P("section", "dp"),
            P("dp", None),
            P(("dp", "section"), None),
            P(("dp", "section"), None),
            P(("dp", "section"), None),
        ),
        out_specs=(
            P(("dp", "section"), None),
            P(("dp", "section"), None),
            P(None, "section"),
            P("section", None),
        ),
        check_vma=False,
    )
```

```python
import functools

import jax
import jax.numpy as jnp
from jax import lax
from jax.experimental import pallas as pl
from jax.experimental.pallas import tpu as pltpu
from jax.sharding import PartitionSpec as P


def gelu_pair(values):
    coeff = 0.7978845608
    inner = coeff * (values + 0.044715 * values * values * values)
    tangent = jnp.tanh(inner)
    activated = 0.5 * values * (1.0 + tangent)
    derivative = 0.5 * (1.0 + tangent) + 0.5 * values * (1.0 - tangent * tangent) * coeff * (
        1.0 + 3.0 * 0.044715 * values * values
    )
    return (activated, derivative)


def gather_weights_plan(
    patches, gain, expand_weight, project_weight, counts, positions, text, cotangent
):
    sections = lax.axis_size("section")
    slot_count = patches.shape[0]
    features = patches.shape[1]
    capacity = slot_count // sections
    inputs = patches.astype(jnp.float32)
    inv_rms = lax.rsqrt(jnp.mean(inputs * inputs, axis=-1, keepdims=True) + 1e-06)
    normed = (inputs * inv_rms * gain).astype(jnp.bfloat16)
    gathered = lax.all_gather(normed, "section", axis=0, tiled=True)
    expand_full, project_full = (
        lax.all_gather(expand_weight, "dp", axis=0, tiled=True),
        lax.all_gather(project_weight, "dp", axis=1, tiled=True),
    )
    preact = jnp.dot(gathered, expand_full, preferred_element_type=jnp.float32)
    activated, derivative = gelu_pair(preact)
    hidden = activated.astype(jnp.bfloat16)
    row_block = hidden
    mixed = lax.psum_scatter(
        jnp.dot(row_block, project_full, preferred_element_type=jnp.float32).astype(jnp.bfloat16),
        "section",
        scatter_dimension=0,
        tiled=True,
    ).astype(jnp.float32)
    out_rows = (inputs + mixed).astype(jnp.bfloat16)
    arrived = lax.all_to_all(out_rows, "section", split_axis=0, concat_axis=0, tiled=True)
    section_id = lax.axis_index("section")
    arrival = jnp.arange(slot_count, dtype=jnp.int32)
    source = arrival // capacity
    slot_index = section_id * capacity + arrival % capacity
    is_live = (slot_index < counts[0][source])[:, None]
    targets = positions[0]
    current = text[targets]
    embedded = text.at[targets].set(jnp.where(is_live, arrived, current))
    picked = jnp.where(is_live, cotangent[targets], jnp.zeros_like(current))
    collected = lax.all_gather(picked, "section", axis=0, tiled=True)
    grad_all = (
        collected.reshape(sections, sections, capacity, features)
        .transpose(1, 0, 2, 3)
        .reshape(sections * slot_count, features)
    )
    returned = lax.dynamic_slice_in_dim(grad_all, section_id * slot_count, slot_count, 0)
    grad_own = returned.astype(jnp.float32)
    project_local = lax.dot_general(
        hidden, grad_all, (((0,), (0,)), ((), ())), preferred_element_type=jnp.float32
    )
    grad_hidden = lax.dot_general(
        grad_all, project_full, (((1,), (1,)), ((), ())), preferred_element_type=jnp.float32
    )
    grad_pre = (grad_hidden * derivative).astype(jnp.bfloat16)
    row_block = grad_pre
    grad_normed = lax.psum_scatter(
        lax.dot_general(
            row_block, expand_full, (((1,), (1,)), ((), ())), preferred_element_type=jnp.float32
        ).astype(jnp.bfloat16),
        "section",
        scatter_dimension=0,
        tiled=True,
    ).astype(jnp.float32)
    expand_local = lax.dot_general(
        gathered, grad_pre, (((0,), (0,)), ((), ())), preferred_element_type=jnp.float32
    )
    project_total, expand_total = (
        lax.psum(project_local.astype(jnp.bfloat16), "dp").astype(jnp.float32),
        lax.psum(expand_local.astype(jnp.bfloat16), "dp").astype(jnp.float32),
    )
    scaled_grad = grad_normed * gain
    centred = jnp.mean(scaled_grad * inputs, axis=-1, keepdims=True)
    grad_rows = (grad_own + inv_rms * scaled_grad - inputs * inv_rms**3 * centred).astype(
        jnp.bfloat16
    )
    return (
        embedded,
        grad_rows,
        expand_total.astype(jnp.bfloat16),
        project_total.astype(jnp.bfloat16),
    )


def bit_steps(size):
    steps = []
    step = size // 2
    while step >= 1:
        steps.append(step)
        step //= 2
    return steps


def swap(array, axis, step):
    size = lax.axis_size(axis)
    return lax.ppermute(array, axis, [(i, i ^ step) for i in range(size)])


def masked_steps(index, steps):
    mask = 0
    for place, step in enumerate(steps):
        mask = mask + ((index >> place) & 1) * step
    return mask


VMEM_SPEC = pl.BlockSpec(memory_space=pltpu.VMEM)
SMEM_SPEC = pl.BlockSpec(memory_space=pltpu.SMEM)


def log2(value):
    return value.bit_length() - 1


def landing(place_ref, count_ref, section, slots, capacity, length):
    row = lax.broadcasted_iota(jnp.int32, (slots, length), 0)
    column = lax.broadcasted_iota(jnp.int32, (slots, length), 1)
    spot = jnp.full((slots, length), -1, jnp.int32)
    for q in range(slots):
        live = section * capacity + q % capacity < count_ref[0, q // capacity]
        spot = jnp.where(row == q, jnp.where(live, place_ref[0, q], -1), spot)
    return (spot == column).astype(jnp.float32)


def fetch(copies):
    for copy in copies:
        copy.start()
    for copy in copies:
        copy.wait()


def pick_kernel(
    capacity, counts_at, places_at, patches_at, cotangent_at, pair_ref,
    count_ref, place_ref, patch_ref, cotangent_ref, sems,
):
    ends = (
        (counts_at, count_ref), (places_at, place_ref),
        (patches_at, patch_ref), (cotangent_at, cotangent_ref),
    )
    fetch([pltpu.make_async_copy(a, b, sems.at[i]) for i, (a, b) in enumerate(ends)])
    slots = patch_ref.shape[0]
    section = lax.axis_index("section")
    chooser = landing(
        place_ref, count_ref, section, slots, capacity, cotangent_ref.shape[0]
    ).astype(jnp.bfloat16)
    picked = jnp.dot(chooser, cotangent_ref[...], preferred_element_type=jnp.float32)
    pair_ref[0] = jnp.concatenate(
        [patch_ref[...].astype(jnp.float32), picked], axis=0
    ).astype(jnp.bfloat16)


def repack_kernel(expand_at, project_at, *refs):
    blocks, sems = refs[:-1], refs[-1]
    units = blocks[0].shape[2]
    copies = []
    for i, block in enumerate(blocks):
        start = pl.multiple_of((lax.axis_index("dp") ^ (i + 1)) * units, 128)
        for k, source in enumerate((expand_at, project_at)):
            copies.append(
                pltpu.make_async_copy(
                    source.at[:, pl.ds(start, units)], block.at[k], sems.at[2 * i + k]
                )
            )
    fetch(copies)


def turn_kernel(normed_ref, grad_ref, normed_turned_ref, grad_turned_ref):
    normed_turned_ref[...] = normed_ref[...].T
    grad_turned_ref[...] = grad_ref[...].T


def join_kernel(first_ref, second_ref, out_ref):
    count = first_ref.shape[0]
    out_ref[:count] = first_ref[...]
    out_ref[count:] = second_ref[...]


def order_kernel(
    sections, capacity, dp_steps, section_steps,
    me_ref, near_ref, far_ref, gain_ref, normed_ref, grad_ref, extra_ref,
):
    rows = normed_ref.shape[0]
    slots = sections * capacity
    half = near_ref.shape[0] * near_ref.shape[1]
    me_dp, me_section = me_ref[0], me_ref[1]
    column = lax.broadcasted_iota(jnp.int32, (8, half), 1)
    row = lax.broadcasted_iota(jnp.int32, (rows, half), 0)
    kind = column & (2 * slots - 1)
    slot = kind & (slots - 1)
    inputs = grad = None
    for side, ref in enumerate((near_ref, far_ref)):
        block = (column >> log2(2 * slots)) + side * (half // (2 * slots))
        source_dp = me_dp ^ masked_steps(block, dp_steps)
        source_section = me_section ^ masked_steps(block >> len(dp_steps), section_steps)
        patch_at = (source_dp * sections + source_section) * slots + slot
        grad_at = (
            (source_dp * sections + (slot >> log2(capacity))) * slots
            + source_section * capacity
            + (slot & (capacity - 1))
        )
        patch_at = jnp.where(kind < slots, patch_at, -1)[:1]
        grad_at = jnp.where(kind >= slots, grad_at, -1)[:1]
        values = ref[...].reshape(half, ref.shape[2])
        chosen = (row == patch_at).astype(jnp.float32).astype(jnp.bfloat16)
        found = jnp.dot(chosen, values, preferred_element_type=jnp.float32)
        inputs = found if inputs is None else inputs + found
        chosen = (row == grad_at).astype(jnp.float32).astype(jnp.bfloat16)
        found = jnp.dot(chosen, values, preferred_element_type=jnp.float32)
        grad = found if grad is None else grad + found
    inv_rms = lax.rsqrt(jnp.mean(inputs * inputs, axis=-1, keepdims=True) + 1e-06)
    normed_ref[...] = (inputs * inv_rms * gain_ref[...]).astype(jnp.bfloat16)
    grad = grad.astype(jnp.bfloat16)
    grad_ref[...] = grad
    mine = lax.broadcasted_iota(jnp.int32, (slots, rows), 0)
    every = lax.broadcasted_iota(jnp.int32, (slots, rows), 1)
    coming_at = (
        (me_dp * sections + (mine >> log2(capacity))) * slots
        + me_section * capacity
        + (mine & (capacity - 1))
    )
    own_at = (me_dp * sections + me_section) * slots + mine
    coming = jnp.dot(
        (every == coming_at).astype(jnp.float32).astype(jnp.bfloat16),
        inputs.astype(jnp.bfloat16),
        preferred_element_type=jnp.float32,
    )
    own = jnp.dot(
        (every == own_at).astype(jnp.float32).astype(jnp.bfloat16),
        grad,
        preferred_element_type=jnp.float32,
    )
    extra_ref[...] = jnp.concatenate([coming, own], axis=0)


def place_blocks(distances, sources, targets, sems):
    me = lax.axis_index("dp")
    copies = []
    for i, (distance, source) in enumerate(zip(distances, sources)):
        part = source.shape[1]
        at = pl.ds(pl.multiple_of((me ^ distance) * part, 8), part)
        for k, target in enumerate(targets):
            copies.append(
                pltpu.make_async_copy(source.at[k], target.at[at, :], sems.at[2 * i + k])
            )
    fetch(copies)


def first_unpack_kernel(distances, own_expand_at, own_project_at, *refs):
    sources, (expand_ref, project_ref, sems) = refs[: len(distances)], refs[-3:]
    part, units = own_expand_at.shape[0], expand_ref.shape[1]
    me = lax.axis_index("dp")
    mine = pl.ds(pl.multiple_of(me * units, 128), units)
    at = pl.ds(pl.multiple_of(me * part, 8), part)
    own = [
        pltpu.make_async_copy(
            source.at[:, mine], target.at[at, :], sems.at[2 * len(distances) + k]
        )
        for k, (source, target) in enumerate(
            ((own_expand_at, expand_ref), (own_project_at, project_ref))
        )
    ]
    for copy in own:
        copy.start()
    place_blocks(distances, sources, (expand_ref, project_ref), sems)
    for copy in own:
        copy.wait()


def next_unpack_kernel(distances, expand_part_ref, project_part_ref, *refs):
    sources, (expand_ref, project_ref, sems) = refs[: len(distances)], refs[-3:]
    place_blocks(distances, sources, (expand_ref, project_ref), sems)


def hidden_kernel(
    distances, expand_part_ref, project_part_ref, normed_ref, grad_ref, *refs
):
    sources, (expand_ref, project_ref, both_ref, sems) = refs[: len(distances)], refs[-4:]
    place_blocks(distances, sources, (expand_ref, project_ref), sems)
    preact = jnp.dot(normed_ref[...], expand_ref[...], preferred_element_type=jnp.float32)
    activated, derivative = gelu_pair(preact)
    both_ref[0] = activated.astype(jnp.bfloat16)
    grad_hidden = jnp.dot(grad_ref[...], project_ref[...], preferred_element_type=jnp.float32)
    both_ref[1] = (grad_hidden * derivative).astype(jnp.bfloat16)


def share_kernel(
    sections, capacity, steps,
    me_ref, both_ref, expand_ref, project_ref, keep_ref, send_ref,
):
    rows = both_ref.shape[1]
    slots = sections * capacity
    row = lax.broadcasted_iota(jnp.int32, (rows, rows), 0)
    column = lax.broadcasted_iota(jnp.int32, (rows, rows), 1)
    inside = row & (slots - 1)
    replica = (row >> log2(slots)) & (rows // (sections * slots) - 1)
    away = row >> log2(rows // sections)
    goal = me_ref[1] ^ masked_steps(away, steps[::-1])
    base = replica * (slots * sections)
    mixed_from = (
        base + (inside >> log2(capacity)) * slots + goal * capacity + (inside & (capacity - 1))
    )
    normed_from = base + goal * slots + inside
    for k, (source, weight_ref) in enumerate(
        ((mixed_from, project_ref), (normed_from, expand_ref))
    ):
        turn = (column == source).astype(jnp.float32).astype(jnp.bfloat16)
        turned = jnp.dot(turn, both_ref[k], preferred_element_type=jnp.float32).astype(jnp.bfloat16)
        share = lax.dot_general(
            turned, weight_ref[...], (((1,), (1,)), ((), ())), preferred_element_type=jnp.float32
        )
        share = share.reshape(2, *keep_ref.shape[1:])
        keep_ref[k] = share[0]
        send_ref[k] = share[1].astype(jnp.bfloat16)


def halve_kernel(keep_ref, got_ref, next_keep_ref, next_send_ref):
    half = next_keep_ref.shape[1]
    total = keep_ref[...] + got_ref[...].astype(jnp.float32)
    next_keep_ref[...] = total[:, :half]
    next_send_ref[...] = total[:, half:].astype(jnp.bfloat16)


def address_kernel(keep_ref, got_ref, out_ref):
    total = keep_ref[...] + got_ref[...].astype(jnp.float32)
    for d in range(out_ref.shape[0]):
        out_ref[d] = jnp.concatenate([total[0, d], total[1, d]], axis=0).astype(jnp.bfloat16)


def weight_grad_kernel(
    hidden_distances, pre_distances, hidden_ref, pre_ref, grad_ref, normed_ref, *refs
):
    project_at, expand_at, result_ref, sems = refs[-4:]
    _, count, features, units = result_ref.shape
    pieces = sems.shape[2]
    piece = features // pieces
    copies = []
    for i in range(count):
        for k, (block_ref, rows_ref, out_at, distances) in enumerate(
            (
                (pre_ref, normed_ref, expand_at, pre_distances),
                (hidden_ref, grad_ref, project_at, hidden_distances),
            )
        ):
            result_ref[k, i] = jnp.dot(
                rows_ref[...], block_ref[i], preferred_element_type=jnp.float32
            ).astype(jnp.bfloat16)
            source = lax.axis_index("dp") ^ distances[i]
            columns = pl.ds(pl.multiple_of(source * units, 128), units)
            for j in range(pieces):
                at = pl.ds(j * piece, piece)
                copies.append(
                    pltpu.make_async_copy(
                        result_ref.at[k, i, at, :], out_at.at[at, columns], sems.at[k, i, j]
                    )
                )
                copies[-1].start()
    for copy in copies:
        copy.wait()


def finish_kernel(
    capacity,
    me_ref, count_ref, place_ref, tail_ref, extra_ref, patch_ref, text_ref, gain_ref,
    embedded_ref, grad_rows_ref,
):
    slots = patch_ref.shape[0]
    total = tail_ref[0].astype(jnp.float32)
    for d in range(1, tail_ref.shape[0]):
        total += tail_ref[d].astype(jnp.float32)
    mixed, grad_normed = total[:slots], total[slots:]
    out_rows = (extra_ref[:slots, :] + mixed).astype(jnp.bfloat16)
    length = text_ref.shape[0]
    chooser = landing(place_ref, count_ref, me_ref[1], slots, capacity, length)
    contract = (((0,), (0,)), ((), ()))
    placed = lax.dot_general(
        chooser.astype(jnp.bfloat16), out_rows, contract, preferred_element_type=jnp.float32
    )
    taken = lax.dot_general(
        chooser.astype(jnp.bfloat16), jnp.ones((slots, 128), jnp.bfloat16),
        contract, preferred_element_type=jnp.float32,
    )[:, :1]
    embedded_ref[...] = jnp.where(
        taken > 0.5, placed, text_ref[...].astype(jnp.float32)
    ).astype(jnp.bfloat16)
    inputs = patch_ref[...].astype(jnp.float32)
    inv_rms = lax.rsqrt(jnp.mean(inputs * inputs, axis=-1, keepdims=True) + 1e-06)
    scaled_grad = grad_normed * gain_ref[...]
    centred = jnp.mean(scaled_grad * inputs, axis=-1, keepdims=True)
    grad_rows_ref[...] = (
        extra_ref[slots:, :] + inv_rms * scaled_grad - inputs * (inv_rms**3 * centred)
    ).astype(jnp.bfloat16)


def weight_grads(
    hidden, hidden_distances, pre, pre_distances, grad_turned, normed_turned, width, before
):
    count, rows, units = hidden.shape
    features = grad_turned.shape[0]
    pieces = 2 if features % 32 == 0 else 1
    anywhere = pl.BlockSpec(memory_space=pl.ANY)
    return pl.pallas_call(
        functools.partial(weight_grad_kernel, hidden_distances, pre_distances),
        in_specs=[VMEM_SPEC] * 4 + [anywhere] * len(before),
        out_specs=[anywhere] * 2,
        out_shape=[jax.ShapeDtypeStruct((features, width), jnp.bfloat16)] * 2,
        scratch_shapes=[
            pltpu.VMEM((2, count, features, units), jnp.bfloat16),
            pltpu.SemaphoreType.DMA((2, count, pieces)),
        ],
        input_output_aliases={4: 0, 5: 1} if before else {},
        compiler_params=pltpu.CompilerParams(vmem_limit_bytes=12 << 20),
        cost_estimate=pl.CostEstimate(
            flops=4 * count * rows * features * units,
            bytes_accessed=4 * count * units * features + 4 * rows * features,
            transcendentals=0,
        ),
    )(hidden, pre, grad_turned, normed_turned, *before)


def call(kernel, out_shape, smem, vmem, scratch=()):
    single = not isinstance(out_shape, (list, tuple))
    return pl.pallas_call(
        kernel,
        out_shape=out_shape,
        in_specs=[SMEM_SPEC] * len(smem) + [VMEM_SPEC] * len(vmem),
        out_specs=VMEM_SPEC if single else [VMEM_SPEC] * len(out_shape),
        scratch_shapes=scratch,
        compiler_params=pltpu.CompilerParams(vmem_limit_bytes=12 << 20),
    )(*smem, *vmem)


def arrival_groups(dp):
    half, quarter = 1 << (dp - 1), 1 << (dp - 2)
    last = (2 * quarter - 1,) if quarter > 1 else (2 * half - 1,)
    middle = tuple(i for i in (quarter, 2 * half - 1) if i not in last)
    early = tuple(i for i in range(1, 2 * half) if i not in last + middle)
    return early, middle, last


def join(first, second):
    both = (first.shape[0] + second.shape[0], *first.shape[1:])
    return call(join_kernel, jax.ShapeDtypeStruct(both, first.dtype), (), (first, second))


def join_pairs_kernel(first_ref, second_ref, hidden_ref, pre_ref):
    for k, out_ref in enumerate((hidden_ref, pre_ref)):
        out_ref[0] = first_ref[k]
        out_ref[1] = second_ref[k]


def join_pairs(first, second):
    out = jax.ShapeDtypeStruct(first.shape, first.dtype)
    return call(join_pairs_kernel, [out, out], (), (first, second))


def move_rows_plan(
    patches, gain, expand_weight, project_weight, counts, positions, text, cotangent
):
    sections = lax.axis_size("section")
    replicas = lax.axis_size("dp")
    devices = sections * replicas
    slots, features = patches.shape
    part, width = expand_weight.shape
    units = width // replicas
    capacity = slots // sections
    rows = devices * slots
    dp_steps, section_steps = bit_steps(replicas), bit_steps(sections)
    me = jnp.stack([lax.axis_index("dp"), lax.axis_index("section")]).astype(jnp.int32)
    gain = gain.reshape(1, features)
    project_turned = project_weight.T
    kept, wide = jnp.bfloat16, jnp.float32
    shape = jax.ShapeDtypeStruct

    hbm = pl.BlockSpec(memory_space=pltpu.HBM)

    def in_hbm(*arrays):
        return [pltpu.with_memory_space_constraint(array, pltpu.HBM) for array in arrays]

    held = pl.pallas_call(
        functools.partial(pick_kernel, capacity),
        out_shape=shape((1, 2 * slots, features), kept),
        in_specs=[hbm] * 4,
        out_specs=VMEM_SPEC,
        scratch_shapes=[
            pltpu.SMEM(counts.shape, counts.dtype),
            pltpu.SMEM(positions.shape, positions.dtype),
            pltpu.VMEM(patches.shape, kept),
            pltpu.VMEM(cotangent.shape, kept),
            pltpu.SemaphoreType.DMA((4,)),
        ],
        compiler_params=pltpu.CompilerParams(vmem_limit_bytes=12 << 20),
    )(*in_hbm(counts, positions, patches, cotangent))
    blocks = pl.pallas_call(
        repack_kernel,
        out_shape=[shape((2, part, units), kept)] * (replicas - 1),
        in_specs=[hbm] * 2,
        out_specs=[VMEM_SPEC] * (replicas - 1),
        scratch_shapes=[pltpu.SemaphoreType.DMA((2 * replicas - 2,))],
        compiler_params=pltpu.CompilerParams(vmem_limit_bytes=12 << 20),
    )(*in_hbm(expand_weight, project_turned))
    arrived = []
    for distance in range(1, replicas):
        arrived.append(swap(blocks[distance - 1], "dp", distance))

    exchanges = [("dp", step) for step in dp_steps] + [("section", step) for step in section_steps]
    for axis, step in exchanges:
        got = swap(held, axis, step)
        if held.shape[0] < devices // 2:
            held = join(held, got)
    normed, grad_all, extra = call(
        functools.partial(order_kernel, sections, capacity, dp_steps, section_steps),
        [shape((rows, features), kept)] * 2 + [shape((2 * slots, features), wide)],
        (me,), (held, got, gain),
    )
    normed_turned, grad_turned = call(
        turn_kernel, [shape((features, rows), kept)] * 2, (), (normed, grad_all)
    )
    anywhere = pl.BlockSpec(memory_space=pl.ANY)
    slices = [shape((features, units), kept)] * 2
    groups = arrival_groups(log2(replicas))

    def unpacking(kernel, group, operands, specs, extra=(), aliases=()):
        return pl.pallas_call(
            functools.partial(kernel, group),
            out_shape=[*slices, *extra],
            in_specs=[*specs, *[anywhere] * len(group)],
            out_specs=[VMEM_SPEC] * (2 + len(extra)),
            scratch_shapes=[pltpu.SemaphoreType.DMA((2 * len(group) + 2,))],
            input_output_aliases=dict(aliases),
            compiler_params=pltpu.CompilerParams(vmem_limit_bytes=12 << 20),
        )(*operands, *(arrived[distance - 1] for distance in group))

    in_place = ((0, 0), (1, 1))
    held_slices = unpacking(
        first_unpack_kernel, groups[0], in_hbm(expand_weight, project_turned), [hbm] * 2
    )
    held_slices = unpacking(
        next_unpack_kernel, groups[1], held_slices, [VMEM_SPEC] * 2, aliases=in_place
    )
    expand_slice, project_slice, both = unpacking(
        hidden_kernel, groups[2], (*held_slices, normed, grad_all), [VMEM_SPEC] * 4,
        [shape((2, rows, units), kept)], in_place,
    )

    tail_steps = section_steps[::-1]
    keep, send = call(
        functools.partial(share_kernel, sections, capacity, tail_steps),
        [shape((2, devices // 2, slots, features), kind) for kind in (wide, kept)],
        (me,), (both, expand_slice, project_slice),
    )
    for place, step in enumerate(tail_steps):
        got = swap(send, "section", step)
        if place < len(tail_steps) - 1:
            half = (2, send.shape[1] // 2, slots, features)
            keep, send = call(
                halve_kernel, [shape(half, wide), shape(half, kept)], (), (keep, got)
            )
    tail = call(address_kernel, shape((replicas, 2 * slots, features), kept), (), (keep, got))
    tail = lax.all_to_all(tail, "dp", split_axis=0, concat_axis=0, tiled=True)

    far_both = swap(both, "dp", dp_steps[0])
    pairs = join_pairs(both, far_both)
    gathered = []
    for pair, steps in ((pairs[0], dp_steps[1:]), (pairs[1], dp_steps[:0:-1])):
        held_pairs = {0: pair}
        for step in steps:
            for mask, array in list(held_pairs.items()):
                held_pairs[mask ^ step] = swap(array, "dp", step)
        gathered.append(held_pairs.items())
    grads = ()
    for (hidden_mask, hidden), (pre_mask, pre) in zip(*gathered):
        far = dp_steps[0]
        grads = weight_grads(
            hidden, (hidden_mask, hidden_mask ^ far), pre, (pre_mask, pre_mask ^ far),
            grad_turned, normed_turned, width, grads,
        )
    project_grad, expand_grad = grads
    embedded, grad_rows = call(
        functools.partial(finish_kernel, capacity),
        [shape(text.shape, kept), shape(patches.shape, kept)],
        (me, counts, positions), (tail, extra, patches, text, gain),
    )
    return (embedded, grad_rows, expand_grad, project_grad.T)


def power_of_two(value):
    return value > 0 and value & (value - 1) == 0


def shards(patches, gain, expand_weight, project_weight, counts, positions, text, cotangent):
    replicas, sections = lax.axis_size("dp"), lax.axis_size("section")
    slots, features = patches.shape
    width = expand_weight.shape[1]
    rows = replicas * sections * slots
    fits = rows * (features + width) <= features * width
    even = (
        all(power_of_two(n) for n in (replicas, sections, slots))
        and replicas > 2
        and sections > 1
        and slots % 8 == 0
        and width % (128 * replicas) == 0
    )
    if fits and even:
        plan = move_rows_plan
    else:
        plan = gather_weights_plan
    return plan(
        patches, gain, expand_weight, project_weight, counts, positions, text, cotangent
    )


def solution(mesh):
    return jax.shard_map(
        shards,
        mesh=mesh,
        in_specs=(
            P(("dp", "section"), None),
            P(),
            P("dp", "section"),
            P("section", "dp"),
            P("dp", None),
            P(("dp", "section"), None),
            P(("dp", "section"), None),
            P(("dp", "section"), None),
        ),
        out_specs=(
            P(("dp", "section"), None),
            P(("dp", "section"), None),
            P(None, "section"),
            P("section", None),
        ),
        check_vma=False,
    )
```

```python
import functools

import jax
import jax.numpy as jnp
from jax import lax
from jax.experimental import pallas as pl
from jax.experimental.pallas import tpu as pltpu
from jax.sharding import PartitionSpec as P


def gelu_pair(values):
    coeff = 0.7978845608
    inner = coeff * (values + 0.044715 * values * values * values)
    tangent = jnp.tanh(inner)
    activated = 0.5 * values * (1.0 + tangent)
    derivative = 0.5 * (1.0 + tangent) + 0.5 * values * (1.0 - tangent * tangent) * coeff * (
        1.0 + 3.0 * 0.044715 * values * values
    )
    return (activated, derivative)


def gather_weights_plan(
    patches, gain, expand_weight, project_weight, counts, positions, text, cotangent
):
    sections = lax.axis_size("section")
    slot_count = patches.shape[0]
    features = patches.shape[1]
    capacity = slot_count // sections
    inputs = patches.astype(jnp.float32)
    inv_rms = lax.rsqrt(jnp.mean(inputs * inputs, axis=-1, keepdims=True) + 1e-06)
    normed = (inputs * inv_rms * gain).astype(jnp.bfloat16)
    gathered = lax.all_gather(normed, "section", axis=0, tiled=True)
    expand_full, project_full = (
        lax.all_gather(expand_weight, "dp", axis=0, tiled=True),
        lax.all_gather(project_weight, "dp", axis=1, tiled=True),
    )
    preact = jnp.dot(gathered, expand_full, preferred_element_type=jnp.float32)
    activated, derivative = gelu_pair(preact)
    hidden = activated.astype(jnp.bfloat16)
    row_block = hidden
    mixed = lax.psum_scatter(
        jnp.dot(row_block, project_full, preferred_element_type=jnp.float32).astype(jnp.bfloat16),
        "section",
        scatter_dimension=0,
        tiled=True,
    ).astype(jnp.float32)
    out_rows = (inputs + mixed).astype(jnp.bfloat16)
    arrived = lax.all_to_all(out_rows, "section", split_axis=0, concat_axis=0, tiled=True)
    section_id = lax.axis_index("section")
    arrival = jnp.arange(slot_count, dtype=jnp.int32)
    source = arrival // capacity
    slot_index = section_id * capacity + arrival % capacity
    is_live = (slot_index < counts[0][source])[:, None]
    targets = positions[0]
    current = text[targets]
    embedded = text.at[targets].set(jnp.where(is_live, arrived, current))
    picked = jnp.where(is_live, cotangent[targets], jnp.zeros_like(current))
    collected = lax.all_gather(picked, "section", axis=0, tiled=True)
    grad_all = (
        collected.reshape(sections, sections, capacity, features)
        .transpose(1, 0, 2, 3)
        .reshape(sections * slot_count, features)
    )
    returned = lax.dynamic_slice_in_dim(grad_all, section_id * slot_count, slot_count, 0)
    grad_own = returned.astype(jnp.float32)
    project_local = lax.dot_general(
        hidden, grad_all, (((0,), (0,)), ((), ())), preferred_element_type=jnp.float32
    )
    grad_hidden = lax.dot_general(
        grad_all, project_full, (((1,), (1,)), ((), ())), preferred_element_type=jnp.float32
    )
    grad_pre = (grad_hidden * derivative).astype(jnp.bfloat16)
    row_block = grad_pre
    grad_normed = lax.psum_scatter(
        lax.dot_general(
            row_block, expand_full, (((1,), (1,)), ((), ())), preferred_element_type=jnp.float32
        ).astype(jnp.bfloat16),
        "section",
        scatter_dimension=0,
        tiled=True,
    ).astype(jnp.float32)
    expand_local = lax.dot_general(
        gathered, grad_pre, (((0,), (0,)), ((), ())), preferred_element_type=jnp.float32
    )
    project_total, expand_total = (
        lax.psum(project_local.astype(jnp.bfloat16), "dp").astype(jnp.float32),
        lax.psum(expand_local.astype(jnp.bfloat16), "dp").astype(jnp.float32),
    )
    scaled_grad = grad_normed * gain
    centred = jnp.mean(scaled_grad * inputs, axis=-1, keepdims=True)
    grad_rows = (grad_own + inv_rms * scaled_grad - inputs * inv_rms**3 * centred).astype(
        jnp.bfloat16
    )
    return (
        embedded,
        grad_rows,
        expand_total.astype(jnp.bfloat16),
        project_total.astype(jnp.bfloat16),
    )


def bit_steps(size):
    steps = []
    step = size // 2
    while step >= 1:
        steps.append(step)
        step //= 2
    return steps


def swap(array, axis, step):
    size = lax.axis_size(axis)
    return lax.ppermute(array, axis, [(i, i ^ step) for i in range(size)])


def masked_steps(index, steps):
    mask = 0
    for place, step in enumerate(steps):
        mask = mask + ((index >> place) & 1) * step
    return mask


VMEM_SPEC = pl.BlockSpec(memory_space=pltpu.VMEM)
SMEM_SPEC = pl.BlockSpec(memory_space=pltpu.SMEM)


def log2(value):
    return value.bit_length() - 1


def landing(place_ref, count_ref, section, slots, capacity, length):
    row = lax.broadcasted_iota(jnp.int32, (slots, length), 0)
    column = lax.broadcasted_iota(jnp.int32, (slots, length), 1)
    spot = jnp.full((slots, length), -1, jnp.int32)
    for q in range(slots):
        live = section * capacity + q % capacity < count_ref[0, q // capacity]
        spot = jnp.where(row == q, jnp.where(live, place_ref[0, q], -1), spot)
    return (spot == column).astype(jnp.float32)


def fetch(copies):
    for copy in copies:
        copy.start()
    for copy in copies:
        copy.wait()


def pick_kernel(
    capacity, counts_at, places_at, patches_at, cotangent_at, pair_ref,
    count_ref, place_ref, patch_ref, cotangent_ref, sems,
):
    ends = (
        (counts_at, count_ref), (places_at, place_ref),
        (patches_at, patch_ref), (cotangent_at, cotangent_ref),
    )
    fetch([pltpu.make_async_copy(a, b, sems.at[i]) for i, (a, b) in enumerate(ends)])
    slots = patch_ref.shape[0]
    section = lax.axis_index("section")
    chooser = landing(
        place_ref, count_ref, section, slots, capacity, cotangent_ref.shape[0]
    ).astype(jnp.bfloat16)
    picked = jnp.dot(chooser, cotangent_ref[...], preferred_element_type=jnp.float32)
    pair_ref[0] = jnp.concatenate(
        [patch_ref[...].astype(jnp.float32), picked], axis=0
    ).astype(jnp.bfloat16)


def repack_kernel(expand_at, project_at, *refs):
    blocks, sems = refs[:-1], refs[-1]
    units = blocks[0].shape[2]
    copies = []
    for i, block in enumerate(blocks):
        start = pl.multiple_of((lax.axis_index("dp") ^ (i + 1)) * units, 128)
        for k, source in enumerate((expand_at, project_at)):
            copies.append(
                pltpu.make_async_copy(
                    source.at[:, pl.ds(start, units)], block.at[k], sems.at[2 * i + k]
                )
            )
    fetch(copies)


def turn_kernel(normed_ref, grad_ref, normed_turned_ref, grad_turned_ref):
    normed_turned_ref[...] = normed_ref[...].T
    grad_turned_ref[...] = grad_ref[...].T


def join_kernel(first_ref, second_ref, out_ref):
    count = first_ref.shape[0]
    out_ref[:count] = first_ref[...]
    out_ref[count:] = second_ref[...]


def order_kernel(
    sections, capacity, dp_steps, section_steps,
    me_ref, near_ref, far_ref, gain_ref, normed_ref, grad_ref, extra_ref,
):
    rows = normed_ref.shape[0]
    slots = sections * capacity
    half = near_ref.shape[0] * near_ref.shape[1]
    me_dp, me_section = me_ref[0], me_ref[1]
    column = lax.broadcasted_iota(jnp.int32, (8, half), 1)
    row = lax.broadcasted_iota(jnp.int32, (rows, half), 0)
    kind = column & (2 * slots - 1)
    slot = kind & (slots - 1)
    inputs = grad = None
    for side, ref in enumerate((near_ref, far_ref)):
        block = (column >> log2(2 * slots)) + side * (half // (2 * slots))
        source_dp = me_dp ^ masked_steps(block, dp_steps)
        source_section = me_section ^ masked_steps(block >> len(dp_steps), section_steps)
        patch_at = (source_dp * sections + source_section) * slots + slot
        grad_at = (
            (source_dp * sections + (slot >> log2(capacity))) * slots
            + source_section * capacity
            + (slot & (capacity - 1))
        )
        patch_at = jnp.where(kind < slots, patch_at, -1)[:1]
        grad_at = jnp.where(kind >= slots, grad_at, -1)[:1]
        values = ref[...].reshape(half, ref.shape[2])
        chosen = (row == patch_at).astype(jnp.float32).astype(jnp.bfloat16)
        found = jnp.dot(chosen, values, preferred_element_type=jnp.float32)
        inputs = found if inputs is None else inputs + found
        chosen = (row == grad_at).astype(jnp.float32).astype(jnp.bfloat16)
        found = jnp.dot(chosen, values, preferred_element_type=jnp.float32)
        grad = found if grad is None else grad + found
    inv_rms = lax.rsqrt(jnp.mean(inputs * inputs, axis=-1, keepdims=True) + 1e-06)
    normed_ref[...] = (inputs * inv_rms * gain_ref[...]).astype(jnp.bfloat16)
    grad = grad.astype(jnp.bfloat16)
    grad_ref[...] = grad
    mine = lax.broadcasted_iota(jnp.int32, (slots, rows), 0)
    every = lax.broadcasted_iota(jnp.int32, (slots, rows), 1)
    coming_at = (
        (me_dp * sections + (mine >> log2(capacity))) * slots
        + me_section * capacity
        + (mine & (capacity - 1))
    )
    own_at = (me_dp * sections + me_section) * slots + mine
    coming = jnp.dot(
        (every == coming_at).astype(jnp.float32).astype(jnp.bfloat16),
        inputs.astype(jnp.bfloat16),
        preferred_element_type=jnp.float32,
    )
    own = jnp.dot(
        (every == own_at).astype(jnp.float32).astype(jnp.bfloat16),
        grad,
        preferred_element_type=jnp.float32,
    )
    extra_ref[...] = jnp.concatenate([coming, own], axis=0)


def place_blocks(distances, sources, targets, sems):
    me = lax.axis_index("dp")
    copies = []
    for i, (distance, source) in enumerate(zip(distances, sources)):
        part = source.shape[1]
        at = pl.ds(pl.multiple_of((me ^ distance) * part, 8), part)
        for k, target in enumerate(targets):
            copies.append(
                pltpu.make_async_copy(source.at[k], target.at[at, :], sems.at[2 * i + k])
            )
    fetch(copies)


def first_unpack_kernel(distances, own_expand_at, own_project_at, *refs):
    sources, (expand_ref, project_ref, sems) = refs[: len(distances)], refs[-3:]
    part, units = own_expand_at.shape[0], expand_ref.shape[1]
    me = lax.axis_index("dp")
    mine = pl.ds(pl.multiple_of(me * units, 128), units)
    at = pl.ds(pl.multiple_of(me * part, 8), part)
    own = [
        pltpu.make_async_copy(
            source.at[:, mine], target.at[at, :], sems.at[2 * len(distances) + k]
        )
        for k, (source, target) in enumerate(
            ((own_expand_at, expand_ref), (own_project_at, project_ref))
        )
    ]
    for copy in own:
        copy.start()
    place_blocks(distances, sources, (expand_ref, project_ref), sems)
    for copy in own:
        copy.wait()


def next_unpack_kernel(distances, expand_part_ref, project_part_ref, *refs):
    sources, (expand_ref, project_ref, sems) = refs[: len(distances)], refs[-3:]
    place_blocks(distances, sources, (expand_ref, project_ref), sems)


def hidden_kernel(
    distances, expand_part_ref, project_part_ref, normed_ref, grad_ref, *refs
):
    sources, (expand_ref, project_ref, both_ref, sems) = refs[: len(distances)], refs[-4:]
    place_blocks(distances, sources, (expand_ref, project_ref), sems)
    preact = jnp.dot(normed_ref[...], expand_ref[...], preferred_element_type=jnp.float32)
    activated, derivative = gelu_pair(preact)
    both_ref[0] = activated.astype(jnp.bfloat16)
    grad_hidden = jnp.dot(grad_ref[...], project_ref[...], preferred_element_type=jnp.float32)
    both_ref[1] = (grad_hidden * derivative).astype(jnp.bfloat16)


def share_kernel(
    sections, capacity, steps,
    me_ref, both_ref, expand_ref, project_ref, keep_ref, send_ref,
):
    rows = both_ref.shape[1]
    slots = sections * capacity
    row = lax.broadcasted_iota(jnp.int32, (rows, rows), 0)
    column = lax.broadcasted_iota(jnp.int32, (rows, rows), 1)
    inside = row & (slots - 1)
    replica = (row >> log2(slots)) & (rows // (sections * slots) - 1)
    away = row >> log2(rows // sections)
    goal = me_ref[1] ^ masked_steps(away, steps[::-1])
    base = replica * (slots * sections)
    mixed_from = (
        base + (inside >> log2(capacity)) * slots + goal * capacity + (inside & (capacity - 1))
    )
    normed_from = base + goal * slots + inside
    for k, (source, weight_ref) in enumerate(
        ((mixed_from, project_ref), (normed_from, expand_ref))
    ):
        turn = (column == source).astype(jnp.float32).astype(jnp.bfloat16)
        turned = jnp.dot(turn, both_ref[k], preferred_element_type=jnp.float32).astype(jnp.bfloat16)
        share = lax.dot_general(
            turned, weight_ref[...], (((1,), (1,)), ((), ())), preferred_element_type=jnp.float32
        )
        share = share.reshape(2, *keep_ref.shape[1:])
        keep_ref[k] = share[0]
        send_ref[k] = share[1].astype(jnp.bfloat16)


def halve_kernel(keep_ref, got_ref, next_keep_ref, next_send_ref):
    half = next_keep_ref.shape[1]
    total = keep_ref[...] + got_ref[...].astype(jnp.float32)
    next_keep_ref[...] = total[:, :half]
    next_send_ref[...] = total[:, half:].astype(jnp.bfloat16)


def address_kernel(keep_ref, got_ref, out_ref):
    total = keep_ref[...] + got_ref[...].astype(jnp.float32)
    for d in range(out_ref.shape[0]):
        out_ref[d] = jnp.concatenate([total[0, d], total[1, d]], axis=0).astype(jnp.bfloat16)


def weight_grad_kernel(distances, grad_ref, normed_ref, *refs):
    project_at, expand_at, result_ref, sems = refs[-4:]
    blocks = refs[: len(distances)]
    features, units = result_ref.shape[2:]
    pieces = sems.shape[2]
    piece = features // pieces
    copies = []
    for i, (distance, block_ref) in enumerate(zip(distances, blocks)):
        source = lax.axis_index("dp") ^ distance
        columns = pl.ds(pl.multiple_of(source * units, 128), units)
        for k, (rows_ref, out_at) in enumerate(((grad_ref, project_at), (normed_ref, expand_at))):
            result_ref[k, i] = jnp.dot(
                rows_ref[...], block_ref[k], preferred_element_type=jnp.float32
            ).astype(jnp.bfloat16)
            for j in range(pieces):
                at = pl.ds(j * piece, piece)
                copies.append(
                    pltpu.make_async_copy(
                        result_ref.at[k, i, at, :], out_at.at[at, columns], sems.at[k, i, j]
                    )
                )
                copies[-1].start()
    for copy in copies:
        copy.wait()


def finish_kernel(
    capacity,
    me_ref, count_ref, place_ref, tail_ref, extra_ref, patch_ref, text_ref, gain_ref,
    embedded_ref, grad_rows_ref,
):
    slots = patch_ref.shape[0]
    total = tail_ref[0].astype(jnp.float32)
    for d in range(1, tail_ref.shape[0]):
        total += tail_ref[d].astype(jnp.float32)
    mixed, grad_normed = total[:slots], total[slots:]
    out_rows = (extra_ref[:slots, :] + mixed).astype(jnp.bfloat16)
    length = text_ref.shape[0]
    chooser = landing(place_ref, count_ref, me_ref[1], slots, capacity, length)
    contract = (((0,), (0,)), ((), ()))
    placed = lax.dot_general(
        chooser.astype(jnp.bfloat16), out_rows, contract, preferred_element_type=jnp.float32
    )
    taken = lax.dot_general(
        chooser.astype(jnp.bfloat16), jnp.ones((slots, 128), jnp.bfloat16),
        contract, preferred_element_type=jnp.float32,
    )[:, :1]
    embedded_ref[...] = jnp.where(
        taken > 0.5, placed, text_ref[...].astype(jnp.float32)
    ).astype(jnp.bfloat16)
    inputs = patch_ref[...].astype(jnp.float32)
    inv_rms = lax.rsqrt(jnp.mean(inputs * inputs, axis=-1, keepdims=True) + 1e-06)
    scaled_grad = grad_normed * gain_ref[...]
    centred = jnp.mean(scaled_grad * inputs, axis=-1, keepdims=True)
    grad_rows_ref[...] = (
        extra_ref[slots:, :] + inv_rms * scaled_grad - inputs * (inv_rms**3 * centred)
    ).astype(jnp.bfloat16)


def weight_grads(blocks, distances, grad_turned, normed_turned, width, before):
    count = len(blocks)
    _, rows, units = blocks[0].shape
    features = grad_turned.shape[0]
    pieces = 2 if features % 32 == 0 else 1
    anywhere = pl.BlockSpec(memory_space=pl.ANY)
    aliases = {2 + count: 0, 3 + count: 1} if before else {}
    return pl.pallas_call(
        functools.partial(weight_grad_kernel, distances),
        in_specs=[VMEM_SPEC] * (2 + count) + [anywhere] * len(before),
        out_specs=[anywhere] * 2,
        out_shape=[jax.ShapeDtypeStruct((features, width), jnp.bfloat16)] * 2,
        scratch_shapes=[
            pltpu.VMEM((2, count, features, units), jnp.bfloat16),
            pltpu.SemaphoreType.DMA((2, count, pieces)),
        ],
        input_output_aliases=aliases,
        compiler_params=pltpu.CompilerParams(vmem_limit_bytes=12 << 20),
        cost_estimate=pl.CostEstimate(
            flops=4 * count * rows * features * units,
            bytes_accessed=4 * count * units * features + 4 * rows * features,
            transcendentals=0,
        ),
    )(grad_turned, normed_turned, *blocks, *before)


def call(kernel, out_shape, smem, vmem, scratch=()):
    single = not isinstance(out_shape, (list, tuple))
    return pl.pallas_call(
        kernel,
        out_shape=out_shape,
        in_specs=[SMEM_SPEC] * len(smem) + [VMEM_SPEC] * len(vmem),
        out_specs=VMEM_SPEC if single else [VMEM_SPEC] * len(out_shape),
        scratch_shapes=scratch,
        compiler_params=pltpu.CompilerParams(vmem_limit_bytes=12 << 20),
    )(*smem, *vmem)


def arrival_groups(dp):
    half, quarter = 1 << (dp - 1), 1 << (dp - 2)
    last = (2 * quarter - 1,) if quarter > 1 else (2 * half - 1,)
    middle = tuple(i for i in (quarter, 2 * half - 1) if i not in last)
    early = tuple(i for i in range(1, 2 * half) if i not in last + middle)
    return early, middle, last


def join(first, second):
    both = (first.shape[0] + second.shape[0], *first.shape[1:])
    return call(join_kernel, jax.ShapeDtypeStruct(both, first.dtype), (), (first, second))


def unit_order(dp):
    far = 1 << (dp - 1)

    def key(distance):
        hops = distance.bit_count()
        return (hops, hops > 1 and distance >= far, -distance)

    return sorted(range(1, 2 * far), key=key)


def gradient_groups(dp):
    order = unit_order(dp)
    order = order[1:dp] + order[dp : dp + 1] + order[:1] + order[dp + 1 :]
    return [(0,)] + [tuple(order[i : i + 2]) for i in range(0, len(order), 2)]


def move_rows_plan(
    patches, gain, expand_weight, project_weight, counts, positions, text, cotangent
):
    sections = lax.axis_size("section")
    replicas = lax.axis_size("dp")
    devices = sections * replicas
    slots, features = patches.shape
    part, width = expand_weight.shape
    units = width // replicas
    capacity = slots // sections
    rows = devices * slots
    dp_steps, section_steps = bit_steps(replicas), bit_steps(sections)
    me = jnp.stack([lax.axis_index("dp"), lax.axis_index("section")]).astype(jnp.int32)
    gain = gain.reshape(1, features)
    project_turned = project_weight.T
    kept, wide = jnp.bfloat16, jnp.float32
    shape = jax.ShapeDtypeStruct

    hbm = pl.BlockSpec(memory_space=pltpu.HBM)

    def in_hbm(*arrays):
        return [pltpu.with_memory_space_constraint(array, pltpu.HBM) for array in arrays]

    held = pl.pallas_call(
        functools.partial(pick_kernel, capacity),
        out_shape=shape((1, 2 * slots, features), kept),
        in_specs=[hbm] * 4,
        out_specs=VMEM_SPEC,
        scratch_shapes=[
            pltpu.SMEM(counts.shape, counts.dtype),
            pltpu.SMEM(positions.shape, positions.dtype),
            pltpu.VMEM(patches.shape, kept),
            pltpu.VMEM(cotangent.shape, kept),
            pltpu.SemaphoreType.DMA((4,)),
        ],
        compiler_params=pltpu.CompilerParams(vmem_limit_bytes=12 << 20),
    )(*in_hbm(counts, positions, patches, cotangent))
    blocks = pl.pallas_call(
        repack_kernel,
        out_shape=[shape((2, part, units), kept)] * (replicas - 1),
        in_specs=[hbm] * 2,
        out_specs=[VMEM_SPEC] * (replicas - 1),
        scratch_shapes=[pltpu.SemaphoreType.DMA((2 * replicas - 2,))],
        compiler_params=pltpu.CompilerParams(vmem_limit_bytes=12 << 20),
    )(*in_hbm(expand_weight, project_turned))
    arrived = []
    for distance in range(1, replicas):
        arrived.append(swap(blocks[distance - 1], "dp", distance))

    exchanges = [("dp", step) for step in dp_steps] + [("section", step) for step in section_steps]
    for axis, step in exchanges:
        got = swap(held, axis, step)
        if held.shape[0] < devices // 2:
            held = join(held, got)
    normed, grad_all, extra = call(
        functools.partial(order_kernel, sections, capacity, dp_steps, section_steps),
        [shape((rows, features), kept)] * 2 + [shape((2 * slots, features), wide)],
        (me,), (held, got, gain),
    )
    normed_turned, grad_turned = call(
        turn_kernel, [shape((features, rows), kept)] * 2, (), (normed, grad_all)
    )
    anywhere = pl.BlockSpec(memory_space=pl.ANY)
    slices = [shape((features, units), kept)] * 2
    groups = arrival_groups(log2(replicas))

    def unpacking(kernel, group, operands, specs, extra=(), aliases=()):
        return pl.pallas_call(
            functools.partial(kernel, group),
            out_shape=[*slices, *extra],
            in_specs=[*specs, *[anywhere] * len(group)],
            out_specs=[VMEM_SPEC] * (2 + len(extra)),
            scratch_shapes=[pltpu.SemaphoreType.DMA((2 * len(group) + 2,))],
            input_output_aliases=dict(aliases),
            compiler_params=pltpu.CompilerParams(vmem_limit_bytes=12 << 20),
        )(*operands, *(arrived[distance - 1] for distance in group))

    in_place = ((0, 0), (1, 1))
    held_slices = unpacking(
        first_unpack_kernel, groups[0], in_hbm(expand_weight, project_turned), [hbm] * 2
    )
    held_slices = unpacking(
        next_unpack_kernel, groups[1], held_slices, [VMEM_SPEC] * 2, aliases=in_place
    )
    expand_slice, project_slice, both = unpacking(
        hidden_kernel, groups[2], (*held_slices, normed, grad_all), [VMEM_SPEC] * 4,
        [shape((2, rows, units), kept)], in_place,
    )

    tail_steps = section_steps[::-1]
    keep, send = call(
        functools.partial(share_kernel, sections, capacity, tail_steps),
        [shape((2, devices // 2, slots, features), kind) for kind in (wide, kept)],
        (me,), (both, expand_slice, project_slice),
    )
    for place, step in enumerate(tail_steps):
        got = swap(send, "section", step)
        if place < len(tail_steps) - 1:
            half = (2, send.shape[1] // 2, slots, features)
            keep, send = call(
                halve_kernel, [shape(half, wide), shape(half, kept)], (), (keep, got)
            )
    tail = call(address_kernel, shape((replicas, 2 * slots, features), kept), (), (keep, got))
    tail = lax.all_to_all(tail, "dp", split_axis=0, concat_axis=0, tiled=True)

    units_from = {0: both}
    for step in dp_steps:
        for distance, block in list(units_from.items()):
            units_from[distance ^ step] = swap(block, "dp", step)
    grads = ()
    for distances in gradient_groups(log2(replicas)):
        grads = weight_grads(
            [units_from[distance] for distance in distances], distances,
            grad_turned, normed_turned, width, grads,
        )
    project_grad, expand_grad = grads
    embedded, grad_rows = call(
        functools.partial(finish_kernel, capacity),
        [shape(text.shape, kept), shape(patches.shape, kept)],
        (me, counts, positions), (tail, extra, patches, text, gain),
    )
    return (embedded, grad_rows, expand_grad, project_grad.T)


def power_of_two(value):
    return value > 0 and value & (value - 1) == 0


def shards(patches, gain, expand_weight, project_weight, counts, positions, text, cotangent):
    replicas, sections = lax.axis_size("dp"), lax.axis_size("section")
    slots, features = patches.shape
    width = expand_weight.shape[1]
    rows = replicas * sections * slots
    fits = rows * (features + width) <= features * width
    even = (
        all(power_of_two(n) for n in (replicas, sections, slots))
        and replicas > 2
        and sections > 1
        and slots % 8 == 0
        and width % (128 * replicas) == 0
    )
    if fits and even:
        plan = move_rows_plan
    else:
        plan = gather_weights_plan
    return plan(
        patches, gain, expand_weight, project_weight, counts, positions, text, cotangent
    )


def solution(mesh):
    return jax.shard_map(
        shards,
        mesh=mesh,
        in_specs=(
            P(("dp", "section"), None),
            P(),
            P("dp", "section"),
            P("section", "dp"),
            P("dp", None),
            P(("dp", "section"), None),
            P(("dp", "section"), None),
            P(("dp", "section"), None),
        ),
        out_specs=(
            P(("dp", "section"), None),
            P(("dp", "section"), None),
            P(None, "section"),
            P("section", None),
        ),
        check_vma=False,
    )
```

```python
import functools

import jax
import jax.numpy as jnp
from jax import lax
from jax.experimental import pallas as pl
from jax.experimental.pallas import tpu as pltpu
from jax.sharding import PartitionSpec as P


def gelu_pair(values):
    coeff = 0.7978845608
    inner = coeff * (values + 0.044715 * values * values * values)
    tangent = jnp.tanh(inner)
    activated = 0.5 * values * (1.0 + tangent)
    derivative = 0.5 * (1.0 + tangent) + 0.5 * values * (1.0 - tangent * tangent) * coeff * (
        1.0 + 3.0 * 0.044715 * values * values
    )
    return (activated, derivative)


def gather_weights_plan(
    patches, gain, expand_weight, project_weight, counts, positions, text, cotangent
):
    sections = lax.axis_size("section")
    slot_count = patches.shape[0]
    features = patches.shape[1]
    capacity = slot_count // sections
    inputs = patches.astype(jnp.float32)
    inv_rms = lax.rsqrt(jnp.mean(inputs * inputs, axis=-1, keepdims=True) + 1e-06)
    normed = (inputs * inv_rms * gain).astype(jnp.bfloat16)
    gathered = lax.all_gather(normed, "section", axis=0, tiled=True)
    expand_full, project_full = (
        lax.all_gather(expand_weight, "dp", axis=0, tiled=True),
        lax.all_gather(project_weight, "dp", axis=1, tiled=True),
    )
    preact = jnp.dot(gathered, expand_full, preferred_element_type=jnp.float32)
    activated, derivative = gelu_pair(preact)
    hidden = activated.astype(jnp.bfloat16)
    row_block = hidden
    mixed = lax.psum_scatter(
        jnp.dot(row_block, project_full, preferred_element_type=jnp.float32).astype(jnp.bfloat16),
        "section",
        scatter_dimension=0,
        tiled=True,
    ).astype(jnp.float32)
    out_rows = (inputs + mixed).astype(jnp.bfloat16)
    arrived = lax.all_to_all(out_rows, "section", split_axis=0, concat_axis=0, tiled=True)
    section_id = lax.axis_index("section")
    arrival = jnp.arange(slot_count, dtype=jnp.int32)
    source = arrival // capacity
    slot_index = section_id * capacity + arrival % capacity
    is_live = (slot_index < counts[0][source])[:, None]
    targets = positions[0]
    current = text[targets]
    embedded = text.at[targets].set(jnp.where(is_live, arrived, current))
    picked = jnp.where(is_live, cotangent[targets], jnp.zeros_like(current))
    collected = lax.all_gather(picked, "section", axis=0, tiled=True)
    grad_all = (
        collected.reshape(sections, sections, capacity, features)
        .transpose(1, 0, 2, 3)
        .reshape(sections * slot_count, features)
    )
    returned = lax.dynamic_slice_in_dim(grad_all, section_id * slot_count, slot_count, 0)
    grad_own = returned.astype(jnp.float32)
    project_local = lax.dot_general(
        hidden, grad_all, (((0,), (0,)), ((), ())), preferred_element_type=jnp.float32
    )
    grad_hidden = lax.dot_general(
        grad_all, project_full, (((1,), (1,)), ((), ())), preferred_element_type=jnp.float32
    )
    grad_pre = (grad_hidden * derivative).astype(jnp.bfloat16)
    row_block = grad_pre
    grad_normed = lax.psum_scatter(
        lax.dot_general(
            row_block, expand_full, (((1,), (1,)), ((), ())), preferred_element_type=jnp.float32
        ).astype(jnp.bfloat16),
        "section",
        scatter_dimension=0,
        tiled=True,
    ).astype(jnp.float32)
    expand_local = lax.dot_general(
        gathered, grad_pre, (((0,), (0,)), ((), ())), preferred_element_type=jnp.float32
    )
    project_total, expand_total = (
        lax.psum(project_local.astype(jnp.bfloat16), "dp").astype(jnp.float32),
        lax.psum(expand_local.astype(jnp.bfloat16), "dp").astype(jnp.float32),
    )
    scaled_grad = grad_normed * gain
    centred = jnp.mean(scaled_grad * inputs, axis=-1, keepdims=True)
    grad_rows = (grad_own + inv_rms * scaled_grad - inputs * inv_rms**3 * centred).astype(
        jnp.bfloat16
    )
    return (
        embedded,
        grad_rows,
        expand_total.astype(jnp.bfloat16),
        project_total.astype(jnp.bfloat16),
    )


def bit_steps(size):
    steps = []
    step = size // 2
    while step >= 1:
        steps.append(step)
        step //= 2
    return steps


def swap(array, axis, step):
    size = lax.axis_size(axis)
    return lax.ppermute(array, axis, [(i, i ^ step) for i in range(size)])


def masked_steps(index, steps):
    mask = 0
    for place, step in enumerate(steps):
        mask = mask + ((index >> place) & 1) * step
    return mask


VMEM_SPEC = pl.BlockSpec(memory_space=pltpu.VMEM)
SMEM_SPEC = pl.BlockSpec(memory_space=pltpu.SMEM)


def log2(value):
    return value.bit_length() - 1


def landing(place_ref, count_ref, section, slots, capacity, length):
    row = lax.broadcasted_iota(jnp.int32, (slots, length), 0)
    column = lax.broadcasted_iota(jnp.int32, (slots, length), 1)
    spot = jnp.full((slots, length), -1, jnp.int32)
    for q in range(slots):
        live = section * capacity + q % capacity < count_ref[0, q // capacity]
        spot = jnp.where(row == q, jnp.where(live, place_ref[0, q], -1), spot)
    return (spot == column).astype(jnp.float32)


def fetch(copies):
    for copy in copies:
        copy.start()
    for copy in copies:
        copy.wait()


def pick_kernel(
    capacity, counts_at, places_at, patches_at, cotangent_at, pair_ref,
    count_ref, place_ref, patch_ref, cotangent_ref, sems,
):
    ends = (
        (counts_at, count_ref), (places_at, place_ref),
        (patches_at, patch_ref), (cotangent_at, cotangent_ref),
    )
    fetch([pltpu.make_async_copy(a, b, sems.at[i]) for i, (a, b) in enumerate(ends)])
    slots = patch_ref.shape[0]
    section = lax.axis_index("section")
    chooser = landing(
        place_ref, count_ref, section, slots, capacity, cotangent_ref.shape[0]
    ).astype(jnp.bfloat16)
    picked = jnp.dot(chooser, cotangent_ref[...], preferred_element_type=jnp.float32)
    pair_ref[0] = jnp.concatenate(
        [patch_ref[...].astype(jnp.float32), picked], axis=0
    ).astype(jnp.bfloat16)


def repack_kernel(expand_at, project_at, *refs):
    blocks, sems = refs[:-1], refs[-1]
    units = blocks[0].shape[2]
    copies = []
    for i, block in enumerate(blocks):
        start = pl.multiple_of((lax.axis_index("dp") ^ (i + 1)) * units, 128)
        for k, source in enumerate((expand_at, project_at)):
            copies.append(
                pltpu.make_async_copy(
                    source.at[:, pl.ds(start, units)], block.at[k], sems.at[2 * i + k]
                )
            )
    fetch(copies)


def turn_kernel(normed_ref, grad_ref, normed_turned_ref, grad_turned_ref):
    normed_turned_ref[...] = normed_ref[...].T
    grad_turned_ref[...] = grad_ref[...].T


def join_kernel(first_ref, second_ref, out_ref):
    count = first_ref.shape[0]
    out_ref[:count] = first_ref[...]
    out_ref[count:] = second_ref[...]


def order_kernel(
    sections, capacity, dp_steps, section_steps,
    me_ref, near_ref, far_ref, gain_ref, normed_ref, grad_ref, extra_ref,
):
    rows = normed_ref.shape[0]
    slots = sections * capacity
    half = near_ref.shape[0] * near_ref.shape[1]
    me_dp, me_section = me_ref[0], me_ref[1]
    column = lax.broadcasted_iota(jnp.int32, (8, half), 1)
    row = lax.broadcasted_iota(jnp.int32, (rows, half), 0)
    kind = column & (2 * slots - 1)
    slot = kind & (slots - 1)
    inputs = grad = None
    for side, ref in enumerate((near_ref, far_ref)):
        block = (column >> log2(2 * slots)) + side * (half // (2 * slots))
        source_dp = me_dp ^ masked_steps(block, dp_steps)
        source_section = me_section ^ masked_steps(block >> len(dp_steps), section_steps)
        patch_at = (source_dp * sections + source_section) * slots + slot
        grad_at = (
            (source_dp * sections + (slot >> log2(capacity))) * slots
            + source_section * capacity
            + (slot & (capacity - 1))
        )
        patch_at = jnp.where(kind < slots, patch_at, -1)[:1]
        grad_at = jnp.where(kind >= slots, grad_at, -1)[:1]
        values = ref[...].reshape(half, ref.shape[2])
        chosen = (row == patch_at).astype(jnp.float32).astype(jnp.bfloat16)
        found = jnp.dot(chosen, values, preferred_element_type=jnp.float32)
        inputs = found if inputs is None else inputs + found
        chosen = (row == grad_at).astype(jnp.float32).astype(jnp.bfloat16)
        found = jnp.dot(chosen, values, preferred_element_type=jnp.float32)
        grad = found if grad is None else grad + found
    inv_rms = lax.rsqrt(jnp.mean(inputs * inputs, axis=-1, keepdims=True) + 1e-06)
    normed_ref[...] = (inputs * inv_rms * gain_ref[...]).astype(jnp.bfloat16)
    grad = grad.astype(jnp.bfloat16)
    grad_ref[...] = grad
    mine = lax.broadcasted_iota(jnp.int32, (slots, rows), 0)
    every = lax.broadcasted_iota(jnp.int32, (slots, rows), 1)
    coming_at = (
        (me_dp * sections + (mine >> log2(capacity))) * slots
        + me_section * capacity
        + (mine & (capacity - 1))
    )
    own_at = (me_dp * sections + me_section) * slots + mine
    coming = jnp.dot(
        (every == coming_at).astype(jnp.float32).astype(jnp.bfloat16),
        inputs.astype(jnp.bfloat16),
        preferred_element_type=jnp.float32,
    )
    own = jnp.dot(
        (every == own_at).astype(jnp.float32).astype(jnp.bfloat16),
        grad,
        preferred_element_type=jnp.float32,
    )
    extra_ref[...] = jnp.concatenate([coming, own], axis=0)


def place_blocks(distances, sources, targets, sems):
    me = lax.axis_index("dp")
    copies = []
    for i, (distance, source) in enumerate(zip(distances, sources)):
        part = source.shape[1]
        at = pl.ds(pl.multiple_of((me ^ distance) * part, 8), part)
        for k, target in enumerate(targets):
            copies.append(
                pltpu.make_async_copy(source.at[k], target.at[at, :], sems.at[2 * i + k])
            )
    fetch(copies)


def first_unpack_kernel(distances, own_expand_at, own_project_at, *refs):
    sources, (expand_ref, project_ref, sems) = refs[: len(distances)], refs[-3:]
    part, units = own_expand_at.shape[0], expand_ref.shape[1]
    me = lax.axis_index("dp")
    mine = pl.ds(pl.multiple_of(me * units, 128), units)
    at = pl.ds(pl.multiple_of(me * part, 8), part)
    own = [
        pltpu.make_async_copy(
            source.at[:, mine], target.at[at, :], sems.at[2 * len(distances) + k]
        )
        for k, (source, target) in enumerate(
            ((own_expand_at, expand_ref), (own_project_at, project_ref))
        )
    ]
    for copy in own:
        copy.start()
    place_blocks(distances, sources, (expand_ref, project_ref), sems)
    for copy in own:
        copy.wait()


def next_unpack_kernel(distances, expand_part_ref, project_part_ref, *refs):
    sources, (expand_ref, project_ref, sems) = refs[: len(distances)], refs[-3:]
    place_blocks(distances, sources, (expand_ref, project_ref), sems)


def hidden_kernel(
    distances, expand_part_ref, project_part_ref, normed_ref, grad_ref, *refs
):
    sources, (expand_ref, project_ref, both_ref, sems) = refs[: len(distances)], refs[-4:]
    place_blocks(distances, sources, (expand_ref, project_ref), sems)
    preact = jnp.dot(normed_ref[...], expand_ref[...], preferred_element_type=jnp.float32)
    activated, derivative = gelu_pair(preact)
    both_ref[0] = activated.astype(jnp.bfloat16)
    grad_hidden = jnp.dot(grad_ref[...], project_ref[...], preferred_element_type=jnp.float32)
    both_ref[1] = (grad_hidden * derivative).astype(jnp.bfloat16)


def share_kernel(
    sections, capacity, steps,
    me_ref, both_ref, expand_ref, project_ref, keep_ref, send_ref,
):
    rows = both_ref.shape[1]
    slots = sections * capacity
    row = lax.broadcasted_iota(jnp.int32, (rows, rows), 0)
    column = lax.broadcasted_iota(jnp.int32, (rows, rows), 1)
    inside = row & (slots - 1)
    replica = (row >> log2(slots)) & (rows // (sections * slots) - 1)
    away = row >> log2(rows // sections)
    goal = me_ref[1] ^ masked_steps(away, steps[::-1])
    base = replica * (slots * sections)
    mixed_from = (
        base + (inside >> log2(capacity)) * slots + goal * capacity + (inside & (capacity - 1))
    )
    normed_from = base + goal * slots + inside
    for k, (source, weight_ref) in enumerate(
        ((mixed_from, project_ref), (normed_from, expand_ref))
    ):
        turn = (column == source).astype(jnp.float32).astype(jnp.bfloat16)
        turned = jnp.dot(turn, both_ref[k], preferred_element_type=jnp.float32).astype(jnp.bfloat16)
        share = lax.dot_general(
            turned, weight_ref[...], (((1,), (1,)), ((), ())), preferred_element_type=jnp.float32
        )
        share = share.reshape(2, *keep_ref.shape[1:])
        keep_ref[k] = share[0]
        send_ref[k] = share[1].astype(jnp.bfloat16)


def halve_kernel(keep_ref, got_ref, next_keep_ref, next_send_ref):
    half = next_keep_ref.shape[1]
    total = keep_ref[...] + got_ref[...].astype(jnp.float32)
    next_keep_ref[...] = total[:, :half]
    next_send_ref[...] = total[:, half:].astype(jnp.bfloat16)


def address_kernel(keep_ref, got_ref, out_ref):
    total = keep_ref[...] + got_ref[...].astype(jnp.float32)
    for d in range(out_ref.shape[0]):
        out_ref[d] = jnp.concatenate([total[0, d], total[1, d]], axis=0).astype(jnp.bfloat16)


def weight_grad_kernel(distances, grad_ref, normed_ref, *refs):
    project_at, expand_at, result_ref, sems = refs[-4:]
    blocks = refs[: len(distances)]
    features, units = result_ref.shape[2:]
    pieces = sems.shape[2]
    piece = features // pieces
    copies = []
    for i, (distance, block_ref) in enumerate(zip(distances, blocks)):
        source = lax.axis_index("dp") ^ distance
        columns = pl.ds(pl.multiple_of(source * units, 128), units)
        for k, (rows_ref, out_at) in enumerate(((grad_ref, project_at), (normed_ref, expand_at))):
            result_ref[k, i] = jnp.dot(
                rows_ref[...], block_ref[k], preferred_element_type=jnp.float32
            ).astype(jnp.bfloat16)
            for j in range(pieces):
                at = pl.ds(j * piece, piece)
                copies.append(
                    pltpu.make_async_copy(
                        result_ref.at[k, i, at, :], out_at.at[at, columns], sems.at[k, i, j]
                    )
                )
                copies[-1].start()
    for copy in copies:
        copy.wait()


def finish_kernel(
    capacity,
    me_ref, count_ref, place_ref, tail_ref, extra_ref, patch_ref, text_ref, gain_ref,
    embedded_ref, grad_rows_ref,
):
    slots = patch_ref.shape[0]
    total = tail_ref[0].astype(jnp.float32)
    for d in range(1, tail_ref.shape[0]):
        total += tail_ref[d].astype(jnp.float32)
    mixed, grad_normed = total[:slots], total[slots:]
    out_rows = (extra_ref[:slots, :] + mixed).astype(jnp.bfloat16)
    length = text_ref.shape[0]
    chooser = landing(place_ref, count_ref, me_ref[1], slots, capacity, length)
    contract = (((0,), (0,)), ((), ()))
    placed = lax.dot_general(
        chooser.astype(jnp.bfloat16), out_rows, contract, preferred_element_type=jnp.float32
    )
    taken = lax.dot_general(
        chooser.astype(jnp.bfloat16), jnp.ones((slots, 128), jnp.bfloat16),
        contract, preferred_element_type=jnp.float32,
    )[:, :1]
    embedded_ref[...] = jnp.where(
        taken > 0.5, placed, text_ref[...].astype(jnp.float32)
    ).astype(jnp.bfloat16)
    inputs = patch_ref[...].astype(jnp.float32)
    inv_rms = lax.rsqrt(jnp.mean(inputs * inputs, axis=-1, keepdims=True) + 1e-06)
    scaled_grad = grad_normed * gain_ref[...]
    centred = jnp.mean(scaled_grad * inputs, axis=-1, keepdims=True)
    grad_rows_ref[...] = (
        extra_ref[slots:, :] + inv_rms * scaled_grad - inputs * (inv_rms**3 * centred)
    ).astype(jnp.bfloat16)


def weight_grads(blocks, distances, grad_turned, normed_turned, width, before):
    count = len(blocks)
    _, rows, units = blocks[0].shape
    features = grad_turned.shape[0]
    pieces = 2 if features % 32 == 0 else 1
    anywhere = pl.BlockSpec(memory_space=pl.ANY)
    aliases = {2 + count: 0, 3 + count: 1} if before else {}
    return pl.pallas_call(
        functools.partial(weight_grad_kernel, distances),
        in_specs=[VMEM_SPEC] * (2 + count) + [anywhere] * len(before),
        out_specs=[anywhere] * 2,
        out_shape=[jax.ShapeDtypeStruct((features, width), jnp.bfloat16)] * 2,
        scratch_shapes=[
            pltpu.VMEM((2, count, features, units), jnp.bfloat16),
            pltpu.SemaphoreType.DMA((2, count, pieces)),
        ],
        input_output_aliases=aliases,
        compiler_params=pltpu.CompilerParams(vmem_limit_bytes=12 << 20),
        cost_estimate=pl.CostEstimate(
            flops=4 * count * rows * features * units,
            bytes_accessed=4 * count * units * features + 4 * rows * features,
            transcendentals=0,
        ),
    )(grad_turned, normed_turned, *blocks, *before)


def call(kernel, out_shape, smem, vmem, scratch=()):
    single = not isinstance(out_shape, (list, tuple))
    return pl.pallas_call(
        kernel,
        out_shape=out_shape,
        in_specs=[SMEM_SPEC] * len(smem) + [VMEM_SPEC] * len(vmem),
        out_specs=VMEM_SPEC if single else [VMEM_SPEC] * len(out_shape),
        scratch_shapes=scratch,
        compiler_params=pltpu.CompilerParams(vmem_limit_bytes=12 << 20),
    )(*smem, *vmem)


def arrival_groups(dp):
    half, quarter = 1 << (dp - 1), 1 << (dp - 2)
    last = (2 * quarter - 1,) if quarter > 1 else (2 * half - 1,)
    middle = tuple(i for i in (quarter, 2 * half - 1) if i not in last)
    early = tuple(i for i in range(1, 2 * half) if i not in last + middle)
    return early, middle, last


def join(first, second):
    both = (first.shape[0] + second.shape[0], *first.shape[1:])
    return call(join_kernel, jax.ShapeDtypeStruct(both, first.dtype), (), (first, second))


def unit_order(dp):
    far = 1 << (dp - 1)

    def key(distance):
        hops = distance.bit_count()
        return (hops, hops > 1 and distance < far, distance if hops > 1 else -distance)

    return sorted(range(1, 2 * far), key=key)


def gradient_groups(dp):
    order = unit_order(dp)
    order = order[1:dp] + order[dp : dp + 1] + order[:1] + order[dp + 1 :]
    return [(0,)] + [tuple(order[i : i + 2]) for i in range(0, len(order), 2)]


def move_rows_plan(
    patches, gain, expand_weight, project_weight, counts, positions, text, cotangent
):
    sections = lax.axis_size("section")
    replicas = lax.axis_size("dp")
    devices = sections * replicas
    slots, features = patches.shape
    part, width = expand_weight.shape
    units = width // replicas
    capacity = slots // sections
    rows = devices * slots
    dp_steps, section_steps = bit_steps(replicas), bit_steps(sections)
    me = jnp.stack([lax.axis_index("dp"), lax.axis_index("section")]).astype(jnp.int32)
    gain = gain.reshape(1, features)
    project_turned = project_weight.T
    kept, wide = jnp.bfloat16, jnp.float32
    shape = jax.ShapeDtypeStruct

    hbm = pl.BlockSpec(memory_space=pltpu.HBM)

    def in_hbm(*arrays):
        return [pltpu.with_memory_space_constraint(array, pltpu.HBM) for array in arrays]

    held = pl.pallas_call(
        functools.partial(pick_kernel, capacity),
        out_shape=shape((1, 2 * slots, features), kept),
        in_specs=[hbm] * 4,
        out_specs=VMEM_SPEC,
        scratch_shapes=[
            pltpu.SMEM(counts.shape, counts.dtype),
            pltpu.SMEM(positions.shape, positions.dtype),
            pltpu.VMEM(patches.shape, kept),
            pltpu.VMEM(cotangent.shape, kept),
            pltpu.SemaphoreType.DMA((4,)),
        ],
        compiler_params=pltpu.CompilerParams(vmem_limit_bytes=12 << 20),
    )(*in_hbm(counts, positions, patches, cotangent))
    blocks = pl.pallas_call(
        repack_kernel,
        out_shape=[shape((2, part, units), kept)] * (replicas - 1),
        in_specs=[hbm] * 2,
        out_specs=[VMEM_SPEC] * (replicas - 1),
        scratch_shapes=[pltpu.SemaphoreType.DMA((2 * replicas - 2,))],
        compiler_params=pltpu.CompilerParams(vmem_limit_bytes=12 << 20),
    )(*in_hbm(expand_weight, project_turned))
    arrived = []
    for distance in range(1, replicas):
        arrived.append(swap(blocks[distance - 1], "dp", distance))

    exchanges = [("dp", step) for step in dp_steps] + [("section", step) for step in section_steps]
    for axis, step in exchanges:
        got = swap(held, axis, step)
        if held.shape[0] < devices // 2:
            held = join(held, got)
    normed, grad_all, extra = call(
        functools.partial(order_kernel, sections, capacity, dp_steps, section_steps),
        [shape((rows, features), kept)] * 2 + [shape((2 * slots, features), wide)],
        (me,), (held, got, gain),
    )
    normed_turned, grad_turned = call(
        turn_kernel, [shape((features, rows), kept)] * 2, (), (normed, grad_all)
    )
    anywhere = pl.BlockSpec(memory_space=pl.ANY)
    slices = [shape((features, units), kept)] * 2
    groups = arrival_groups(log2(replicas))

    def unpacking(kernel, group, operands, specs, extra=(), aliases=()):
        return pl.pallas_call(
            functools.partial(kernel, group),
            out_shape=[*slices, *extra],
            in_specs=[*specs, *[anywhere] * len(group)],
            out_specs=[VMEM_SPEC] * (2 + len(extra)),
            scratch_shapes=[pltpu.SemaphoreType.DMA((2 * len(group) + 2,))],
            input_output_aliases=dict(aliases),
            compiler_params=pltpu.CompilerParams(vmem_limit_bytes=12 << 20),
        )(*operands, *(arrived[distance - 1] for distance in group))

    in_place = ((0, 0), (1, 1))
    held_slices = unpacking(
        first_unpack_kernel, groups[0], in_hbm(expand_weight, project_turned), [hbm] * 2
    )
    held_slices = unpacking(
        next_unpack_kernel, groups[1], held_slices, [VMEM_SPEC] * 2, aliases=in_place
    )
    expand_slice, project_slice, both = unpacking(
        hidden_kernel, groups[2], (*held_slices, normed, grad_all), [VMEM_SPEC] * 4,
        [shape((2, rows, units), kept)], in_place,
    )

    tail_steps = section_steps[::-1]
    keep, send = call(
        functools.partial(share_kernel, sections, capacity, tail_steps),
        [shape((2, devices // 2, slots, features), kind) for kind in (wide, kept)],
        (me,), (both, expand_slice, project_slice),
    )
    for place, step in enumerate(tail_steps):
        got = swap(send, "section", step)
        if place < len(tail_steps) - 1:
            half = (2, send.shape[1] // 2, slots, features)
            keep, send = call(
                halve_kernel, [shape(half, wide), shape(half, kept)], (), (keep, got)
            )
    tail = call(address_kernel, shape((replicas, 2 * slots, features), kept), (), (keep, got))
    tail = lax.all_to_all(tail, "dp", split_axis=0, concat_axis=0, tiled=True)

    units_from = {0: both}
    for distance in unit_order(log2(replicas)):
        step = distance & -distance
        if distance == replicas - 1 and replicas > 4:
            step *= 2
        units_from[distance] = swap(units_from[distance ^ step], "dp", step)
    grads = ()
    for distances in gradient_groups(log2(replicas)):
        grads = weight_grads(
            [units_from[distance] for distance in distances], distances,
            grad_turned, normed_turned, width, grads,
        )
    project_grad, expand_grad = grads
    embedded, grad_rows = call(
        functools.partial(finish_kernel, capacity),
        [shape(text.shape, kept), shape(patches.shape, kept)],
        (me, counts, positions), (tail, extra, patches, text, gain),
    )
    return (embedded, grad_rows, expand_grad, project_grad.T)


def power_of_two(value):
    return value > 0 and value & (value - 1) == 0


def shards(patches, gain, expand_weight, project_weight, counts, positions, text, cotangent):
    replicas, sections = lax.axis_size("dp"), lax.axis_size("section")
    slots, features = patches.shape
    width = expand_weight.shape[1]
    rows = replicas * sections * slots
    fits = rows * (features + width) <= features * width
    even = (
        all(power_of_two(n) for n in (replicas, sections, slots))
        and replicas > 2
        and sections > 1
        and slots % 8 == 0
        and width % (128 * replicas) == 0
    )
    if fits and even:
        plan = move_rows_plan
    else:
        plan = gather_weights_plan
    return plan(
        patches, gain, expand_weight, project_weight, counts, positions, text, cotangent
    )


def solution(mesh):
    return jax.shard_map(
        shards,
        mesh=mesh,
        in_specs=(
            P(("dp", "section"), None),
            P(),
            P("dp", "section"),
            P("section", "dp"),
            P("dp", None),
            P(("dp", "section"), None),
            P(("dp", "section"), None),
            P(("dp", "section"), None),
        ),
        out_specs=(
            P(("dp", "section"), None),
            P(("dp", "section"), None),
            P(None, "section"),
            P("section", None),
        ),
        check_vma=False,
    )
```

```python
import functools

import jax
import jax.numpy as jnp
from jax import lax
from jax.experimental import pallas as pl
from jax.experimental.pallas import tpu as pltpu
from jax.sharding import PartitionSpec as P


def gelu_pair(values):
    coeff = 0.7978845608
    inner = coeff * (values + 0.044715 * values * values * values)
    tangent = jnp.tanh(inner)
    activated = 0.5 * values * (1.0 + tangent)
    derivative = 0.5 * (1.0 + tangent) + 0.5 * values * (1.0 - tangent * tangent) * coeff * (
        1.0 + 3.0 * 0.044715 * values * values
    )
    return (activated, derivative)


def gather_weights_plan(
    patches, gain, expand_weight, project_weight, counts, positions, text, cotangent
):
    sections = lax.axis_size("section")
    slot_count = patches.shape[0]
    features = patches.shape[1]
    capacity = slot_count // sections
    inputs = patches.astype(jnp.float32)
    inv_rms = lax.rsqrt(jnp.mean(inputs * inputs, axis=-1, keepdims=True) + 1e-06)
    normed = (inputs * inv_rms * gain).astype(jnp.bfloat16)
    gathered = lax.all_gather(normed, "section", axis=0, tiled=True)
    expand_full, project_full = (
        lax.all_gather(expand_weight, "dp", axis=0, tiled=True),
        lax.all_gather(project_weight, "dp", axis=1, tiled=True),
    )
    preact = jnp.dot(gathered, expand_full, preferred_element_type=jnp.float32)
    activated, derivative = gelu_pair(preact)
    hidden = activated.astype(jnp.bfloat16)
    row_block = hidden
    mixed = lax.psum_scatter(
        jnp.dot(row_block, project_full, preferred_element_type=jnp.float32).astype(jnp.bfloat16),
        "section",
        scatter_dimension=0,
        tiled=True,
    ).astype(jnp.float32)
    out_rows = (inputs + mixed).astype(jnp.bfloat16)
    arrived = lax.all_to_all(out_rows, "section", split_axis=0, concat_axis=0, tiled=True)
    section_id = lax.axis_index("section")
    arrival = jnp.arange(slot_count, dtype=jnp.int32)
    source = arrival // capacity
    slot_index = section_id * capacity + arrival % capacity
    is_live = (slot_index < counts[0][source])[:, None]
    targets = positions[0]
    current = text[targets]
    embedded = text.at[targets].set(jnp.where(is_live, arrived, current))
    picked = jnp.where(is_live, cotangent[targets], jnp.zeros_like(current))
    collected = lax.all_gather(picked, "section", axis=0, tiled=True)
    grad_all = (
        collected.reshape(sections, sections, capacity, features)
        .transpose(1, 0, 2, 3)
        .reshape(sections * slot_count, features)
    )
    returned = lax.dynamic_slice_in_dim(grad_all, section_id * slot_count, slot_count, 0)
    grad_own = returned.astype(jnp.float32)
    project_local = lax.dot_general(
        hidden, grad_all, (((0,), (0,)), ((), ())), preferred_element_type=jnp.float32
    )
    grad_hidden = lax.dot_general(
        grad_all, project_full, (((1,), (1,)), ((), ())), preferred_element_type=jnp.float32
    )
    grad_pre = (grad_hidden * derivative).astype(jnp.bfloat16)
    row_block = grad_pre
    grad_normed = lax.psum_scatter(
        lax.dot_general(
            row_block, expand_full, (((1,), (1,)), ((), ())), preferred_element_type=jnp.float32
        ).astype(jnp.bfloat16),
        "section",
        scatter_dimension=0,
        tiled=True,
    ).astype(jnp.float32)
    expand_local = lax.dot_general(
        gathered, grad_pre, (((0,), (0,)), ((), ())), preferred_element_type=jnp.float32
    )
    project_total, expand_total = (
        lax.psum(project_local.astype(jnp.bfloat16), "dp").astype(jnp.float32),
        lax.psum(expand_local.astype(jnp.bfloat16), "dp").astype(jnp.float32),
    )
    scaled_grad = grad_normed * gain
    centred = jnp.mean(scaled_grad * inputs, axis=-1, keepdims=True)
    grad_rows = (grad_own + inv_rms * scaled_grad - inputs * inv_rms**3 * centred).astype(
        jnp.bfloat16
    )
    return (
        embedded,
        grad_rows,
        expand_total.astype(jnp.bfloat16),
        project_total.astype(jnp.bfloat16),
    )


def bit_steps(size):
    steps = []
    step = size // 2
    while step >= 1:
        steps.append(step)
        step //= 2
    return steps


def swap(array, axis, step):
    size = lax.axis_size(axis)
    return lax.ppermute(array, axis, [(i, i ^ step) for i in range(size)])


def masked_steps(index, steps):
    mask = 0
    for place, step in enumerate(steps):
        mask = mask + ((index >> place) & 1) * step
    return mask


VMEM_SPEC = pl.BlockSpec(memory_space=pltpu.VMEM)
SMEM_SPEC = pl.BlockSpec(memory_space=pltpu.SMEM)


def log2(value):
    return value.bit_length() - 1


def landing(place_ref, count_ref, section, slots, capacity, length):
    row = lax.broadcasted_iota(jnp.int32, (slots, length), 0)
    column = lax.broadcasted_iota(jnp.int32, (slots, length), 1)
    spot = jnp.full((slots, length), -1, jnp.int32)
    for q in range(slots):
        live = section * capacity + q % capacity < count_ref[0, q // capacity]
        spot = jnp.where(row == q, jnp.where(live, place_ref[0, q], -1), spot)
    return (spot == column).astype(jnp.float32)


def fetch(copies):
    for copy in copies:
        copy.start()
    for copy in copies:
        copy.wait()


def pick_kernel(
    capacity, counts_at, places_at, patches_at, cotangent_at, pair_ref,
    count_ref, place_ref, patch_ref, cotangent_ref, sems,
):
    ends = (
        (counts_at, count_ref), (places_at, place_ref),
        (patches_at, patch_ref), (cotangent_at, cotangent_ref),
    )
    fetch([pltpu.make_async_copy(a, b, sems.at[i]) for i, (a, b) in enumerate(ends)])
    slots = patch_ref.shape[0]
    section = lax.axis_index("section")
    chooser = landing(
        place_ref, count_ref, section, slots, capacity, cotangent_ref.shape[0]
    ).astype(jnp.bfloat16)
    picked = jnp.dot(chooser, cotangent_ref[...], preferred_element_type=jnp.float32)
    pair_ref[0] = jnp.concatenate(
        [patch_ref[...].astype(jnp.float32), picked], axis=0
    ).astype(jnp.bfloat16)


def repack_kernel(distances, expand_at, project_at, *refs):
    blocks, sems = refs[:-1], refs[-1]
    units = blocks[0].shape[2]
    copies = []
    for i, (distance, block) in enumerate(zip(distances, blocks)):
        start = pl.multiple_of((lax.axis_index("dp") ^ distance) * units, 128)
        for k, source in enumerate((expand_at, project_at)):
            copies.append(
                pltpu.make_async_copy(
                    source.at[:, pl.ds(start, units)], block.at[k], sems.at[2 * i + k]
                )
            )
    fetch(copies)


def turn_kernel(normed_ref, grad_ref, normed_turned_ref, grad_turned_ref):
    normed_turned_ref[...] = normed_ref[...].T
    grad_turned_ref[...] = grad_ref[...].T


def join_kernel(first_ref, second_ref, out_ref):
    count = first_ref.shape[0]
    out_ref[:count] = first_ref[...]
    out_ref[count:] = second_ref[...]


def order_kernel(
    sections, capacity, dp_steps, section_steps,
    me_ref, near_ref, far_ref, gain_ref, normed_ref, grad_ref, extra_ref,
):
    rows = normed_ref.shape[0]
    slots = sections * capacity
    half = near_ref.shape[0] * near_ref.shape[1]
    me_dp, me_section = me_ref[0], me_ref[1]
    column = lax.broadcasted_iota(jnp.int32, (8, half), 1)
    row = lax.broadcasted_iota(jnp.int32, (rows, half), 0)
    kind = column & (2 * slots - 1)
    slot = kind & (slots - 1)
    inputs = grad = None
    for side, ref in enumerate((near_ref, far_ref)):
        block = (column >> log2(2 * slots)) + side * (half // (2 * slots))
        source_dp = me_dp ^ masked_steps(block, dp_steps)
        source_section = me_section ^ masked_steps(block >> len(dp_steps), section_steps)
        patch_at = (source_dp * sections + source_section) * slots + slot
        grad_at = (
            (source_dp * sections + (slot >> log2(capacity))) * slots
            + source_section * capacity
            + (slot & (capacity - 1))
        )
        patch_at = jnp.where(kind < slots, patch_at, -1)[:1]
        grad_at = jnp.where(kind >= slots, grad_at, -1)[:1]
        values = ref[...].reshape(half, ref.shape[2])
        chosen = (row == patch_at).astype(jnp.float32).astype(jnp.bfloat16)
        found = jnp.dot(chosen, values, preferred_element_type=jnp.float32)
        inputs = found if inputs is None else inputs + found
        chosen = (row == grad_at).astype(jnp.float32).astype(jnp.bfloat16)
        found = jnp.dot(chosen, values, preferred_element_type=jnp.float32)
        grad = found if grad is None else grad + found
    inv_rms = lax.rsqrt(jnp.mean(inputs * inputs, axis=-1, keepdims=True) + 1e-06)
    normed_ref[...] = (inputs * inv_rms * gain_ref[...]).astype(jnp.bfloat16)
    grad = grad.astype(jnp.bfloat16)
    grad_ref[...] = grad
    mine = lax.broadcasted_iota(jnp.int32, (slots, rows), 0)
    every = lax.broadcasted_iota(jnp.int32, (slots, rows), 1)
    coming_at = (
        (me_dp * sections + (mine >> log2(capacity))) * slots
        + me_section * capacity
        + (mine & (capacity - 1))
    )
    own_at = (me_dp * sections + me_section) * slots + mine
    coming = jnp.dot(
        (every == coming_at).astype(jnp.float32).astype(jnp.bfloat16),
        inputs.astype(jnp.bfloat16),
        preferred_element_type=jnp.float32,
    )
    own = jnp.dot(
        (every == own_at).astype(jnp.float32).astype(jnp.bfloat16),
        grad,
        preferred_element_type=jnp.float32,
    )
    extra_ref[...] = jnp.concatenate([coming, own], axis=0)


def place_blocks(distances, sources, targets, sems):
    me = lax.axis_index("dp")
    copies = []
    for i, (distance, source) in enumerate(zip(distances, sources)):
        part = source.shape[1]
        at = pl.ds(pl.multiple_of((me ^ distance) * part, 8), part)
        for k, target in enumerate(targets):
            copies.append(
                pltpu.make_async_copy(source.at[k], target.at[at, :], sems.at[2 * i + k])
            )
    fetch(copies)


def first_unpack_kernel(distances, own_expand_at, own_project_at, *refs):
    sources, (expand_ref, project_ref, sems) = refs[: len(distances)], refs[-3:]
    part, units = own_expand_at.shape[0], expand_ref.shape[1]
    me = lax.axis_index("dp")
    mine = pl.ds(pl.multiple_of(me * units, 128), units)
    at = pl.ds(pl.multiple_of(me * part, 8), part)
    own = [
        pltpu.make_async_copy(
            source.at[:, mine], target.at[at, :], sems.at[2 * len(distances) + k]
        )
        for k, (source, target) in enumerate(
            ((own_expand_at, expand_ref), (own_project_at, project_ref))
        )
    ]
    for copy in own:
        copy.start()
    place_blocks(distances, sources, (expand_ref, project_ref), sems)
    for copy in own:
        copy.wait()


def next_unpack_kernel(distances, expand_part_ref, project_part_ref, *refs):
    sources, (expand_ref, project_ref, sems) = refs[: len(distances)], refs[-3:]
    place_blocks(distances, sources, (expand_ref, project_ref), sems)


def hidden_kernel(
    distances, expand_part_ref, project_part_ref, normed_ref, grad_ref, *refs
):
    sources, (expand_ref, project_ref, both_ref, sems) = refs[: len(distances)], refs[-4:]
    place_blocks(distances, sources, (expand_ref, project_ref), sems)
    preact = jnp.dot(normed_ref[...], expand_ref[...], preferred_element_type=jnp.float32)
    activated, derivative = gelu_pair(preact)
    both_ref[0] = activated.astype(jnp.bfloat16)
    grad_hidden = jnp.dot(grad_ref[...], project_ref[...], preferred_element_type=jnp.float32)
    both_ref[1] = (grad_hidden * derivative).astype(jnp.bfloat16)


def share_kernel(
    sections, capacity, steps,
    me_ref, both_ref, expand_ref, project_ref, keep_ref, send_ref,
):
    rows = both_ref.shape[1]
    slots = sections * capacity
    row = lax.broadcasted_iota(jnp.int32, (rows, rows), 0)
    column = lax.broadcasted_iota(jnp.int32, (rows, rows), 1)
    inside = row & (slots - 1)
    replica = (row >> log2(slots)) & (rows // (sections * slots) - 1)
    away = row >> log2(rows // sections)
    goal = me_ref[1] ^ masked_steps(away, steps[::-1])
    base = replica * (slots * sections)
    mixed_from = (
        base + (inside >> log2(capacity)) * slots + goal * capacity + (inside & (capacity - 1))
    )
    normed_from = base + goal * slots + inside
    for k, (source, weight_ref) in enumerate(
        ((mixed_from, project_ref), (normed_from, expand_ref))
    ):
        turn = (column == source).astype(jnp.float32).astype(jnp.bfloat16)
        turned = jnp.dot(turn, both_ref[k], preferred_element_type=jnp.float32).astype(jnp.bfloat16)
        share = lax.dot_general(
            turned, weight_ref[...], (((1,), (1,)), ((), ())), preferred_element_type=jnp.float32
        )
        share = share.reshape(2, *keep_ref.shape[1:])
        keep_ref[k] = share[0]
        send_ref[k] = share[1].astype(jnp.bfloat16)


def halve_kernel(keep_ref, got_ref, next_keep_ref, next_send_ref):
    half = next_keep_ref.shape[1]
    total = keep_ref[...] + got_ref[...].astype(jnp.float32)
    next_keep_ref[...] = total[:, :half]
    next_send_ref[...] = total[:, half:].astype(jnp.bfloat16)


def address_kernel(keep_ref, got_ref, out_ref):
    total = keep_ref[...] + got_ref[...].astype(jnp.float32)
    for d in range(out_ref.shape[0]):
        out_ref[d] = jnp.concatenate([total[0, d], total[1, d]], axis=0).astype(jnp.bfloat16)


def weight_grad_kernel(distances, grad_ref, normed_ref, *refs):
    project_at, expand_at, result_ref, sems = refs[-4:]
    blocks = refs[: len(distances)]
    features, units = result_ref.shape[2:]
    pieces = sems.shape[2]
    piece = features // pieces
    copies = []
    for i, (distance, block_ref) in enumerate(zip(distances, blocks)):
        source = lax.axis_index("dp") ^ distance
        columns = pl.ds(pl.multiple_of(source * units, 128), units)
        for k, (rows_ref, out_at) in enumerate(((grad_ref, project_at), (normed_ref, expand_at))):
            result_ref[k, i] = jnp.dot(
                rows_ref[...], block_ref[k], preferred_element_type=jnp.float32
            ).astype(jnp.bfloat16)
            for j in range(pieces):
                at = pl.ds(j * piece, piece)
                copies.append(
                    pltpu.make_async_copy(
                        result_ref.at[k, i, at, :], out_at.at[at, columns], sems.at[k, i, j]
                    )
                )
                copies[-1].start()
    for copy in copies:
        copy.wait()


def finish_kernel(
    capacity,
    me_ref, count_ref, place_ref, tail_ref, extra_ref, patch_ref, text_ref, gain_ref,
    embedded_ref, grad_rows_ref,
):
    slots = patch_ref.shape[0]
    total = tail_ref[0].astype(jnp.float32)
    for d in range(1, tail_ref.shape[0]):
        total += tail_ref[d].astype(jnp.float32)
    mixed, grad_normed = total[:slots], total[slots:]
    out_rows = (extra_ref[:slots, :] + mixed).astype(jnp.bfloat16)
    length = text_ref.shape[0]
    chooser = landing(place_ref, count_ref, me_ref[1], slots, capacity, length)
    contract = (((0,), (0,)), ((), ()))
    placed = lax.dot_general(
        chooser.astype(jnp.bfloat16), out_rows, contract, preferred_element_type=jnp.float32
    )
    taken = lax.dot_general(
        chooser.astype(jnp.bfloat16), jnp.ones((slots, 128), jnp.bfloat16),
        contract, preferred_element_type=jnp.float32,
    )[:, :1]
    embedded_ref[...] = jnp.where(
        taken > 0.5, placed, text_ref[...].astype(jnp.float32)
    ).astype(jnp.bfloat16)
    inputs = patch_ref[...].astype(jnp.float32)
    inv_rms = lax.rsqrt(jnp.mean(inputs * inputs, axis=-1, keepdims=True) + 1e-06)
    scaled_grad = grad_normed * gain_ref[...]
    centred = jnp.mean(scaled_grad * inputs, axis=-1, keepdims=True)
    grad_rows_ref[...] = (
        extra_ref[slots:, :] + inv_rms * scaled_grad - inputs * (inv_rms**3 * centred)
    ).astype(jnp.bfloat16)


def weight_grads(blocks, distances, grad_turned, normed_turned, width, before):
    count = len(blocks)
    _, rows, units = blocks[0].shape
    features = grad_turned.shape[0]
    pieces = 2 if features % 32 == 0 else 1
    anywhere = pl.BlockSpec(memory_space=pl.ANY)
    aliases = {2 + count: 0, 3 + count: 1} if before else {}
    return pl.pallas_call(
        functools.partial(weight_grad_kernel, distances),
        in_specs=[VMEM_SPEC] * (2 + count) + [anywhere] * len(before),
        out_specs=[anywhere] * 2,
        out_shape=[jax.ShapeDtypeStruct((features, width), jnp.bfloat16)] * 2,
        scratch_shapes=[
            pltpu.VMEM((2, count, features, units), jnp.bfloat16),
            pltpu.SemaphoreType.DMA((2, count, pieces)),
        ],
        input_output_aliases=aliases,
        compiler_params=pltpu.CompilerParams(vmem_limit_bytes=12 << 20),
        cost_estimate=pl.CostEstimate(
            flops=4 * count * rows * features * units,
            bytes_accessed=4 * count * units * features + 4 * rows * features,
            transcendentals=0,
        ),
    )(grad_turned, normed_turned, *blocks, *before)


def call(kernel, out_shape, smem, vmem, scratch=()):
    single = not isinstance(out_shape, (list, tuple))
    return pl.pallas_call(
        kernel,
        out_shape=out_shape,
        in_specs=[SMEM_SPEC] * len(smem) + [VMEM_SPEC] * len(vmem),
        out_specs=VMEM_SPEC if single else [VMEM_SPEC] * len(out_shape),
        scratch_shapes=scratch,
        compiler_params=pltpu.CompilerParams(vmem_limit_bytes=12 << 20),
    )(*smem, *vmem)


def arrival_groups(dp):
    half, quarter = 1 << (dp - 1), 1 << (dp - 2)
    last = (2 * quarter - 1,) if quarter > 1 else (2 * half - 1,)
    middle = tuple(i for i in (quarter, 2 * half - 1) if i not in last)
    early = tuple(i for i in range(1, 2 * half) if i not in last + middle)
    return early, middle, last


def join(first, second):
    both = (first.shape[0] + second.shape[0], *first.shape[1:])
    return call(join_kernel, jax.ShapeDtypeStruct(both, first.dtype), (), (first, second))


def unit_order(dp):
    far = 1 << (dp - 1)

    def key(distance):
        hops = distance.bit_count()
        return (hops, hops > 1 and distance < far, distance if hops > 1 else -distance)

    return sorted(range(1, 2 * far), key=key)


def gradient_groups(dp):
    order = unit_order(dp)
    order = order[1:dp] + order[dp : dp + 1] + order[:1] + order[dp + 1 :]
    pairs = [tuple(order[i : i + 2]) for i in range(0, len(order) - 3, 2)]
    return [(0,), *pairs, tuple(order[-3:-2]), tuple(order[-2:])]


def move_rows_plan(
    patches, gain, expand_weight, project_weight, counts, positions, text, cotangent
):
    sections = lax.axis_size("section")
    replicas = lax.axis_size("dp")
    devices = sections * replicas
    slots, features = patches.shape
    part, width = expand_weight.shape
    units = width // replicas
    capacity = slots // sections
    rows = devices * slots
    dp_steps, section_steps = bit_steps(replicas), bit_steps(sections)
    me = jnp.stack([lax.axis_index("dp"), lax.axis_index("section")]).astype(jnp.int32)
    gain = gain.reshape(1, features)
    project_turned = project_weight.T
    kept, wide = jnp.bfloat16, jnp.float32
    shape = jax.ShapeDtypeStruct

    hbm = pl.BlockSpec(memory_space=pltpu.HBM)

    def in_hbm(*arrays):
        return [pltpu.with_memory_space_constraint(array, pltpu.HBM) for array in arrays]

    held = pl.pallas_call(
        functools.partial(pick_kernel, capacity),
        out_shape=shape((1, 2 * slots, features), kept),
        in_specs=[hbm] * 4,
        out_specs=VMEM_SPEC,
        scratch_shapes=[
            pltpu.SMEM(counts.shape, counts.dtype),
            pltpu.SMEM(positions.shape, positions.dtype),
            pltpu.VMEM(patches.shape, kept),
            pltpu.VMEM(cotangent.shape, kept),
            pltpu.SemaphoreType.DMA((4,)),
        ],
        compiler_params=pltpu.CompilerParams(vmem_limit_bytes=12 << 20),
    )(*in_hbm(counts, positions, patches, cotangent))
    far = dp_steps[0]
    soon = tuple(range(far, 2 * far - 1))
    later = tuple(i for i in range(1, replicas) if i not in soon)
    blocks = {}
    for distances in (soon, later):
        packed = pl.pallas_call(
            functools.partial(repack_kernel, distances),
            out_shape=[shape((2, part, units), kept)] * len(distances),
            in_specs=[hbm] * 2,
            out_specs=[VMEM_SPEC] * len(distances),
            scratch_shapes=[pltpu.SemaphoreType.DMA((2 * len(distances),))],
            compiler_params=pltpu.CompilerParams(vmem_limit_bytes=12 << 20),
        )(*in_hbm(expand_weight, project_turned))
        blocks.update(zip(distances, packed))
    arrived = []
    for distance in range(1, replicas):
        arrived.append(swap(blocks[distance], "dp", distance))

    exchanges = [("dp", step) for step in dp_steps] + [("section", step) for step in section_steps]
    for axis, step in exchanges:
        got = swap(held, axis, step)
        if held.shape[0] < devices // 2:
            held = join(held, got)
    normed, grad_all, extra = call(
        functools.partial(order_kernel, sections, capacity, dp_steps, section_steps),
        [shape((rows, features), kept)] * 2 + [shape((2 * slots, features), wide)],
        (me,), (held, got, gain),
    )
    normed_turned, grad_turned = call(
        turn_kernel, [shape((features, rows), kept)] * 2, (), (normed, grad_all)
    )
    anywhere = pl.BlockSpec(memory_space=pl.ANY)
    slices = [shape((features, units), kept)] * 2
    groups = arrival_groups(log2(replicas))

    def unpacking(kernel, group, operands, specs, extra=(), aliases=()):
        return pl.pallas_call(
            functools.partial(kernel, group),
            out_shape=[*slices, *extra],
            in_specs=[*specs, *[anywhere] * len(group)],
            out_specs=[VMEM_SPEC] * (2 + len(extra)),
            scratch_shapes=[pltpu.SemaphoreType.DMA((2 * len(group) + 2,))],
            input_output_aliases=dict(aliases),
            compiler_params=pltpu.CompilerParams(vmem_limit_bytes=12 << 20),
        )(*operands, *(arrived[distance - 1] for distance in group))

    in_place = ((0, 0), (1, 1))
    held_slices = unpacking(
        first_unpack_kernel, groups[0], in_hbm(expand_weight, project_turned), [hbm] * 2
    )
    held_slices = unpacking(
        next_unpack_kernel, groups[1], held_slices, [VMEM_SPEC] * 2, aliases=in_place
    )
    expand_slice, project_slice, both = unpacking(
        hidden_kernel, groups[2], (*held_slices, normed, grad_all), [VMEM_SPEC] * 4,
        [shape((2, rows, units), kept)], in_place,
    )

    tail_steps = section_steps[::-1]
    keep, send = call(
        functools.partial(share_kernel, sections, capacity, tail_steps),
        [shape((2, devices // 2, slots, features), kind) for kind in (wide, kept)],
        (me,), (both, expand_slice, project_slice),
    )
    for place, step in enumerate(tail_steps):
        got = swap(send, "section", step)
        if place < len(tail_steps) - 1:
            half = (2, send.shape[1] // 2, slots, features)
            keep, send = call(
                halve_kernel, [shape(half, wide), shape(half, kept)], (), (keep, got)
            )
    tail = call(address_kernel, shape((replicas, 2 * slots, features), kept), (), (keep, got))
    tail = lax.all_to_all(tail, "dp", split_axis=0, concat_axis=0, tiled=True)

    units_from = {0: both}
    for distance in unit_order(log2(replicas)):
        step = distance & -distance
        if distance == replicas - 1 and replicas > 4:
            step *= 2
        units_from[distance] = swap(units_from[distance ^ step], "dp", step)
    grads = ()
    for distances in gradient_groups(log2(replicas)):
        grads = weight_grads(
            [units_from[distance] for distance in distances], distances,
            grad_turned, normed_turned, width, grads,
        )
    project_grad, expand_grad = grads
    embedded, grad_rows = call(
        functools.partial(finish_kernel, capacity),
        [shape(text.shape, kept), shape(patches.shape, kept)],
        (me, counts, positions), (tail, extra, patches, text, gain),
    )
    return (embedded, grad_rows, expand_grad, project_grad.T)


def power_of_two(value):
    return value > 0 and value & (value - 1) == 0


def shards(patches, gain, expand_weight, project_weight, counts, positions, text, cotangent):
    replicas, sections = lax.axis_size("dp"), lax.axis_size("section")
    slots, features = patches.shape
    width = expand_weight.shape[1]
    rows = replicas * sections * slots
    fits = rows * (features + width) <= features * width
    even = (
        all(power_of_two(n) for n in (replicas, sections, slots))
        and replicas > 2
        and sections > 1
        and slots % 8 == 0
        and width % (128 * replicas) == 0
    )
    if fits and even:
        plan = move_rows_plan
    else:
        plan = gather_weights_plan
    return plan(
        patches, gain, expand_weight, project_weight, counts, positions, text, cotangent
    )


def solution(mesh):
    return jax.shard_map(
        shards,
        mesh=mesh,
        in_specs=(
            P(("dp", "section"), None),
            P(),
            P("dp", "section"),
            P("section", "dp"),
            P("dp", None),
            P(("dp", "section"), None),
            P(("dp", "section"), None),
            P(("dp", "section"), None),
        ),
        out_specs=(
            P(("dp", "section"), None),
            P(("dp", "section"), None),
            P(None, "section"),
            P("section", None),
        ),
        check_vma=False,
    )
```
